32 devices in a mesh: wide: 16 (over z, x, core), narrow: 2 (over y).
Axes of the slice: x: 2, y: 2, z: 4, core: 2. Of those that a mesh axis runs over, the one named last changes fastest.
Arguments:
- tokens: bfloat16 [16384, 512], P(('wide', 'narrow')), may hold values from -6 to 6
- input_weight: bfloat16 [2, 512, 3, 512], P(None, None, None, 'narrow'), may hold values from -0.25 to 0.25
- query_bias: float32 [2, 512], P(None, 'narrow'), may hold values from -4 to 4
- value_bias: float32 [2, 512], P(None, 'narrow'), may hold values from -0.5 to 0.5
- output_weight: bfloat16 [2, 512, 512], P(None, 'narrow'), may hold values from -4 to 4
- output_bias: float32 [2, 512], replicated, may hold values from -3 to 3
- first_gain: float32 [2, 512], replicated, may hold values from 0.5 to 1.5
- first_shift: float32 [2, 512], replicated, may hold values from -3 to 3
- expand_weight: bfloat16 [2, 512, 2048], P(None, None, 'narrow'), may hold values from -0.25 to 0.25
- expand_bias: float32 [2, 2048], P(None, 'narrow'), may hold values from -3 to 3
- shrink_weight: bfloat16 [2, 2048, 512], P(None, 'narrow'), may hold values from -0.125 to 0.125
- shrink_bias: float32 [2, 512], replicated, may hold values from -3 to 3
- second_gain: float32 [2, 512], replicated, may hold values from 0.5 to 1.5
- second_shift: float32 [2, 512], replicated, may hold values from -3 to 3
- lengths: int32 [32], P('wide'), may hold values from 0 to 1024, as said below
- bucket: int32 [16], P('wide'), may hold values from 0 to 1, as said below
- cotangent: bfloat16 [16384, 512], P(('wide', 'narrow')), may hold values from -6 to 6
Outputs:
- layer_output: float32 [16384, 512], P(('wide', 'narrow'))
- input_grad: float32 [16384, 512], P(('wide', 'narrow'))
- input_weight_grad: float32 [2, 512, 3, 512], P(None, None, None, 'narrow')
- query_bias_grad: float32 [2, 512], P(None, 'narrow')
- value_bias_grad: float32 [2, 512], P(None, 'narrow')
- output_weight_grad: float32 [2, 512, 512], P(None, 'narrow')
- output_bias_grad: float32 [2, 512], replicated
- first_gain_grad: float32 [2, 512], replicated
- first_shift_grad: float32 [2, 512], replicated
- expand_weight_grad: float32 [2, 512, 2048], P(None, None, 'narrow')
- expand_bias_grad: float32 [2, 2048], P(None, 'narrow')
- shrink_weight_grad: float32 [2, 2048, 512], P(None, 'narrow')
- shrink_bias_grad: float32 [2, 512], replicated
- second_gain_grad: float32 [2, 512], replicated
- second_shift_grad: float32 [2, 512], replicated
The draws below stay inside these ranges and needn't reach their ends.
Inputs may be any that keep to these rules, and one draw needn't show every extreme that they name: Entries 2 i and 2 i + 1 are the lengths of the sequences of index i of wide: either 1024 and 0 or half of 1024 twice; exactly half of the indices hold a single sequence. `bucket`: 0 where index i of wide holds one sequence of 1024 tokens, 1 where it holds two of half that length; agrees with lengths.
All inputs are finite; a program needn't handle non-finite values.
Results may differ from the reference program's by a relative error of at most 0.025.
Values may be sent and summed in bfloat16 or wider, within the bound.
A program may use at most 128 MiB of HBM per device.

```python
import jax
import jax.numpy as jnp
from jax import lax

D = 512
HEADS = 8
DH = 64
FF = 2048
LAYERS = 2
TOK_DEV = 1024
TOKENS = 16384
N_WIDE = 16


def long_groups(key):
    ranking = jax.random.permutation(jax.random.fold_in(key, 11), N_WIDE)
    return ranking < N_WIDE // 2


def draw_lengths(key, part):
    single = long_groups(key)
    leading = jnp.where(single, TOK_DEV, TOK_DEV // 2)
    trailing = jnp.where(single, 0, TOK_DEV // 2)
    return jnp.stack([leading, trailing], 1).reshape(2 * N_WIDE).astype(jnp.int32)


def draw_bucket(key, part):
    return jnp.where(long_groups(key), 0, 1).astype(jnp.int32)


def levels(rng, dims, cuts, least, high):
    level = 1.0
    for axis_at, shards_of in cuts:
        heights = jax.random.uniform(jax.random.fold_in(jax.random.fold_in(rng, 6), axis_at), (shards_of,), jnp.float32, least / len(cuts), high / len(cuts))
        level = level * jnp.repeat(jnp.exp(heights), dims[axis_at] // shards_of).reshape((-1,) + (1,) * (len(dims) - 1 - axis_at))
    return level


def gaussian(key, extent, scale, most, cuts=(), kind=jnp.bfloat16):
    level = levels(key, extent, cuts, -0.22, 0.18) if cuts else 1.0
    values = jax.random.normal(key, extent, jnp.float32) * scale * level
    return jnp.minimum(jnp.maximum(values, -most), most).astype(kind)


def setup_inputs(seed: int = 0) -> dict:
    splits = jax.random.split(jax.random.key(seed), 18)
    return {
        "tokens": gaussian(splits[0], (TOKENS, D), 1.0, 6.0, ((0, 32),)),
        "input_weight": gaussian(splits[1], (LAYERS, D, 3, D), D ** -0.5, 0.25, ((3, 2),)),
        "query_bias": gaussian(splits[2], (LAYERS, D), 1.0, 4.0, ((1, 2),), jnp.float32),
        "value_bias": gaussian(splits[3], (LAYERS, D), ((4 * D // max(1, 4 * D // TOK_DEV)) ** -0.5), 0.5, ((1, 2),), jnp.float32),
        "output_weight": gaussian(splits[4], (LAYERS, D, D), (max(1, 4 * D // TOK_DEV)) ** -0.5, 4.0, ((1, 2),)),
        "output_bias": gaussian(splits[5], (LAYERS, D), 0.5, 3.0, (), jnp.float32),
        "first_gain": jnp.clip(1.0 + 0.1 * jax.random.normal(splits[6], (LAYERS, D), jnp.float32), 0.5, 1.5),
        "first_shift": gaussian(splits[7], (LAYERS, D), 0.5, 3.0, (), jnp.float32),
        "expand_weight": gaussian(splits[8], (LAYERS, D, FF), D ** -0.5, 0.25, ((2, 2),)),
        "expand_bias": gaussian(splits[9], (LAYERS, FF), 0.5, 3.0, ((1, 2),), jnp.float32),
        "shrink_weight": gaussian(splits[10], (LAYERS, FF, D), FF ** -0.5, 0.125, ((1, 2),)),
        "shrink_bias": gaussian(splits[11], (LAYERS, D), 0.5, 3.0, (), jnp.float32),
        "second_gain": jnp.clip(1.0 + 0.1 * jax.random.normal(splits[12], (LAYERS, D), jnp.float32), 0.5, 1.5),
        "second_shift": gaussian(splits[13], (LAYERS, D), 0.5, 3.0, (), jnp.float32),
        "lengths": draw_lengths(jax.random.fold_in(splits[17], 71), 0),
        "bucket": draw_bucket(jax.random.fold_in(splits[17], 71), 0),
        "cotangent": gaussian(splits[16], (TOKENS, D), 1.0, 6.0, ((0, 32),)),
    }


@jax.custom_vjp
def low(v):
    return lax.optimization_barrier(v.astype(jnp.bfloat16)).astype(jnp.float32)

@jax.custom_vjp
def low_back(v):
    return v

def low_keep(v):
    return (low(v), None)

def low_pass(kept, grad):
    return (grad,)

def back_keep(v):
    return (v, None)

def back_low(kept, grad):
    return (low(grad),)
low.defvjp(low_keep, low_pass)
low_back.defvjp(back_keep, back_low)
EPSILON = 1e-12
MASKED = -1000000000.0
HIGHEST = lax.Precision.HIGHEST

def layer_norm(values, gain, shift):
    centre = values - lax.optimization_barrier(jnp.mean(values, -1, keepdims=True))
    spread = lax.optimization_barrier(jnp.mean(centre * centre, -1, keepdims=True))
    return centre * lax.rsqrt(spread + EPSILON) * gain + shift

def attend(queries, key_rows, value_rows, segment):
    total_rows = queries.shape[0]
    block_rows = min(total_rows, 512)
    block_count = total_rows // block_rows
    scaling = DH ** (-0.5)

    def one_block(inputs):
        query_rows, query_seg = inputs
        scores = low_back(jnp.einsum('qhd,khd->hqk', query_rows, key_rows, precision=HIGHEST) * scaling)
        scores = jnp.where((query_seg[:, None] == segment[None, :])[None], scores, MASKED)
        row_peak = lax.optimization_barrier(jnp.max(scores, -1, keepdims=True))
        weights = jnp.exp(scores - row_peak)
        softmax_rows = weights / lax.optimization_barrier(jnp.sum(weights, -1, keepdims=True))
        return jnp.einsum('hqk,khd->qhd', low(softmax_rows), value_rows, precision=HIGHEST)
    mixed_rows = lax.map(jax.checkpoint(one_block), (queries.reshape(block_count, block_rows, HEADS, DH), segment.reshape(block_count, block_rows)))
    return mixed_rows.reshape(total_rows, HEADS * DH)

def layer_forward(params, hidden, segment):
    input_weight, query_bias, value_bias, output_weight, output_bias, first_gain, first_shift, expand_weight, expand_bias, shrink_weight, shrink_bias, second_gain, second_shift = params
    total_rows = hidden.shape[0]
    hidden_low = low(hidden)
    triple = jnp.einsum('td,dce->tce', hidden_low, input_weight, precision=HIGHEST)
    queries = low(low_back(triple[:, 0] + query_bias)).reshape(total_rows, HEADS, DH)
    key_rows = low(low_back(triple[:, 1])).reshape(total_rows, HEADS, DH)
    value_rows = low(low_back(triple[:, 2] + value_bias)).reshape(total_rows, HEADS, DH)
    mixed_rows = low(low_back(attend(queries, key_rows, value_rows, segment)))
    summed = hidden + low_back(jnp.dot(mixed_rows, output_weight, precision=HIGHEST)) + output_bias
    normed = layer_norm(summed, first_gain, first_shift)
    inner_rows = low_back(jnp.dot(low(normed), expand_weight, precision=HIGHEST) + expand_bias)
    activated = low(jax.nn.gelu(inner_rows, approximate=False))
    widened = normed + low_back(jnp.dot(activated, shrink_weight, precision=HIGHEST)) + shrink_bias
    return layer_norm(widened, second_gain, second_shift)

def stack_forward(params, hidden, segment):
    for layer_index in range(LAYERS):
        hidden = layer_forward(tuple((item[layer_index] for item in params)), hidden, segment)
    return hidden

def reference(tokens, input_weight, query_bias, value_bias, output_weight, output_bias, first_gain, first_shift, expand_weight, expand_bias, shrink_weight, shrink_bias, second_gain, second_shift, lengths, bucket, cotangent):
    params = tuple((item.astype(jnp.float32) for item in (input_weight, query_bias, value_bias, output_weight, output_bias, first_gain, first_shift, expand_weight, expand_bias, shrink_weight, shrink_bias, second_gain, second_shift)))
    pairs = lengths.reshape(N_WIDE, 2).astype(jnp.int32)
    boundary = jnp.where(bucket == 1, pairs[:, 0], TOK_DEV).astype(jnp.int32)
    places = jnp.arange(TOK_DEV, dtype=jnp.int32)
    segments = (places[None, :] >= boundary[:, None]).astype(jnp.int32)
    inputs = tokens.astype(jnp.float32).reshape(N_WIDE, TOK_DEV, D)
    cotangents = cotangent.astype(jnp.float32).reshape(N_WIDE, TOK_DEV, D)

    def one_group(carried, group):
        group_rows, group_cot, group_seg = group
        result, pull = jax.vjp(lambda weights_all, rows: stack_forward(weights_all, rows, group_seg), params, group_rows)
        weight_grads, row_grads = pull(group_cot)
        return (tuple((total + extra for total, extra in zip(carried, weight_grads))), (result, row_grads))
    zero_grads = tuple((jnp.zeros_like(item) for item in params))
    grads, (results, row_grads) = lax.scan(one_group, zero_grads, (inputs, cotangents, segments))
    return (results.reshape(TOKENS, D), row_grads.reshape(TOKENS, D), grads[0], grads[1], grads[2], grads[3], grads[4], grads[5], grads[6], grads[7], grads[8], grads[9], grads[10], grads[11], grads[12])
```

```python
import functools

import jax
import jax.numpy as jnp
from jax import lax
from jax.experimental import pallas as pl
from jax.experimental.pallas import tpu as pltpu
from jax.sharding import PartitionSpec as P

DH = 64
EPSILON = 1e-12
MASKED = -1e9
AXES = ("wide", "narrow")
F32 = jnp.float32
BF16 = jnp.bfloat16
LAYER_VECTORS = 6


def dot(a, b):
    return lax.dot_general(a, b, (((1,), (0,)), ((), ())), preferred_element_type=F32)


def dot_rt(a, b):
    return lax.dot_general(a, b, (((1,), (1,)), ((), ())), preferred_element_type=F32)


def dot_lt(a, b):
    return lax.dot_general(a, b, (((0,), (0,)), ((), ())), preferred_element_type=F32)


def start_quarters(own, mine, theirs, buffer, sem, core):
    own_one, own_two = own
    copies = (
        pltpu.make_async_copy(own_one, buffer.at[0], sem.at[0]),
        pltpu.make_async_copy(mine, buffer.at[1], sem.at[1]),
        pltpu.make_async_copy(own_two, buffer.at[2], sem.at[2]),
        pltpu.make_async_copy(theirs, buffer.at[3], sem.at[3]),
    )
    for copy in copies:
        copy.start()
    return copies


def finish(copies):
    for copy in copies:
        copy.wait()


def lane_halves(shape):
    lane = lax.broadcasted_iota(jnp.int32, shape, len(shape) - 1)
    return lane < DH


def normalise(x):
    centre = x - jnp.mean(x, -1, keepdims=True)
    scale = lax.rsqrt(jnp.mean(centre * centre, -1, keepdims=True) + EPSILON)
    return centre * scale, scale


def gelu_parts(a):
    square = jnp.exp(-0.5 * a * a)
    size = jnp.abs(a)
    t = 1.0 / (1.0 + (0.3275911 * 0.7071067811865476) * size)
    poly = t * (
        0.127414796
        + t * (-0.142248368 + t * (0.7107068705 + t * (-0.7265760135 + t * 0.5307027145)))
    )
    tail = poly * square
    phi = jnp.where(a >= 0, 1.0 - tail, tail)
    return a * phi, phi + a * square * 0.3989422804014327


def project(hidden_low, weight, query_bias, value_bias, query_ref, pair_ref):
    def one(index, carry):
        triple = dot(hidden_low, weight[index])
        width = triple.shape[1] // 3
        query = (triple[:, :width] + query_bias[index]).astype(BF16)
        query_ref[index] = query * BF16(DH ** (-0.5))
        pair_ref[index, :, :width] = triple[:, width : 2 * width].astype(BF16)
        pair_ref[index, :, width:] = (triple[:, 2 * width :] + value_bias[index]).astype(BF16)
        return carry

    lax.fori_loop(0, 4, one, 0)


def first_kernel(tokens, weight_own, weight_mine, weight_theirs, query_bias, value_bias, query_ref, pair_ref, buffer, sem):
    core = lax.rem(lax.axis_index("wide"), 2)
    copies = start_quarters(
        (weight_own.at[core], weight_own.at[1 - core]), weight_mine, weight_theirs, buffer, sem, core
    )
    finish(copies)
    project(tokens[...], buffer, query_bias, value_bias, query_ref, pair_ref)


def forward_kernel(layer, last, *refs):
    (bias, query, pair, remote, hidden, wo_own, wo_mine, wo_theirs, we_own, we_mine, we_theirs, ws_own, ws_mine, ws_theirs, vectors, expand_bias), refs = refs[:16], refs[16:]
    if not last:
        (wi_own, wi_mine, wi_theirs, query_bias, value_bias), refs = refs[:5], refs[5:]
    (mixed_ref, total_ref, normed_ref, first_ref, first_scale, active_ref, slope_ref, second_ref, second_scale, hidden_ref), refs = refs[:10], refs[10:]
    if not last:
        (low_ref, query_ref, pair_ref), refs = refs[:3], refs[3:]
    (wo, we, ws, acc, sem), refs = refs[:5], refs[5:]
    core = lax.rem(lax.axis_index("wide"), 2)
    units = we.shape[2]
    wo_copies = start_quarters((wo_own.at[layer, core], wo_own.at[layer, 1 - core]), wo_mine, wo_theirs, wo, sem.at[0], core)

    def columns(index):
        return we_own.at[layer, :, pl.ds(pl.multiple_of(index * units, 128), units)]

    we_copies = start_quarters((columns(core), columns(1 - core)), we_mine, we_theirs, we, sem.at[1], core)
    ws_copies = start_quarters((ws_own.at[layer, core], ws_own.at[layer, 1 - core]), ws_mine, ws_theirs, ws, sem.at[2], core)
    if not last:
        wi = refs[0]
        wi_copies = start_quarters((wi_own.at[core], wi_own.at[1 - core]), wi_mine, wi_theirs, wi, sem.at[3], core)
    shift = bias[0]
    rows, width = query.shape[1], query.shape[2]
    acc[...] = hidden[...] + vectors[0:1]
    finish(wo_copies)
    halves = lane_halves((rows, width))

    def one_pair(index, carry):
        there = lax.rem(index + 2, 4)
        queries = query[index]
        key_here, value_here = pair[index, :, :width], pair[index, :, width:]
        key_there, value_there = remote[there, :, :width], remote[there, :, width:]
        mixed, total = [], []
        for part in range(2):
            mask = halves if part == 0 else jnp.logical_not(halves)
            masked = jnp.where(mask, queries, BF16(0))
            here = dot_rt(masked, key_here)
            away = dot_rt(masked, key_there)
            peak = jnp.maximum(jnp.max(here, -1, keepdims=True), jnp.max(away, -1, keepdims=True) + shift)
            here = jnp.exp(here - peak)
            away = jnp.exp(away - (peak - shift))
            weight = jnp.sum(here, -1, keepdims=True) + jnp.sum(away, -1, keepdims=True)
            both = dot(here.astype(BF16), value_here) + dot(away.astype(BF16), value_there)
            mixed.append(both * (1.0 / weight))
            total.append(jnp.broadcast_to(peak + jnp.log(weight), (rows, width)))
        low = jnp.where(halves, mixed[0], mixed[1]).astype(BF16)
        mixed_ref[index] = low
        totals = jnp.where(halves, total[0], total[1]).T
        total_ref[index] = jnp.concatenate([totals[0:8], totals[DH : DH + 8]], 0)
        acc[...] += dot(low, wo[index])
        return carry

    lax.fori_loop(0, 4, one_pair, 0)
    first, scale = normalise(acc[...])
    first_ref[...] = first
    first_scale[...] = scale
    normed = first * vectors[1:2] + vectors[2:3]
    normed_low = normed.astype(BF16)
    normed_ref[...] = normed_low
    acc[...] = normed + vectors[3:4]
    finish(we_copies)
    finish(ws_copies)

    def one_quarter(index, carry):
        active, slope = gelu_parts(dot(normed_low, we[index]) + expand_bias[index])
        low = active.astype(BF16)
        active_ref[index] = low
        slope_ref[index] = slope.astype(BF16)
        acc[...] += dot(low, ws[index])
        return carry

    lax.fori_loop(0, 4, one_quarter, 0)
    second, scale = normalise(acc[...])
    second_ref[...] = second
    second_scale[...] = scale
    result = second * vectors[4:5] + vectors[5:6]
    hidden_ref[...] = result
    if not last:
        low_ref[...] = result.astype(BF16)
        finish(wi_copies)
        project(low_ref[...], wi, query_bias, value_bias, query_ref, pair_ref)


def column_sum(x):
    return jnp.sum(x, 0, keepdims=True)


def norm_backward(grad, normed, scale, gain):
    scaled = grad * gain
    return (
        scaled - jnp.mean(scaled, -1, keepdims=True) - normed * jnp.mean(scaled * normed, -1, keepdims=True)
    ) * scale


def block_kernel(layer, *refs):
    (grad, second, second_scale, active, slope, normed, first, first_scale, mixed, vectors, wo_own, wo_mine, wo_theirs, we_own, we_mine, we_theirs, ws_own, ws_mine, ws_theirs), refs = refs[:19], refs[19:]
    (shrink_ref, expand_ref, output_ref, summed_ref, mixed_grad_ref, inner_ref, vector_ref, expand_bias_ref), refs = refs[:8], refs[8:]
    wo, we, ws, acc, turned, sem = refs
    core = lax.rem(lax.axis_index("wide"), 2)
    units = we.shape[2]
    ws_copies = start_quarters((ws_own.at[layer, core], ws_own.at[layer, 1 - core]), ws_mine, ws_theirs, ws, sem.at[2], core)

    def columns(index):
        return we_own.at[layer, :, pl.ds(pl.multiple_of(index * units, 128), units)]

    we_copies = start_quarters((columns(core), columns(1 - core)), we_mine, we_theirs, we, sem.at[1], core)
    wo_copies = start_quarters((wo_own.at[layer, core], wo_own.at[layer, 1 - core]), wo_mine, wo_theirs, wo, sem.at[0], core)
    rows, width = mixed.shape[1], mixed.shape[2]
    incoming = grad[...].astype(F32)
    widened = norm_backward(incoming, second[...], second_scale[...], vectors[4:5])
    vector_ref[0:1] = column_sum(incoming)
    vector_ref[1:2] = column_sum(incoming * second[...])
    vector_ref[2:3] = column_sum(widened)
    acc[...] = widened
    branch = widened.astype(BF16)
    turned[...] = normed[...].T
    finish(ws_copies)
    finish(we_copies)

    def one_quarter(index, carry):
        active_grad = dot_rt(branch, ws[index])
        inner = (active_grad * slope[index].astype(F32)).astype(BF16)
        shrink_ref[index] = dot_lt(active[index], branch).astype(BF16)
        expand_ref[index] = dot(turned[...], inner).astype(BF16)
        expand_bias_ref[index] = jnp.broadcast_to(column_sum(inner.astype(F32)), expand_bias_ref.shape[1:])
        acc[...] += dot_rt(inner, we[index])
        return carry

    lax.fori_loop(0, 4, one_quarter, 0)
    outgoing = acc[...]
    summed = norm_backward(outgoing, first[...], first_scale[...], vectors[1:2])
    vector_ref[3:4] = column_sum(outgoing)
    vector_ref[4:5] = column_sum(outgoing * first[...])
    vector_ref[5:6] = column_sum(summed)
    vector_ref[6:8] = jnp.zeros((2, summed.shape[1]), F32)
    summed_ref[...] = summed
    low = summed.astype(BF16)
    finish(wo_copies)
    half = lax.broadcasted_iota(jnp.int32, (16, width), 1) // DH
    which = lax.broadcasted_iota(jnp.int32, (16, width), 0) // 8
    selector = (half == which).astype(F32)

    def one_pair(index, carry):
        mixed_grad = dot_rt(low, wo[index]).astype(BF16)
        mixed_grad_ref[index] = mixed_grad
        output_ref[index] = dot_lt(mixed[index], low).astype(BF16)
        product = mixed_grad.astype(F32) * mixed[index].astype(F32)
        inner_ref[index] = lax.dot_general(
            selector, product, (((1,), (1,)), ((), ())), precision=lax.Precision.HIGHEST, preferred_element_type=F32
        )
        return carry

    lax.fori_loop(0, 4, one_pair, 0)


def attention_kernel(bias, query, pair, remote, mixed_grad, total, inner, query_grad_ref, here_ref, away_ref):
    rows, width = query.shape[1], query.shape[2]
    halves = lane_halves((rows, width))
    shift = bias[0]

    def one_pair(index, carry):
        there = lax.rem(index + 2, 4)
        queries, grads = query[index], mixed_grad[index]
        turned = None
        for side in range(2):
            source, place = (pair, index) if side == 0 else (remote, there)
            keys, values = source[place, :, :width], source[place, :, width:]
            key_grad = value_grad = None
            for part in range(2):
                mask = halves if part == 0 else jnp.logical_not(halves)
                masked_query = jnp.where(mask, queries, BF16(0))
                masked_grad = jnp.where(mask, grads, BF16(0))
                masked_key = jnp.where(mask, keys, BF16(0))
                level = total[index, 8 * part : 8 * part + 1]
                if side == 1:
                    level = level - shift
                weights = jnp.exp(dot_rt(keys, masked_query) - level)
                update = dot(weights.astype(BF16), masked_grad)
                value_grad = update if value_grad is None else value_grad + update
                slopes = dot_rt(values, masked_grad) - inner[index, 8 * part : 8 * part + 1]
                slopes = (weights * slopes).astype(BF16)
                update = dot(slopes, masked_query)
                key_grad = update if key_grad is None else key_grad + update
                update = dot_lt(masked_key, slopes)
                turned = update if turned is None else turned + update
            if side == 0:
                here_ref[index, :, :width] = key_grad
                here_ref[index, :, width:] = value_grad
            else:
                away_ref[there, :, :width] = key_grad.astype(BF16)
                away_ref[there, :, width:] = value_grad.astype(BF16)
        query_grad_ref[index] = (turned * DH ** (-0.5)).T.astype(BF16)
        return carry

    lax.fori_loop(0, 4, one_pair, 0)


def input_kernel(query_grad, here, away, hidden_low, summed, wi_own, wi_mine, wi_theirs, weight_ref, grad_ref, query_bias_ref, value_bias_ref, wi, turned, acc, sem):
    core = lax.rem(lax.axis_index("wide"), 2)
    copies = start_quarters((wi_own.at[core], wi_own.at[1 - core]), wi_mine, wi_theirs, wi, sem, core)
    width = query_grad.shape[2]
    turned[...] = hidden_low[...].T
    acc[...] = summed[...]
    finish(copies)

    def one(index, carry):
        pair_grad = (here[index] + away[index].astype(F32)).astype(BF16)
        triple = jnp.concatenate([query_grad[index], pair_grad], 1)
        weight_ref[index] = dot(turned[...], triple).astype(BF16)
        acc[...] += dot_rt(triple, wi[index])
        sums = column_sum(triple.astype(F32))
        query_bias_ref[index] = jnp.broadcast_to(sums[:, :width], query_bias_ref.shape[1:])
        value_bias_ref[index] = jnp.broadcast_to(sums[:, 2 * width :], value_bias_ref.shape[1:])
        return carry

    lax.fori_loop(0, 4, one, 0)
    grad_ref[...] = acc[...]


VM = pl.BlockSpec(memory_space=pltpu.VMEM)
AN = pl.BlockSpec(memory_space=pl.ANY)
SM = pl.BlockSpec(memory_space=pltpu.SMEM)


def shaped(dtype, *dims):
    return jax.ShapeDtypeStruct(dims, dtype)


def cost(flops, size):
    return pl.CostEstimate(flops=flops, bytes_accessed=size, transcendentals=0)


def call(body, name, ins, outs, scratch, args, flops=10**9):
    return pl.pallas_call(
        body,
        out_shape=outs,
        in_specs=ins,
        out_specs=[VM] * len(outs),
        scratch_shapes=scratch,
        compiler_params=pltpu.CompilerParams(vmem_limit_bytes=60 * 2**20),
        cost_estimate=cost(flops, 10**7),
        name=name,
    )(*args)


def permutations(mesh_shape):
    wide, narrow = mesh_shape
    line = lambda w, y: w * narrow + y
    every = [(w, y) for w in range(wide) for y in range(narrow)]
    swap = [(line(w, y), line((w & ~1) | y, w & 1)) for w, y in every]
    across = [(line(w, y), line(w, 1 - y)) for w, y in every]
    partner = [(line(w, y), line(w ^ 1, y)) for w, y in every]
    return swap, across, partner


def local(
    tokens, input_weight, query_bias, value_bias, output_weight, output_bias, first_gain, first_shift,
    expand_weight, expand_bias, shrink_weight, shrink_bias, second_gain, second_shift, lengths, bucket, cotangent,
):
    wide, narrow = lax.axis_size("wide"), lax.axis_size("narrow")
    assert narrow == 2 and wide % 2 == 0
    swap, across, partner = permutations((wide, narrow))
    core = lax.axis_index("wide") % 2
    send = lambda x, pairs: lax.ppermute(x, AXES, pairs)
    layers, depth = input_weight.shape[0], input_weight.shape[1]
    rows = tokens.shape[0]
    width = input_weight.shape[3] // 2
    units = expand_weight.shape[2] // 2

    tokens = send(tokens, swap)
    single = send(jnp.broadcast_to(bucket, (8, 128)).astype(F32), swap)[0, 0] < 0.5
    shift = jnp.where(single, 0.0, MASKED).astype(F32).reshape(1)

    input_own = (
        input_weight.reshape(layers, depth, 3, 2, width).transpose(0, 3, 1, 2, 4).reshape(layers, 2, depth, 3 * width)
    )
    output_own = output_weight.reshape(layers, 2, width, depth)
    shrink_own = shrink_weight.reshape(layers, 2, units, depth)
    pick = lambda x: lax.dynamic_index_in_dim(x, core, 0, keepdims=False)

    small = jnp.concatenate([query_bias, value_bias, expand_bias], 1)
    small_away = send(small, across)

    def fetch(piece):
        mine = send(piece, across)
        return mine, send(mine, partner)

    fetched = []
    for layer in range(layers):
        fetched.append((
            fetch(pick(input_own[layer])),
            fetch(pick(output_own[layer])),
            fetch(lax.dynamic_slice_in_dim(expand_weight[layer], core * units, units, 1)),
            fetch(pick(shrink_own[layer])),
        ))

    def quarters(own, away, at, size):
        own = own[:, at : at + 2 * size].reshape(layers, 2, 1, size)
        away = away[:, at : at + 2 * size].reshape(layers, 2, 1, size)
        both = jnp.stack([own, away], 2)
        both = jnp.where(core == 0, both, both[:, ::-1])
        return both.reshape(layers, 4, 1, size)

    query_biases = quarters(small, small_away, 0, width)
    value_biases = quarters(small, small_away, 2 * width, width)
    expand_biases = quarters(small, small_away, 4 * width, units)
    vectors = jnp.stack(
        [output_bias, first_gain, first_shift, shrink_bias, second_gain, second_shift, output_bias, output_bias], 1
    )

    wi_scratch = pltpu.VMEM((4, depth, 3 * width), BF16)
    wo_scratch = pltpu.VMEM((4, width, depth), BF16)
    we_scratch = pltpu.VMEM((4, depth, units), BF16)
    ws_scratch = pltpu.VMEM((4, units, depth), BF16)
    acc_scratch = pltpu.VMEM((rows, depth), F32)
    turn_scratch = pltpu.VMEM((depth, rows), BF16)
    query_shape = shaped(BF16, 4, rows, width)
    pair_shape = shaped(BF16, 4, rows, 2 * width)
    row_shape = shaped(F32, rows, depth)
    low_shape = shaped(BF16, rows, depth)
    scale_shape = shaped(F32, rows, 1)
    stat_shape = shaped(F32, 4, 16, rows)
    wide_shape = shaped(BF16, 4, rows, units)

    query, pair = call(
        first_kernel, "first",
        [VM, AN, AN, AN, VM, VM], [query_shape, pair_shape],
        [wi_scratch, pltpu.SemaphoreType.DMA((4,))],
        (tokens, input_own[0], *fetched[0][0], query_biases[0], value_biases[0]),
    )
    hidden, low = tokens.astype(F32), tokens
    saved = []
    for layer in range(layers):
        last = layer == layers - 1
        remote = send(pair, partner)
        ins = [SM, VM, VM, VM, VM] + [AN] * 9 + [VM, VM]
        args = [shift, query, pair, remote, hidden, output_own, *fetched[layer][1], expand_weight, *fetched[layer][2], shrink_own, *fetched[layer][3], vectors[layer], expand_biases[layer]]
        outs = [query_shape, stat_shape, low_shape, row_shape, scale_shape, wide_shape, wide_shape, row_shape, scale_shape, row_shape]
        scratch = [wo_scratch, we_scratch, ws_scratch, acc_scratch, pltpu.SemaphoreType.DMA((4, 4))]
        if not last:
            ins += [AN] * 3 + [VM, VM]
            args += [input_own[layer + 1], *fetched[layer + 1][0], query_biases[layer + 1], value_biases[layer + 1]]
            outs += [low_shape, query_shape, pair_shape]
            scratch += [wi_scratch]
        results = call(functools.partial(forward_kernel, layer, last), f"forward_{layer}", ins, outs, scratch, args, 5 * 10**9)
        saved.append((low, query, pair, remote) + tuple(results[:9]))
        hidden = results[9]
        if not last:
            low, query, pair = results[10:]
    layer_output = send(hidden.astype(BF16), swap).astype(F32)

    grad = send(cotangent, swap)
    collected = [None] * layers
    for layer in reversed(range(layers)):
        low, query, pair, remote, mixed, total, normed, first, first_scale, active, slope, second, second_scale = saved[layer]
        shrink_grad, expand_grad, output_grad, summed, mixed_grad, inner, vector_grad, expand_bias_grad = call(
            functools.partial(block_kernel, layer), f"block_{layer}",
            [VM] * 10 + [AN] * 9,
            [shaped(BF16, 4, units, depth), shaped(BF16, 4, depth, units), shaped(BF16, 4, width, depth), row_shape, query_shape, stat_shape, shaped(F32, 8, depth), shaped(F32, 4, 8, units)],
            [wo_scratch, we_scratch, ws_scratch, acc_scratch, turn_scratch, pltpu.SemaphoreType.DMA((3, 4))],
            (grad, second, second_scale, active, slope, normed, first, first_scale, mixed, vectors[layer], output_own, *fetched[layer][1], expand_weight, *fetched[layer][2], shrink_own, *fetched[layer][3]),
            5 * 10**9,
        )
        query_grad, here, away = call(
            attention_kernel, f"attention_{layer}",
            [SM] + [VM] * 6, [query_shape, shaped(F32, 4, rows, 2 * width), pair_shape], [],
            (shift, query, pair, remote, mixed_grad, total, inner), 5 * 10**9,
        )
        back = send(away, partner)
        input_grad, grad, query_bias_grad, value_bias_grad = call(
            input_kernel, f"input_{layer}",
            [VM] * 5 + [AN] * 3,
            [shaped(BF16, 4, depth, 3 * width), row_shape, shaped(F32, 4, 8, width), shaped(F32, 4, 8, width)],
            [wi_scratch, turn_scratch, acc_scratch, pltpu.SemaphoreType.DMA((4,))],
            (query_grad, here, back, low, summed, input_own[layer], *fetched[layer][0]), 2 * 10**9,
        )
        collected[layer] = (shrink_grad, expand_grad, output_grad, input_grad, vector_grad, expand_bias_grad, query_bias_grad, value_bias_grad)
    input_rows = send(grad.astype(BF16), swap).astype(F32)
    return reduce_all(collected, layer_output, input_rows, send, core, across, partner, wide, layers, depth, width, units)


def reduce_all(collected, layer_output, input_rows, send, core, across, partner, wide, layers, depth, width, units):
    names = list(zip(*collected))
    shrink_grad, expand_grad, output_grad, input_grad = (jnp.stack(item, 1) for item in names[:4])
    vector_grad = jnp.stack(names[4], 0)
    narrow_rows = jnp.stack(
        [jnp.concatenate([q[:, 0], v[:, 0], e[:, 0]], 1) for e, q, v in zip(names[5], names[6], names[7])], 1
    )
    same = [[w for w in range(wide) if w % 2 == c] for c in range(2)]

    def reduce_quarters(x):
        mine = (x[:2].astype(F32) + send(x[2:], partner).astype(F32)).astype(BF16)
        mine = (mine[0].astype(F32) + send(mine[1], across).astype(F32)).astype(BF16)
        return mine

    parts = [reduce_quarters(x) for x in (shrink_grad, expand_grad, output_grad, input_grad, narrow_rows.astype(BF16))]
    flat = jnp.concatenate([p.reshape(-1, 512) for p in parts], 0)
    flat = lax.psum(flat, "wide", axis_index_groups=same)
    done, at = [], 0
    for p in parts:
        size = p.size // 512
        done.append(flat[at : at + size].reshape(p.shape))
        at += size
    vector_grad = lax.psum(vector_grad, AXES)

    def spread(x):
        there = send(x, partner)
        x, there = x.astype(F32), there.astype(F32)
        return jnp.where(core == 0, x, there), jnp.where(core == 0, there, x)

    shrink_one, shrink_two = spread(done[0])
    expand_one, expand_two = spread(done[1])
    output_one, output_two = spread(done[2])
    input_one, input_two = spread(done[3])
    rows_one, rows_two = spread(done[4])
    triple = lambda x: x.reshape(layers, depth, 3, width)
    columns = lambda a, b: jnp.concatenate([rows_one[:, a:b], rows_two[:, a:b]], 1)
    return (
        layer_output,
        input_rows,
        jnp.concatenate([triple(input_one), triple(input_two)], 3),
        columns(0, width),
        columns(width, 2 * width),
        jnp.concatenate([output_one, output_two], 1),
        vector_grad[:, 5],
        vector_grad[:, 4],
        vector_grad[:, 3],
        jnp.concatenate([expand_one, expand_two], 2),
        columns(2 * width, 2 * width + units),
        jnp.concatenate([shrink_one, shrink_two], 1),
        vector_grad[:, 2],
        vector_grad[:, 1],
        vector_grad[:, 0],
    )


def solution(mesh):
    split = P(AXES, None)
    in_specs = (
        split, P(None, None, None, "narrow"), P(None, "narrow"), P(None, "narrow"), P(None, "narrow", None), P(), P(), P(),
        P(None, None, "narrow"), P(None, "narrow"), P(None, "narrow", None), P(), P(), P(), P("wide"), P("wide"), split,
    )
    out_specs = (
        split, split, P(None, None, None, "narrow"), P(None, "narrow"), P(None, "narrow"), P(None, "narrow", None), P(), P(), P(),
        P(None, None, "narrow"), P(None, "narrow"), P(None, "narrow", None), P(), P(), P(),
    )
    return jax.shard_map(local, mesh=mesh, in_specs=in_specs, out_specs=out_specs, check_vma=False)
```

```python
import functools

import jax
import jax.numpy as jnp
from jax import lax
from jax.experimental import pallas as pl
from jax.experimental.pallas import tpu as pltpu
from jax.sharding import PartitionSpec as P

DH = 64
EPSILON = 1e-12
MASKED = -1e9
AXES = ("wide", "narrow")
F32 = jnp.float32
BF16 = jnp.bfloat16
LAYER_VECTORS = 6


def dot(a, b):
    return lax.dot_general(a, b, (((1,), (0,)), ((), ())), preferred_element_type=F32)


def dot_rt(a, b):
    return lax.dot_general(a, b, (((1,), (1,)), ((), ())), preferred_element_type=F32)


def dot_lt(a, b):
    return lax.dot_general(a, b, (((0,), (0,)), ((), ())), preferred_element_type=F32)


def start_quarters(own, mine, theirs, buffer, sem, core):
    own_one, own_two = own
    copies = (
        pltpu.make_async_copy(own_one, buffer.at[0], sem.at[0]),
        pltpu.make_async_copy(mine, buffer.at[1], sem.at[1]),
        pltpu.make_async_copy(own_two, buffer.at[2], sem.at[2]),
        pltpu.make_async_copy(theirs, buffer.at[3], sem.at[3]),
    )
    for copy in copies:
        copy.start()
    return copies


def finish(copies):
    for copy in copies:
        copy.wait()


def lane_halves(shape):
    lane = lax.broadcasted_iota(jnp.int32, shape, len(shape) - 1)
    return lane < DH


def normalise(x):
    centre = x - jnp.mean(x, -1, keepdims=True)
    scale = lax.rsqrt(jnp.mean(centre * centre, -1, keepdims=True) + EPSILON)
    return centre * scale, scale


def gelu_parts(a):
    square = jnp.exp(-0.5 * a * a)
    size = jnp.abs(a)
    t = 1.0 / (1.0 + (0.3275911 * 0.7071067811865476) * size)
    poly = t * (
        0.127414796
        + t * (-0.142248368 + t * (0.7107068705 + t * (-0.7265760135 + t * 0.5307027145)))
    )
    tail = poly * square
    phi = jnp.where(a >= 0, 1.0 - tail, tail)
    return a * phi, phi + a * square * 0.3989422804014327


def project(hidden_low, weight, query_bias, value_bias, query_ref, pair_ref):
    def one(index, carry):
        triple = dot(hidden_low, weight[index])
        width = triple.shape[1] // 3
        query = (triple[:, :width] + query_bias[index]).astype(BF16)
        query_ref[index] = query * BF16(DH ** (-0.5))
        pair_ref[index, :, :width] = triple[:, width : 2 * width].astype(BF16)
        pair_ref[index, :, width:] = (triple[:, 2 * width :] + value_bias[index]).astype(BF16)
        return carry

    lax.fori_loop(0, 4, one, 0)


def first_kernel(tokens, weight_own, weight_mine, weight_theirs, query_bias, value_bias, query_ref, pair_ref, buffer, sem):
    core = lax.rem(lax.axis_index("wide"), 2)
    copies = start_quarters(
        (weight_own.at[core], weight_own.at[1 - core]), weight_mine, weight_theirs, buffer, sem, core
    )
    finish(copies)
    project(tokens[...], buffer, query_bias, value_bias, query_ref, pair_ref)


def forward_kernel(layer, last, *refs):
    (bias, query, pair, remote, hidden, wo_own, wo_mine, wo_theirs, we_own, we_mine, we_theirs, ws_own, ws_mine, ws_theirs, vectors, expand_bias), refs = refs[:16], refs[16:]
    if not last:
        (wi_own, wi_mine, wi_theirs, query_bias, value_bias), refs = refs[:5], refs[5:]
    (mixed_ref, total_ref, normed_ref, first_ref, first_scale, active_ref, slope_ref, second_ref, second_scale, hidden_ref), refs = refs[:10], refs[10:]
    if not last:
        (low_ref, query_ref, pair_ref), refs = refs[:3], refs[3:]
    (wo, we, ws, acc, sem), refs = refs[:5], refs[5:]
    core = lax.rem(lax.axis_index("wide"), 2)
    units = we.shape[2]
    wo_copies = start_quarters((wo_own.at[layer, core], wo_own.at[layer, 1 - core]), wo_mine, wo_theirs, wo, sem.at[0], core)

    def columns(index):
        return we_own.at[layer, :, pl.ds(pl.multiple_of(index * units, 128), units)]

    we_copies = start_quarters((columns(core), columns(1 - core)), we_mine, we_theirs, we, sem.at[1], core)
    ws_copies = start_quarters((ws_own.at[layer, core], ws_own.at[layer, 1 - core]), ws_mine, ws_theirs, ws, sem.at[2], core)
    if not last:
        wi = refs[0]
        wi_copies = start_quarters((wi_own.at[core], wi_own.at[1 - core]), wi_mine, wi_theirs, wi, sem.at[3], core)
    shift = bias[0]
    rows, width = query.shape[1], query.shape[2]
    acc[...] = hidden[...] + vectors[0:1]
    finish(wo_copies)
    halves = lane_halves((rows, width))

    def one_pair(index, carry):
        there = lax.rem(index + 2, 4)
        queries = query[index]
        key_here, value_here = pair[index, :, :width], pair[index, :, width:]
        key_there, value_there = remote[there, :, :width], remote[there, :, width:]
        mixed, total = [], []
        for part in range(2):
            mask = halves if part == 0 else jnp.logical_not(halves)
            masked = jnp.where(mask, queries, BF16(0))
            here = dot_rt(masked, key_here)
            away = dot_rt(masked, key_there)
            peak = jnp.maximum(jnp.max(here, -1, keepdims=True), jnp.max(away, -1, keepdims=True) + shift)
            here = jnp.exp(here - peak)
            away = jnp.exp(away - (peak - shift))
            weight = jnp.sum(here, -1, keepdims=True) + jnp.sum(away, -1, keepdims=True)
            both = dot(here.astype(BF16), value_here) + dot(away.astype(BF16), value_there)
            mixed.append(both * (1.0 / weight))
            total.append(jnp.broadcast_to(peak + jnp.log(weight), (rows, width)))
        low = jnp.where(halves, mixed[0], mixed[1]).astype(BF16)
        mixed_ref[index] = low
        totals = jnp.where(halves, total[0], total[1]).T
        total_ref[index] = jnp.concatenate([totals[0:8], totals[DH : DH + 8]], 0)
        acc[...] += dot(low, wo[index])
        return carry

    lax.fori_loop(0, 4, one_pair, 0)
    first, scale = normalise(acc[...])
    first_ref[...] = first
    first_scale[...] = scale
    normed = first * vectors[1:2] + vectors[2:3]
    normed_low = normed.astype(BF16)
    normed_ref[...] = normed_low
    acc[...] = normed + vectors[3:4]
    finish(we_copies)
    finish(ws_copies)

    def one_quarter(index, carry):
        active, slope = gelu_parts(dot(normed_low, we[index]) + expand_bias[index])
        low = active.astype(BF16)
        active_ref[index] = low
        slope_ref[index] = slope.astype(BF16)
        acc[...] += dot(low, ws[index])
        return carry

    lax.fori_loop(0, 4, one_quarter, 0)
    second, scale = normalise(acc[...])
    second_ref[...] = second
    second_scale[...] = scale
    result = second * vectors[4:5] + vectors[5:6]
    hidden_ref[...] = result
    if not last:
        low_ref[...] = result.astype(BF16)
        finish(wi_copies)
        project(low_ref[...], wi, query_bias, value_bias, query_ref, pair_ref)


def place_quarter(mine_ref, theirs_ref, index, at, size, value):
    @pl.when(index < 2)
    def _():
        mine_ref[index, at : at + size] = value

    @pl.when(index >= 2)
    def _():
        theirs_ref[index - 2, at : at + size] = value


def column_sum(x):
    return jnp.sum(x, 0, keepdims=True)


def norm_backward(grad, normed, scale, gain):
    scaled = grad * gain
    return (
        scaled - jnp.mean(scaled, -1, keepdims=True) - normed * jnp.mean(scaled * normed, -1, keepdims=True)
    ) * scale


def block_kernel(layer, *refs):
    (grad, second, second_scale, active, slope, normed, first, first_scale, mixed, vectors, wo_own, wo_mine, wo_theirs, we_own, we_mine, we_theirs, ws_own, ws_mine, ws_theirs), refs = refs[:19], refs[19:]
    (mine_ref, theirs_ref, summed_ref, mixed_grad_ref, inner_ref, vector_ref, expand_bias_ref), refs = refs[:7], refs[7:]
    wo, we, ws, acc, turned, sem = refs
    core = lax.rem(lax.axis_index("wide"), 2)
    units = we.shape[2]
    ws_copies = start_quarters((ws_own.at[layer, core], ws_own.at[layer, 1 - core]), ws_mine, ws_theirs, ws, sem.at[2], core)

    def columns(index):
        return we_own.at[layer, :, pl.ds(pl.multiple_of(index * units, 128), units)]

    we_copies = start_quarters((columns(core), columns(1 - core)), we_mine, we_theirs, we, sem.at[1], core)
    wo_copies = start_quarters((wo_own.at[layer, core], wo_own.at[layer, 1 - core]), wo_mine, wo_theirs, wo, sem.at[0], core)
    rows, width = mixed.shape[1], mixed.shape[2]

    def put(index, at, size, value):
        place_quarter(mine_ref, theirs_ref, index, at, size, value)

    incoming = grad[...].astype(F32)
    widened = norm_backward(incoming, second[...], second_scale[...], vectors[4:5])
    vector_ref[0:1] = column_sum(incoming)
    vector_ref[1:2] = column_sum(incoming * second[...])
    vector_ref[2:3] = column_sum(widened)
    acc[...] = widened
    branch = widened.astype(BF16)
    turned[...] = normed[...].T
    finish(ws_copies)
    finish(we_copies)

    def one_quarter(index, carry):
        active_grad = dot_rt(branch, ws[index])
        inner = (active_grad * slope[index].astype(F32)).astype(BF16)
        put(index, 0, units, dot_lt(active[index], branch).astype(BF16))
        put(index, units, turned.shape[0], dot(turned[...], inner).astype(BF16))
        expand_bias_ref[index] = jnp.broadcast_to(column_sum(inner.astype(F32)), expand_bias_ref.shape[1:])
        acc[...] += dot_rt(inner, we[index])
        return carry

    lax.fori_loop(0, 4, one_quarter, 0)
    outgoing = acc[...]
    summed = norm_backward(outgoing, first[...], first_scale[...], vectors[1:2])
    vector_ref[3:4] = column_sum(outgoing)
    vector_ref[4:5] = column_sum(outgoing * first[...])
    vector_ref[5:6] = column_sum(summed)
    vector_ref[6:8] = jnp.zeros((2, summed.shape[1]), F32)
    summed_ref[...] = summed
    low = summed.astype(BF16)
    finish(wo_copies)
    half = lax.broadcasted_iota(jnp.int32, (16, width), 1) // DH
    which = lax.broadcasted_iota(jnp.int32, (16, width), 0) // 8
    selector = (half == which).astype(F32)

    def one_pair(index, carry):
        mixed_grad = dot_rt(low, wo[index]).astype(BF16)
        mixed_grad_ref[index] = mixed_grad
        put(index, units + turned.shape[0], width, dot_lt(mixed[index], low).astype(BF16))
        product = mixed_grad.astype(F32) * mixed[index].astype(F32)
        inner_ref[index] = lax.dot_general(
            selector, product, (((1,), (1,)), ((), ())), precision=lax.Precision.HIGHEST, preferred_element_type=F32
        )
        return carry

    lax.fori_loop(0, 4, one_pair, 0)


def attention_kernel(bias, query, pair, remote, mixed_grad, total, inner, query_grad_ref, here_ref, away_ref):
    rows, width = query.shape[1], query.shape[2]
    halves = lane_halves((rows, width))
    shift = bias[0]

    def one_pair(index, carry):
        there = lax.rem(index + 2, 4)
        queries, grads = query[index], mixed_grad[index]
        turned = None
        for side in range(2):
            source, place = (pair, index) if side == 0 else (remote, there)
            keys, values = source[place, :, :width], source[place, :, width:]
            key_grad = value_grad = None
            for part in range(2):
                mask = halves if part == 0 else jnp.logical_not(halves)
                masked_query = jnp.where(mask, queries, BF16(0))
                masked_grad = jnp.where(mask, grads, BF16(0))
                masked_key = jnp.where(mask, keys, BF16(0))
                level = total[index, 8 * part : 8 * part + 1]
                if side == 1:
                    level = level - shift
                weights = jnp.exp(dot_rt(keys, masked_query) - level)
                update = dot(weights.astype(BF16), masked_grad)
                value_grad = update if value_grad is None else value_grad + update
                slopes = dot_rt(values, masked_grad) - inner[index, 8 * part : 8 * part + 1]
                slopes = (weights * slopes).astype(BF16)
                update = dot(slopes, masked_query)
                key_grad = update if key_grad is None else key_grad + update
                update = dot_lt(masked_key, slopes)
                turned = update if turned is None else turned + update
            if side == 0:
                here_ref[index, :, :width] = key_grad
                here_ref[index, :, width:] = value_grad
            else:
                away_ref[there, :, :width] = key_grad.astype(BF16)
                away_ref[there, :, width:] = value_grad.astype(BF16)
        query_grad_ref[index] = (turned * DH ** (-0.5)).T.astype(BF16)
        return carry

    lax.fori_loop(0, 4, one_pair, 0)


def input_kernel(query_grad, here, away, hidden_low, summed, wi_own, wi_mine, wi_theirs, mine_ref, theirs_ref, grad_ref, triple_ref, wi, turned, acc, sem):
    core = lax.rem(lax.axis_index("wide"), 2)
    copies = start_quarters((wi_own.at[core], wi_own.at[1 - core]), wi_mine, wi_theirs, wi, sem, core)
    turned[...] = hidden_low[...].T
    acc[...] = summed[...]
    finish(copies)

    def one(index, carry):
        pair_grad = (here[index] + away[index].astype(F32)).astype(BF16)
        triple = jnp.concatenate([query_grad[index], pair_grad], 1)
        place_quarter(mine_ref, theirs_ref, index, 0, turned.shape[0], dot(turned[...], triple).astype(BF16))
        acc[...] += dot_rt(triple, wi[index])
        triple_ref[index] = jnp.broadcast_to(column_sum(triple.astype(F32)), triple_ref.shape[1:])
        return carry

    lax.fori_loop(0, 4, one, 0)
    grad_ref[...] = acc[...]


VM = pl.BlockSpec(memory_space=pltpu.VMEM)
AN = pl.BlockSpec(memory_space=pl.ANY)
SM = pl.BlockSpec(memory_space=pltpu.SMEM)


def shaped(dtype, *dims):
    return jax.ShapeDtypeStruct(dims, dtype)


def cost(flops, size):
    return pl.CostEstimate(flops=flops, bytes_accessed=size, transcendentals=0)


def call(body, name, ins, outs, scratch, args, flops=10**9):
    return pl.pallas_call(
        body,
        out_shape=outs,
        in_specs=ins,
        out_specs=[VM] * len(outs),
        scratch_shapes=scratch,
        compiler_params=pltpu.CompilerParams(vmem_limit_bytes=60 * 2**20),
        cost_estimate=cost(flops, 10**7),
        name=name,
    )(*args)


def permutations(mesh_shape):
    wide, narrow = mesh_shape
    line = lambda w, y: w * narrow + y
    every = [(w, y) for w in range(wide) for y in range(narrow)]
    swap = [(line(w, y), line((w & ~1) | y, w & 1)) for w, y in every]
    across = [(line(w, y), line(w, 1 - y)) for w, y in every]
    partner = [(line(w, y), line(w ^ 1, y)) for w, y in every]
    return swap, across, partner


def local(
    tokens, input_weight, query_bias, value_bias, output_weight, output_bias, first_gain, first_shift,
    expand_weight, expand_bias, shrink_weight, shrink_bias, second_gain, second_shift, lengths, bucket, cotangent,
):
    wide, narrow = lax.axis_size("wide"), lax.axis_size("narrow")
    assert narrow == 2 and wide % 2 == 0
    swap, across, partner = permutations((wide, narrow))
    core = lax.axis_index("wide") % 2
    send = lambda x, pairs: lax.ppermute(x, AXES, pairs)
    layers, depth = input_weight.shape[0], input_weight.shape[1]
    rows = tokens.shape[0]
    width = input_weight.shape[3] // 2
    units = expand_weight.shape[2] // 2

    tokens = send(tokens, swap)
    single = send(jnp.broadcast_to(bucket, (8, 128)).astype(F32), swap)[0, 0] < 0.5
    shift = jnp.where(single, 0.0, MASKED).astype(F32).reshape(1)

    input_own = (
        input_weight.reshape(layers, depth, 3, 2, width).transpose(0, 3, 1, 2, 4).reshape(layers, 2, depth, 3 * width)
    )
    output_own = output_weight.reshape(layers, 2, width, depth)
    shrink_own = shrink_weight.reshape(layers, 2, units, depth)
    pick = lambda x: lax.dynamic_index_in_dim(x, core, 0, keepdims=False)

    small = jnp.concatenate([query_bias, value_bias, expand_bias], 1)
    small_away = send(small, across)

    def fetch(piece):
        mine = send(piece, across)
        return mine, send(mine, partner)

    fetched = []
    for layer in range(layers):
        fetched.append((
            fetch(pick(input_own[layer])),
            fetch(pick(output_own[layer])),
            fetch(lax.dynamic_slice_in_dim(expand_weight[layer], core * units, units, 1)),
            fetch(pick(shrink_own[layer])),
        ))

    def quarters(own, away, at, size):
        own = own[:, at : at + 2 * size].reshape(layers, 2, 1, size)
        away = away[:, at : at + 2 * size].reshape(layers, 2, 1, size)
        both = jnp.stack([own, away], 2)
        both = jnp.where(core == 0, both, both[:, ::-1])
        return both.reshape(layers, 4, 1, size)

    query_biases = quarters(small, small_away, 0, width)
    value_biases = quarters(small, small_away, 2 * width, width)
    expand_biases = quarters(small, small_away, 4 * width, units)
    vectors = jnp.stack(
        [output_bias, first_gain, first_shift, shrink_bias, second_gain, second_shift, output_bias, output_bias], 1
    )

    wi_scratch = pltpu.VMEM((4, depth, 3 * width), BF16)
    wo_scratch = pltpu.VMEM((4, width, depth), BF16)
    we_scratch = pltpu.VMEM((4, depth, units), BF16)
    ws_scratch = pltpu.VMEM((4, units, depth), BF16)
    acc_scratch = pltpu.VMEM((rows, depth), F32)
    turn_scratch = pltpu.VMEM((depth, rows), BF16)
    query_shape = shaped(BF16, 4, rows, width)
    pair_shape = shaped(BF16, 4, rows, 2 * width)
    row_shape = shaped(F32, rows, depth)
    low_shape = shaped(BF16, rows, depth)
    scale_shape = shaped(F32, rows, 1)
    stat_shape = shaped(F32, 4, 16, rows)
    wide_shape = shaped(BF16, 4, rows, units)

    query, pair = call(
        first_kernel, "first",
        [VM, AN, AN, AN, VM, VM], [query_shape, pair_shape],
        [wi_scratch, pltpu.SemaphoreType.DMA((4,))],
        (tokens, input_own[0], *fetched[0][0], query_biases[0], value_biases[0]),
    )
    hidden, low = tokens.astype(F32), tokens
    saved = []
    for layer in range(layers):
        last = layer == layers - 1
        remote = send(pair, partner)
        ins = [SM, VM, VM, VM, VM] + [AN] * 9 + [VM, VM]
        args = [shift, query, pair, remote, hidden, output_own, *fetched[layer][1], expand_weight, *fetched[layer][2], shrink_own, *fetched[layer][3], vectors[layer], expand_biases[layer]]
        outs = [query_shape, stat_shape, low_shape, row_shape, scale_shape, wide_shape, wide_shape, row_shape, scale_shape, row_shape]
        scratch = [wo_scratch, we_scratch, ws_scratch, acc_scratch, pltpu.SemaphoreType.DMA((4, 4))]
        if not last:
            ins += [AN] * 3 + [VM, VM]
            args += [input_own[layer + 1], *fetched[layer + 1][0], query_biases[layer + 1], value_biases[layer + 1]]
            outs += [low_shape, query_shape, pair_shape]
            scratch += [wi_scratch]
        results = call(functools.partial(forward_kernel, layer, last), f"forward_{layer}", ins, outs, scratch, args, 5 * 10**9)
        saved.append((low, query, pair, remote) + tuple(results[:9]))
        hidden = results[9]
        if not last:
            low, query, pair = results[10:]
    layer_output = send(hidden.astype(BF16), swap).astype(F32)

    grad = send(cotangent, swap)
    collected = [None] * layers
    for layer in reversed(range(layers)):
        low, query, pair, remote, mixed, total, normed, first, first_scale, active, slope, second, second_scale = saved[layer]
        mine, theirs, summed, mixed_grad, inner, vector_grad, expand_bias_grad = call(
            functools.partial(block_kernel, layer), f"block_{layer}",
            [VM] * 10 + [AN] * 9,
            [shaped(BF16, 2, units + depth + width, depth)] * 2 + [row_shape, query_shape, stat_shape, shaped(F32, 8, depth), shaped(F32, 4, 8, units)],
            [wo_scratch, we_scratch, ws_scratch, acc_scratch, turn_scratch, pltpu.SemaphoreType.DMA((3, 4))],
            (grad, second, second_scale, active, slope, normed, first, first_scale, mixed, vectors[layer], output_own, *fetched[layer][1], expand_weight, *fetched[layer][2], shrink_own, *fetched[layer][3]),
            5 * 10**9,
        )
        blocks = reduce_quarters(mine, theirs, send, partner, across)
        query_grad, here, away = call(
            attention_kernel, f"attention_{layer}",
            [SM] + [VM] * 6, [query_shape, shaped(F32, 4, rows, 2 * width), pair_shape], [],
            (shift, query, pair, remote, mixed_grad, total, inner), 5 * 10**9,
        )
        back = send(away, partner)
        mine, theirs, grad, triple_grad = call(
            input_kernel, f"input_{layer}",
            [VM] * 5 + [AN] * 3,
            [shaped(BF16, 2, depth, 3 * width)] * 2 + [row_shape, shaped(F32, 4, 8, 3 * width)],
            [wi_scratch, turn_scratch, acc_scratch, pltpu.SemaphoreType.DMA((4,))],
            (query_grad, here, back, low, summed, input_own[layer], *fetched[layer][0]), 2 * 10**9,
        )
        collected[layer] = (blocks, mine, theirs, vector_grad, expand_bias_grad, triple_grad)
    input_rows = send(grad.astype(BF16), swap).astype(F32)
    return finish_all(collected, layer_output, input_rows, send, core, across, partner, wide, layers, depth, width, units)


def reduce_quarters(mine, theirs, send, partner, across):
    mine = (mine.astype(F32) + send(theirs, partner).astype(F32)).astype(BF16)
    return (mine[0].astype(F32) + send(mine[1], across).astype(F32)).astype(BF16)


def finish_all(collected, layer_output, input_rows, send, core, across, partner, wide, layers, depth, width, units):
    same = [[w for w in range(wide) if w % 2 == c] for c in range(2)]
    smalls = []
    for blocks, mine, theirs, vector_grad, expand_bias_grad, triple_grad in collected:
        triple = jnp.pad(triple_grad[:, :1], ((0, 0), (0, 0), (0, depth - 3 * width)))
        expand = jnp.pad(expand_bias_grad[:, :1], ((0, 0), (0, 0), (0, depth - units)))
        smalls.append(jnp.concatenate([jnp.broadcast_to(vector_grad[:6], (4, 6, depth)), expand, triple], 1))
    small = jnp.concatenate(smalls, 1)
    done = []
    for layer in range(1, layers):
        blocks, mine, theirs = collected[layer][:3]
        inputs = reduce_quarters(mine, theirs, send, partner, across)
        blocks, inputs = lax.psum((blocks, inputs), "wide", axis_index_groups=same)
        pair = []
        for x in (blocks, inputs):
            there = send(x, partner)
            pair.append(jnp.where(core == 0, jnp.stack([x, there]), jnp.stack([there, x])))
        done.append(pair)
    blocks, mine, theirs = collected[0][:3]
    blocks, inputs, small = finish_call(blocks, mine, theirs, small, wide)
    done.insert(0, [blocks, inputs])
    shrink, expand, output, inputs = [], [], [], []
    for blocks, triple in done:
        blocks, triple = blocks.astype(F32), triple.astype(F32)
        shrink.append(blocks[:, :units].reshape(2 * units, depth))
        expand.append(blocks[:, units : units + depth].transpose(1, 0, 2).reshape(depth, 2 * units))
        output.append(blocks[:, units + depth : units + depth + width].reshape(2 * width, depth))
        inputs.append(triple[:, :depth].reshape(2, depth, 3, width).transpose(1, 2, 0, 3).reshape(depth, 3, 2 * width))
    small = small.reshape(2, layers, 8, depth)
    both = lambda at, a, b: small[:, :, at, a:b].transpose(1, 0, 2).reshape(layers, 2 * (b - a))
    vector = lambda at: small[0, :, at]
    return (
        layer_output,
        input_rows,
        jnp.stack(inputs),
        both(7, 0, width),
        both(7, 2 * width, 3 * width),
        jnp.stack(output),
        vector(5),
        vector(4),
        vector(3),
        jnp.stack(expand),
        both(6, 0, units),
        jnp.stack(shrink),
        vector(2),
        vector(1),
        vector(0),
    )


def finish_kernel(chips, *refs):
    (blocks, inputs_mine, inputs_theirs, small), refs = refs[:4], refs[4:]
    (blocks_out, inputs_out, small_out), refs = refs[:3], refs[3:]
    (held, held_inputs, *landed), refs = refs[:6], refs[6:]
    (core_inputs, mid_inputs, row_inputs, core_small, mid_small, row_small, sum_small, step_small), refs = refs[:8], refs[8:]
    ring_send, ring_recv, pair_send, pair_recv, step_send, step_recv = refs
    wide, narrow = lax.axis_index("wide"), lax.axis_index("narrow")
    core, chip = lax.rem(wide, 2), wide // 2
    odd = lax.rem(chip, 2)
    place = odd * (chips - 1 - chip // 2) + (1 - odd) * (chip // 2)

    def chip_at(position):
        position = lax.rem(position + chips, chips)
        late = position // (chips // 2)
        return late * (2 * (chips - 1 - position) + 1) + (1 - late) * (2 * position)

    def peer(index, other_core=0, other_narrow=0):
        side = core + other_core * (1 - 2 * core)
        return (index * 2 + side, narrow + other_narrow * (1 - 2 * narrow))

    right, left = peer(chip_at(place + 1)), peer(chip_at(place - 1))
    beside, across = peer(chip, 1, 0), peer(chip, 0, 1)
    steps = chips.bit_length() - 1
    bits = []
    for bit in range(steps):
        flag = lax.rem(chip // 2**bit, 2)
        bits.append(peer(chip + 2**bit * (1 - 2 * flag)))
    barrier = pltpu.get_barrier_semaphore()
    partners = [right, left, beside, across] + bits
    for device in partners:
        pl.semaphore_signal(barrier, inc=1, device_id=device, device_id_type=pl.DeviceIdType.MESH)
    pl.semaphore_wait(barrier, len(partners))

    sent = []

    def remote(source, target, send_sem, recv_sem, device):
        copy = pltpu.make_async_remote_copy(source, target, send_sem, recv_sem, device_id=device, device_id_type=pl.DeviceIdType.MESH)
        copy.start()
        sent.append(copy)
        return copy

    class Ring:
        def __init__(self, which, data, out, columns, slots):
            self.which, self.data, self.out, self.columns, self.slots = which, data, out, columns, slots
            self.size = data.shape[0] // chips
            self.now = [None, None]

        def rows(self, index):
            index = lax.rem(index + 2 * chips, chips)
            return pl.ds(pl.multiple_of(index * self.size, 16), self.size)

        def span(self, side):
            at, count = self.columns[side]
            return pl.ds(at, count)

        def start(self):
            for side in range(2):
                self.pass_on(side, 0, self.data.at[self.rows(place), self.span(side)], self.slots[side].at[0])

        def pass_on(self, side, step, source, target):
            self.now[side] = remote(source, target, ring_send.at[self.which, side, step], ring_recv.at[self.which, side, step], (right, left)[side])

        def tick(self, step):
            for side in range(2):
                way = 1 - 2 * side
                span = self.span(side)
                self.now[side].wait_recv()
                if step < chips - 1:
                    rows = self.rows(place - way * (step + 1))
                    total = self.data[rows, span].astype(F32) + self.slots[side][step].astype(F32)
                    total = total.astype(BF16)
                    self.data[rows, span] = total
                    if step < chips - 2:
                        self.pass_on(side, step + 1, self.data.at[rows, span], self.slots[side].at[step + 1])
                    else:
                        self.out[core, rows, span] = total
                        self.pass_on(side, step + 1, self.data.at[rows, span], self.out.at[core, rows, span])
                elif step < 2 * chips - 3:
                    rows = self.rows(place - way * (step - chips + 1))
                    where = self.out.at[core, rows, span]
                    self.pass_on(side, step + 1, where, where)

    def fill(target, value):
        target[0 : value.shape[0]] = value
        if value.shape[0] < target.shape[0]:
            target[value.shape[0] :] = jnp.zeros((target.shape[0] - value.shape[0], target.shape[1]), target.dtype)

    fill(held, blocks[...])
    half = held.shape[1] // 2
    first = Ring(0, held, blocks_out, ((0, half), (half, half)), landed[0:2])
    third = held_inputs.shape[1] // 3
    second = Ring(1, held_inputs, inputs_out, ((0, 2 * third), (2 * third, third)), landed[2:4])
    first.start()
    copy_inputs = remote(inputs_theirs, core_inputs, pair_send.at[0], pair_recv.at[0], beside)
    copy_small = remote(small.at[pl.ds(2, 2)], core_small, pair_send.at[1], pair_recv.at[1], beside)
    copy_small.wait_recv()
    mid_small[...] = small[1] + core_small[1]
    copy_small = remote(mid_small, row_small, pair_send.at[2], pair_recv.at[2], across)
    copy_inputs.wait_recv()
    mid_inputs[...] = (inputs_mine[1].astype(F32) + core_inputs[1].astype(F32)).astype(BF16)
    copy_inputs = remote(mid_inputs, row_inputs, pair_send.at[3], pair_recv.at[3], across)
    fill(held_inputs, (inputs_mine[0].astype(F32) + core_inputs[0].astype(F32)).astype(BF16))
    ticks = 2 * (chips - 1)
    delay = 3
    small_value = None
    for step in range(ticks + delay):
        if step < ticks:
            first.tick(step)
        if step == 0:
            copy_small.wait_recv()
            small_value = small[0] + core_small[0] + row_small[...]
        if 0 < step <= steps:
            copy_small.wait_recv()
            small_value = small_value + step_small[step - 1]
        if step < steps:
            sum_small[step] = small_value
            copy_small = remote(sum_small.at[step], step_small.at[step], step_send.at[step], step_recv.at[step], bits[step])
        if step == steps:
            small_out[core] = small_value
        if step == delay - 1:
            copy_inputs.wait_recv()
            total = held_inputs[0 : row_inputs.shape[0]].astype(F32) + row_inputs[...].astype(F32)
            held_inputs[0 : row_inputs.shape[0]] = total.astype(BF16)
            second.start()
        if step >= delay:
            second.tick(step - delay)
        if step == ticks:
            last = [
                remote(blocks_out.at[core], blocks_out.at[core], pair_send.at[4], pair_recv.at[4], beside),
                remote(small_out.at[core], small_out.at[core], pair_send.at[5], pair_recv.at[5], beside),
            ]
    last.append(remote(inputs_out.at[core], inputs_out.at[core], pair_send.at[6], pair_recv.at[6], beside))
    for copy in last:
        copy.wait_recv()
    for copy in sent:
        copy.wait_send()


def finish_call(blocks, inputs_mine, inputs_theirs, small, wide):
    chips = wide // 2
    size = lambda rows: -(-rows // (16 * chips)) * 16 * chips
    rows, depth = blocks.shape
    input_rows, columns = inputs_mine.shape[1:]
    tall, input_tall = size(rows), size(input_rows)
    steps = chips.bit_length() - 1
    slot = lambda tall, count: pltpu.VMEM((chips - 1, tall // chips, count), BF16)
    small_rows = small.shape[1]
    return pl.pallas_call(
        functools.partial(finish_kernel, chips),
        out_shape=[shaped(BF16, 2, tall, depth), shaped(BF16, 2, input_tall, columns), shaped(F32, 2, small_rows, depth)],
        in_specs=[VM] * 4,
        out_specs=[VM] * 3,
        scratch_shapes=[
            pltpu.VMEM((tall, depth), BF16),
            pltpu.VMEM((input_tall, columns), BF16),
            slot(tall, depth // 2),
            slot(tall, depth // 2),
            slot(input_tall, 2 * columns // 3),
            slot(input_tall, columns // 3),
            pltpu.VMEM((2, input_rows, columns), BF16),
            pltpu.VMEM((input_rows, columns), BF16),
            pltpu.VMEM((input_rows, columns), BF16),
            pltpu.VMEM((2, small_rows, depth), F32),
            pltpu.VMEM((small_rows, depth), F32),
            pltpu.VMEM((small_rows, depth), F32),
            pltpu.VMEM((steps, small_rows, depth), F32),
            pltpu.VMEM((steps, small_rows, depth), F32),
            pltpu.SemaphoreType.DMA((2, 2, 2 * (chips - 1))),
            pltpu.SemaphoreType.DMA((2, 2, 2 * (chips - 1))),
            pltpu.SemaphoreType.DMA((7,)),
            pltpu.SemaphoreType.DMA((7,)),
            pltpu.SemaphoreType.DMA((steps,)),
            pltpu.SemaphoreType.DMA((steps,)),
        ],
        compiler_params=pltpu.CompilerParams(collective_id=0, has_side_effects=True, vmem_limit_bytes=48 * 2**20),
        cost_estimate=cost(10**9, 10**7),
        name="finish",
    )(blocks, inputs_mine, inputs_theirs, small)


def solution(mesh):
    split = P(AXES, None)
    in_specs = (
        split, P(None, None, None, "narrow"), P(None, "narrow"), P(None, "narrow"), P(None, "narrow", None), P(), P(), P(),
        P(None, None, "narrow"), P(None, "narrow"), P(None, "narrow", None), P(), P(), P(), P("wide"), P("wide"), split,
    )
    out_specs = (
        split, split, P(None, None, None, "narrow"), P(None, "narrow"), P(None, "narrow"), P(None, "narrow", None), P(), P(), P(),
        P(None, None, "narrow"), P(None, "narrow"), P(None, "narrow", None), P(), P(), P(),
    )
    return jax.shard_map(local, mesh=mesh, in_specs=in_specs, out_specs=out_specs, check_vma=False)
```

```python
import functools

import jax
import jax.numpy as jnp
from jax import lax
from jax.experimental import pallas as pl
from jax.experimental.pallas import tpu as pltpu
from jax.sharding import PartitionSpec as P

DH = 64
EPSILON = 1e-12
MASKED = -1e9
AXES = ("wide", "narrow")
F32 = jnp.float32
BF16 = jnp.bfloat16
LAYER_VECTORS = 6


def dot(a, b):
    return lax.dot_general(a, b, (((1,), (0,)), ((), ())), preferred_element_type=F32)


def dot_rt(a, b):
    return lax.dot_general(a, b, (((1,), (1,)), ((), ())), preferred_element_type=F32)


def dot_lt(a, b):
    return lax.dot_general(a, b, (((0,), (0,)), ((), ())), preferred_element_type=F32)


def lane_halves(shape):
    lane = lax.broadcasted_iota(jnp.int32, shape, len(shape) - 1)
    return lane < DH


def normalise(x):
    centre = x - jnp.mean(x, -1, keepdims=True)
    scale = lax.rsqrt(jnp.mean(centre * centre, -1, keepdims=True) + EPSILON)
    return centre * scale, scale


def gelu_parts(a):
    square = jnp.exp(-0.5 * a * a)
    size = jnp.abs(a)
    t = 1.0 / (1.0 + (0.3275911 * 0.7071067811865476) * size)
    poly = t * (
        0.127414796
        + t * (-0.142248368 + t * (0.7107068705 + t * (-0.7265760135 + t * 0.5307027145)))
    )
    tail = poly * square
    phi = jnp.where(a >= 0, 1.0 - tail, tail)
    return a * phi, phi + a * square * 0.3989422804014327


class Links:
    def __init__(self):
        self.wide, self.narrow = lax.axis_index("wide"), lax.axis_index("narrow")
        self.core = lax.rem(self.wide, 2)
        self.chip = self.wide // 2
        self.bit = lax.rem(self.chip, 2)
        other_core, other_narrow = self.wide + 1 - 2 * self.core, 1 - self.narrow
        self.beside = (other_core, self.narrow)
        self.across = (self.wide, other_narrow)
        self.along = (self.wide + 2 * (1 - 2 * self.bit), self.narrow)
        self.opposite = (other_core, other_narrow)
        self.moved = self.core + self.narrow == 1

    def greet(self, devices):
        barrier = pltpu.get_barrier_semaphore()
        for device in devices:
            pl.semaphore_signal(barrier, inc=1, device_id=device, device_id_type=pl.DeviceIdType.MESH)
        pl.semaphore_wait(barrier, len(devices))


def remote(source, target, sems, at, device):
    return pltpu.make_async_remote_copy(
        source, target, sems[0].at[at], sems[1].at[at], device_id=device, device_id_type=pl.DeviceIdType.MESH
    )


class Weight:
    def __init__(self, links, number, own, buffer, local_sem, sems):
        self.links, self.number, self.own, self.buffer, self.local_sem, self.sems = links, number, own, buffer, local_sem, sems
        self.half = buffer.shape[1] // 2

    def rows(self, bit):
        return pl.ds(pl.multiple_of(bit * self.half, 16), self.half)

    def local_copies(self):
        core = self.links.core
        return [
            pltpu.make_async_copy(self.own(core, slice(None)), self.buffer.at[0], self.local_sem.at[2 * self.number]),
            pltpu.make_async_copy(self.own(1 - core, slice(None)), self.buffer.at[2], self.local_sem.at[2 * self.number + 1]),
        ]

    def hop(self, kind):
        links, rows = self.links, self.rows(self.links.bit)
        at = 4 * self.number + kind
        if kind == 0:
            return remote(self.own(links.core, rows), self.buffer.at[1, rows], self.sems, at, links.across)
        if kind == 1:
            return remote(self.buffer.at[1, rows], self.buffer.at[1, rows], self.sems, at, links.along)
        if kind == 3:
            rows = self.rows(1 - links.bit)
        return remote(self.buffer.at[1, rows], self.buffer.at[3, rows], self.sems, at, links.beside)

    def start(self):
        self.hop(0).start()

    def start_local(self):
        for copy in self.local_copies():
            copy.start()

    def relay(self):
        self.hop(0).wait_recv()
        self.hop(1).start()
        self.hop(2).start()

    def relay_again(self):
        self.hop(1).wait_recv()
        self.hop(3).start()

    def wait_own(self):
        for copy in self.local_copies():
            copy.wait()

    def wait_fetched(self):
        self.hop(2).wait_recv()
        self.hop(3).wait_recv()

    def wait_sent(self):
        for kind in range(4):
            self.hop(kind).wait_send()


def ordered(step):
    return lax.rem(2 * step, 4) + step // 2


def at_step(step, hooks):
    for number, hook in enumerate(hooks):
        if hook:

            @pl.when(step == number)
            def _(hook=hook):
                for action in hook:
                    action()


def all_forward(layers, *refs):
    (flag, tokens, cotangent, small, vectors, wi_own, wo_own, we_own, ws_own), refs = refs[:9], refs[9:]
    (rows_ref, tokens_in, cotangent_in, flag_in), refs = refs[:4], refs[4:]
    states = [refs[16 * layer : 16 * layer + 16] for layer in range(layers)]
    refs = refs[16 * layers :]
    (small_in, acc, rows_low, rows_in, local_sem, send_sem, recv_sem, kv_send, kv_recv, misc_send, misc_recv) = refs
    links = Links()
    core = links.core
    sems = (send_sem, recv_sem)
    units = ws_own.shape[2]
    width = wo_own.shape[2]
    rows = tokens.shape[0]
    weights = []
    for layer in range(layers):
        buffers = states[layer][:4]
        owns = [
            lambda part, rows, layer=layer: wi_own.at[layer, part, rows],
            lambda part, rows, layer=layer: wo_own.at[layer, part, rows],
            lambda part, rows, layer=layer: we_own.at[layer, rows, pl.ds(pl.multiple_of(part * units, 128), units)],
            lambda part, rows, layer=layer: ws_own.at[layer, part, rows],
        ]
        weights.append([Weight(links, 4 * layer + number, owns[number], buffers[number], local_sem, sems) for number in range(4)])
    every = [weight for group in weights for weight in group]
    for weight in every[:4]:
        weight.start_local()
    links.greet([links.across, links.along, links.beside, links.opposite])
    misc = (misc_send, misc_recv)
    swap_tokens = remote(tokens, tokens_in, misc, 0, links.opposite)
    swap_flag = remote(flag, flag_in, misc, 1, links.opposite)
    copy_small = remote(small, small_in, misc, 2, links.across)
    swap_cotangent = remote(cotangent, cotangent_in, misc, 3, links.opposite)
    swap_rows = remote(rows_low, rows_in, misc, 4, links.opposite)
    copy_small.start()

    @pl.when(links.moved)
    def _():
        swap_tokens.start()
        swap_flag.start()

    @pl.when(jnp.logical_not(links.moved))
    def _():
        tokens_in[...] = tokens[...]
        cotangent_in[...] = cotangent[...]
        flag_in[...] = flag[...]

    for weight in every[:4]:
        weight.start()

    @pl.when(links.moved)
    def _():
        swap_cotangent.start()

    for weight in every[4:]:
        weight.start()
        weight.start_local()

    def bias(layer, at, size, index):
        part = core + (index // 2) * (1 - 2 * core)
        place = pl.ds(pl.multiple_of(at + part * size, 128), size)
        return jnp.where(lax.rem(index, 2) == 0, small[layer : layer + 1, place], small_in[layer : layer + 1, place])

    @pl.when(links.moved)
    def _():
        swap_tokens.wait_recv()
        swap_flag.wait_recv()

    copy_small.wait_recv()
    shift = jnp.where(flag_in[0:1, 0:1] < 0.5, 0.0, MASKED)
    acc[...] = tokens_in[...].astype(F32)
    halves = lane_halves((rows, width))
    for layer in range(layers):
        (wi, wo, we, ws, query_ref, pair_ref, remote_ref, mixed_ref, total_ref, normed_ref, first_ref, first_scale, active_ref, slope_ref, second_ref, second_scale) = states[layer]
        vector = lambda at: vectors[layer, at : at + 1]
        wi_go, wo_go, we_go, ws_go = weights[layer]
        later = weights[layer + 1] if layer + 1 < layers else None
        low = acc[...].astype(BF16)

        def exchange(index):
            return remote(pair_ref.at[index], remote_ref.at[index], (kv_send, kv_recv), (layer, index), links.beside)

        def project(step, carry):
            index = ordered(step)
            triple = dot(low, wi[index])
            query = (triple[:, :width] + bias(layer, 0, width, index)).astype(BF16)
            query_ref[index] = query * BF16(DH ** (-0.5))
            pair_ref[index, :, :width] = triple[:, width : 2 * width].astype(BF16)
            pair_ref[index, :, width:] = (triple[:, 2 * width :] + bias(layer, 2 * width, width, index)).astype(BF16)
            exchange(index).start()
            return carry

        if layer == 0:
            before_pair = [
                [wi_go.relay],
                [wo_go.relay, wi_go.relay_again],
                [we_go.relay, wo_go.relay_again, wi_go.wait_fetched, lambda: lax.fori_loop(2, 4, project, 0)],
                [ws_go.relay, we_go.relay_again],
            ]
            before_quarter = [[later[0].relay, ws_go.relay_again], [later[1].relay, later[0].relay_again], [we_go.wait_fetched, ws_go.wait_fetched, later[1].relay_again], [later[2].relay]] if later else [[ws_go.relay_again], [], [we_go.wait_fetched, ws_go.wait_fetched], []]
            wi_go.wait_own()
            lax.fori_loop(0, 2, project, 0)
        else:
            before_pair = [[ws_go.relay, we_go.relay_again], [], [ws_go.relay_again], []]
            before_quarter = [[], [], [we_go.wait_fetched, ws_go.wait_fetched], []]
            wi_go.wait_own()
            wi_go.wait_fetched()
            lax.fori_loop(0, 4, project, 0)
        acc[...] += vector(0)
        wo_go.wait_own()
        before_pair[2].append(wo_go.wait_fetched)

        def one_pair(step, carry):
            at_step(step, before_pair)
            index = ordered(step)
            there = lax.rem(index + 2, 4)
            exchange(there).wait_recv()
            queries = query_ref[index]
            key_here, value_here = pair_ref[index, :, :width], pair_ref[index, :, width:]
            key_there, value_there = remote_ref[there, :, :width], remote_ref[there, :, width:]
            mixed, total = [], []
            for part in range(2):
                mask = halves if part == 0 else jnp.logical_not(halves)
                masked = jnp.where(mask, queries, BF16(0))
                here = dot_rt(masked, key_here)
                away = dot_rt(masked, key_there)
                peak = jnp.maximum(jnp.max(here, -1, keepdims=True), jnp.max(away, -1, keepdims=True) + shift)
                here = jnp.exp(here - peak)
                away = jnp.exp(away - (peak - shift))
                weight = jnp.sum(here, -1, keepdims=True) + jnp.sum(away, -1, keepdims=True)
                both = dot(here.astype(BF16), value_here) + dot(away.astype(BF16), value_there)
                mixed.append(both * (1.0 / weight))
                total.append(jnp.broadcast_to(peak + jnp.log(weight), (rows, width)))
            mixed_low = jnp.where(halves, mixed[0], mixed[1]).astype(BF16)
            mixed_ref[index] = mixed_low
            totals = jnp.where(halves, total[0], total[1]).T
            total_ref[index] = jnp.concatenate([totals[0:8], totals[DH : DH + 8]], 0)
            acc[...] += dot(mixed_low, wo[index])
            return carry

        lax.fori_loop(0, 4, one_pair, 0)
        first, scale = normalise(acc[...])
        first_ref[...] = first
        first_scale[...] = scale
        normed = first * vector(1) + vector(2)
        normed_ref[...] = normed.astype(BF16)
        acc[...] = normed + vector(3)
        we_go.wait_own()
        ws_go.wait_own()

        def one_quarter(step, carry):
            at_step(step, before_quarter)
            index = ordered(step)
            active, slope = gelu_parts(dot(normed_ref[...], we[index]) + bias(layer, 4 * width, units, index))
            active_low = active.astype(BF16)
            active_ref[index] = active_low
            slope_ref[index] = slope.astype(BF16)
            acc[...] += dot(active_low, ws[index])
            return carry

        lax.fori_loop(0, 4, one_quarter, 0)
        second, scale = normalise(acc[...])
        second_ref[...] = second
        second_scale[...] = scale
        acc[...] = second * vector(4) + vector(5)

    rows_low[...] = acc[...].astype(BF16)

    @pl.when(links.moved)
    def _():
        swap_rows.start()
        swap_rows.wait_recv()
        rows_ref[...] = rows_in[...].astype(F32)

    @pl.when(jnp.logical_not(links.moved))
    def _():
        rows_ref[...] = acc[...]

    @pl.when(links.moved)
    def _():
        swap_cotangent.wait_recv()
        for copy in (swap_tokens, swap_flag, swap_cotangent, swap_rows):
            copy.wait_send()

    copy_small.wait_send()
    for weight in every:
        weight.wait_sent()
    for layer in range(layers):
        pair_ref, remote_ref = states[layer][5:7]
        for index in range(4):
            remote(pair_ref.at[index], remote_ref.at[index], (kv_send, kv_recv), (layer, index), links.beside).wait_send()


def place_quarter(mine_ref, theirs_ref, index, at, size, value):
    @pl.when(index < 2)
    def _():
        mine_ref[index, at : at + size] = value

    @pl.when(index >= 2)
    def _():
        theirs_ref[index - 2, at : at + size] = value


def column_sum(x):
    return jnp.sum(x, 0, keepdims=True)


def norm_backward(grad, normed, scale, gain):
    scaled = grad * gain
    return (
        scaled - jnp.mean(scaled, -1, keepdims=True) - normed * jnp.mean(scaled * normed, -1, keepdims=True)
    ) * scale


def block_kernel(layer, *refs):
    (grad, second, second_scale, active, slope, normed, first, first_scale, mixed, vectors, wo, we, ws), refs = refs[:13], refs[13:]
    (mine_ref, theirs_ref, summed_ref, mixed_grad_ref, inner_ref, vector_ref, expand_bias_ref), refs = refs[:7], refs[7:]
    acc, turned = refs
    units = we.shape[2]
    rows, width = mixed.shape[1], mixed.shape[2]

    def put(index, at, size, value):
        place_quarter(mine_ref, theirs_ref, index, at, size, value)

    incoming = grad[...].astype(F32)
    widened = norm_backward(incoming, second[...], second_scale[...], vectors[4:5])
    vector_ref[0:1] = column_sum(incoming)
    vector_ref[1:2] = column_sum(incoming * second[...])
    vector_ref[2:3] = column_sum(widened)
    acc[...] = widened
    branch = widened.astype(BF16)
    turned[...] = normed[...].T

    def one_quarter(index, carry):
        active_grad = dot_rt(branch, ws[index])
        inner = (active_grad * slope[index].astype(F32)).astype(BF16)
        put(index, 0, units, dot_lt(active[index], branch).astype(BF16))
        put(index, units, turned.shape[0], dot(turned[...], inner).astype(BF16))
        expand_bias_ref[index] = jnp.broadcast_to(column_sum(inner.astype(F32)), expand_bias_ref.shape[1:])
        acc[...] += dot_rt(inner, we[index])
        return carry

    lax.fori_loop(0, 4, one_quarter, 0)
    outgoing = acc[...]
    summed = norm_backward(outgoing, first[...], first_scale[...], vectors[1:2])
    vector_ref[3:4] = column_sum(outgoing)
    vector_ref[4:5] = column_sum(outgoing * first[...])
    vector_ref[5:6] = column_sum(summed)
    vector_ref[6:8] = jnp.zeros((2, summed.shape[1]), F32)
    summed_ref[...] = summed
    low = summed.astype(BF16)
    half = lax.broadcasted_iota(jnp.int32, (16, width), 1) // DH
    which = lax.broadcasted_iota(jnp.int32, (16, width), 0) // 8
    selector = (half == which).astype(F32)

    def one_pair(index, carry):
        mixed_grad = dot_rt(low, wo[index]).astype(BF16)
        mixed_grad_ref[index] = mixed_grad
        put(index, units + turned.shape[0], width, dot_lt(mixed[index], low).astype(BF16))
        product = mixed_grad.astype(F32) * mixed[index].astype(F32)
        inner_ref[index] = lax.dot_general(
            selector, product, (((1,), (1,)), ((), ())), precision=lax.Precision.HIGHEST, preferred_element_type=F32
        )
        return carry

    lax.fori_loop(0, 4, one_pair, 0)


def attention_kernel(bias, query, pair, remote, mixed_grad, total, inner, query_grad_ref, here_ref, away_ref):
    rows, width = query.shape[1], query.shape[2]
    halves = lane_halves((rows, width))
    shift = bias[0]

    def one_pair(index, carry):
        there = lax.rem(index + 2, 4)
        queries, grads = query[index], mixed_grad[index]
        turned = None
        for side in range(2):
            source, place = (pair, index) if side == 0 else (remote, there)
            keys, values = source[place, :, :width], source[place, :, width:]
            key_grad = value_grad = None
            for part in range(2):
                mask = halves if part == 0 else jnp.logical_not(halves)
                masked_query = jnp.where(mask, queries, BF16(0))
                masked_grad = jnp.where(mask, grads, BF16(0))
                masked_key = jnp.where(mask, keys, BF16(0))
                level = total[index, 8 * part : 8 * part + 1]
                if side == 1:
                    level = level - shift
                weights = jnp.exp(dot_rt(keys, masked_query) - level)
                update = dot(weights.astype(BF16), masked_grad)
                value_grad = update if value_grad is None else value_grad + update
                slopes = dot_rt(values, masked_grad) - inner[index, 8 * part : 8 * part + 1]
                slopes = (weights * slopes).astype(BF16)
                update = dot(slopes, masked_query)
                key_grad = update if key_grad is None else key_grad + update
                update = dot_lt(masked_key, slopes)
                turned = update if turned is None else turned + update
            if side == 0:
                here_ref[index, :, :width] = key_grad
                here_ref[index, :, width:] = value_grad
            else:
                away_ref[there, :, :width] = key_grad.astype(BF16)
                away_ref[there, :, width:] = value_grad.astype(BF16)
        query_grad_ref[index] = (turned * DH ** (-0.5)).T.astype(BF16)
        return carry

    lax.fori_loop(0, 4, one_pair, 0)


def input_kernel(query_grad, here, away, hidden_low, summed, wi, mine_ref, theirs_ref, grad_ref, triple_ref, turned, acc):
    turned[...] = hidden_low[...].T
    acc[...] = summed[...]

    def one(index, carry):
        pair_grad = (here[index] + away[index].astype(F32)).astype(BF16)
        triple = jnp.concatenate([query_grad[index], pair_grad], 1)
        place_quarter(mine_ref, theirs_ref, index, 0, turned.shape[0], dot(turned[...], triple).astype(BF16))
        acc[...] += dot_rt(triple, wi[index])
        triple_ref[index] = jnp.broadcast_to(column_sum(triple.astype(F32)), triple_ref.shape[1:])
        return carry

    lax.fori_loop(0, 4, one, 0)
    grad_ref[...] = acc[...]


VM = pl.BlockSpec(memory_space=pltpu.VMEM)
AN = pl.BlockSpec(memory_space=pl.ANY)
SM = pl.BlockSpec(memory_space=pltpu.SMEM)


def shaped(dtype, *dims):
    return jax.ShapeDtypeStruct(dims, dtype)


def cost(flops, size):
    return pl.CostEstimate(flops=flops, bytes_accessed=size, transcendentals=0)


def call(body, name, ins, outs, scratch, args, flops=10**9):
    return pl.pallas_call(
        body,
        out_shape=outs,
        in_specs=ins,
        out_specs=[VM] * len(outs),
        scratch_shapes=scratch,
        compiler_params=pltpu.CompilerParams(vmem_limit_bytes=60 * 2**20),
        cost_estimate=cost(flops, 10**7),
        name=name,
    )(*args)


def permutations(mesh_shape):
    wide, narrow = mesh_shape
    line = lambda w, y: w * narrow + y
    every = [(w, y) for w in range(wide) for y in range(narrow)]
    swap = [(line(w, y), line((w & ~1) | y, w & 1)) for w, y in every]
    across = [(line(w, y), line(w, 1 - y)) for w, y in every]
    partner = [(line(w, y), line(w ^ 1, y)) for w, y in every]
    return swap, across, partner


def local(
    tokens, input_weight, query_bias, value_bias, output_weight, output_bias, first_gain, first_shift,
    expand_weight, expand_bias, shrink_weight, shrink_bias, second_gain, second_shift, lengths, bucket, cotangent,
):
    wide, narrow = lax.axis_size("wide"), lax.axis_size("narrow")
    assert narrow == 2 and wide % 2 == 0
    swap, across, partner = permutations((wide, narrow))
    core = lax.axis_index("wide") % 2
    send = lambda x, pairs: lax.ppermute(x, AXES, pairs)
    layers, depth = input_weight.shape[0], input_weight.shape[1]
    rows = tokens.shape[0]
    width = input_weight.shape[3] // 2
    units = expand_weight.shape[2] // 2

    flag = jnp.broadcast_to(bucket, (8, 128)).astype(F32)
    input_own = (
        input_weight.reshape(layers, depth, 3, 2, width).transpose(0, 3, 1, 2, 4).reshape(layers, 2, depth, 3 * width)
    )
    output_own = output_weight.reshape(layers, 2, width, depth)
    shrink_own = shrink_weight.reshape(layers, 2, units, depth)
    small = jnp.concatenate([query_bias, value_bias, expand_bias], 1)
    vectors = jnp.stack(
        [output_bias, first_gain, first_shift, shrink_bias, second_gain, second_shift, output_bias, output_bias], 1
    )
    acc_scratch = pltpu.VMEM((rows, depth), F32)
    turn_scratch = pltpu.VMEM((depth, rows), BF16)
    query_shape = shaped(BF16, 4, rows, width)
    pair_shape = shaped(BF16, 4, rows, 2 * width)
    row_shape = shaped(F32, rows, depth)
    low_shape = shaped(BF16, rows, depth)
    scale_shape = shaped(F32, rows, 1)
    stat_shape = shaped(F32, 4, 16, rows)
    wide_shape = shaped(BF16, 4, rows, units)
    state_shapes = [
        shaped(BF16, 4, depth, 3 * width), shaped(BF16, 4, width, depth), shaped(BF16, 4, depth, units), shaped(BF16, 4, units, depth),
        query_shape, pair_shape, pair_shape, query_shape, stat_shape, low_shape, row_shape, scale_shape, wide_shape, wide_shape, row_shape, scale_shape,
    ]
    outs = [row_shape, low_shape, low_shape, shaped(F32, 8, 128)] + state_shapes * layers
    results = pl.pallas_call(
        functools.partial(all_forward, layers),
        out_shape=outs,
        in_specs=[VM] * 5 + [AN] * 4,
        out_specs=[VM] * len(outs),
        scratch_shapes=[
            pltpu.VMEM(small.shape, F32), acc_scratch, pltpu.VMEM((rows, depth), BF16), pltpu.VMEM((rows, depth), BF16),
            pltpu.SemaphoreType.DMA((8 * layers,)),
            pltpu.SemaphoreType.DMA((16 * layers,)), pltpu.SemaphoreType.DMA((16 * layers,)),
            pltpu.SemaphoreType.DMA((layers, 4)), pltpu.SemaphoreType.DMA((layers, 4)),
            pltpu.SemaphoreType.DMA((5,)), pltpu.SemaphoreType.DMA((5,)),
        ],
        compiler_params=pltpu.CompilerParams(collective_id=1, has_side_effects=True, vmem_limit_bytes=62 * 2**20),
        cost_estimate=cost(10**10, 10**8),
        name="forward",
    )(flag, tokens, cotangent, small, vectors, input_own, output_own, expand_weight, shrink_own)
    layer_output, low, cotangent, flag = results[:4]
    shift = jnp.where(flag[0, 0] < 0.5, 0.0, MASKED).astype(F32).reshape(1)
    saved = []
    for layer in range(layers):
        state = results[4 + 16 * layer : 20 + 16 * layer]
        vector = lambda at: vectors[layer, at : at + 1]
        saved.append((low,) + tuple(state))
        low = (state[14] * vector(4) + vector(5)).astype(BF16)

    grad = cotangent
    collected = [None] * layers
    for layer in reversed(range(layers)):
        low, wi, wo, we, ws, query, pair, remote_pair, mixed, total, normed, first, first_scale, active, slope, second, second_scale = saved[layer]
        mine, theirs, summed, mixed_grad, inner, vector_grad, expand_bias_grad = call(
            functools.partial(block_kernel, layer), f"block_{layer}",
            [VM] * 13,
            [shaped(BF16, 2, units + depth + width, depth)] * 2 + [row_shape, query_shape, stat_shape, shaped(F32, 8, depth), shaped(F32, 4, 8, units)],
            [acc_scratch, turn_scratch],
            (grad, second, second_scale, active, slope, normed, first, first_scale, mixed, vectors[layer], wo, we, ws),
            5 * 10**9,
        )
        blocks = reduce_quarters(mine, theirs, send, partner, across)
        query_grad, here, away = call(
            attention_kernel, f"attention_{layer}",
            [SM] + [VM] * 6, [query_shape, shaped(F32, 4, rows, 2 * width), pair_shape], [],
            (shift, query, pair, remote_pair, mixed_grad, total, inner), 5 * 10**9,
        )
        back = send(away, partner)
        mine, theirs, grad, triple_grad = call(
            input_kernel, f"input_{layer}",
            [VM] * 6,
            [shaped(BF16, 2, depth, 3 * width)] * 2 + [row_shape, shaped(F32, 4, 8, 3 * width)],
            [turn_scratch, acc_scratch],
            (query_grad, here, back, low, summed, wi), 2 * 10**9,
        )
        collected[layer] = (blocks, mine, theirs, vector_grad, expand_bias_grad, triple_grad)
    input_rows = send(grad.astype(BF16), swap).astype(F32)
    return finish_all(collected, layer_output, input_rows, send, core, across, partner, wide, layers, depth, width, units)


def reduce_quarters(mine, theirs, send, partner, across):
    mine = (mine.astype(F32) + send(theirs, partner).astype(F32)).astype(BF16)
    return (mine[0].astype(F32) + send(mine[1], across).astype(F32)).astype(BF16)


def finish_all(collected, layer_output, input_rows, send, core, across, partner, wide, layers, depth, width, units):
    same = [[w for w in range(wide) if w % 2 == c] for c in range(2)]
    smalls = []
    for blocks, mine, theirs, vector_grad, expand_bias_grad, triple_grad in collected:
        triple = jnp.pad(triple_grad[:, :1], ((0, 0), (0, 0), (0, depth - 3 * width)))
        expand = jnp.pad(expand_bias_grad[:, :1], ((0, 0), (0, 0), (0, depth - units)))
        smalls.append(jnp.concatenate([jnp.broadcast_to(vector_grad[:6], (4, 6, depth)), expand, triple], 1))
    small = jnp.concatenate(smalls, 1)
    done = []
    for layer in range(1, layers):
        blocks, mine, theirs = collected[layer][:3]
        inputs = reduce_quarters(mine, theirs, send, partner, across)
        blocks, inputs = lax.psum((blocks, inputs), "wide", axis_index_groups=same)
        pair = []
        for x in (blocks, inputs):
            there = send(x, partner)
            pair.append(jnp.where(core == 0, jnp.stack([x, there]), jnp.stack([there, x])))
        done.append(pair)
    blocks, mine, theirs = collected[0][:3]
    blocks, inputs, small = finish_call(blocks, mine, theirs, small, wide)
    done.insert(0, [blocks, inputs])
    shrink, expand, output, inputs = [], [], [], []
    for blocks, triple in done:
        blocks, triple = blocks.astype(F32), triple.astype(F32)
        shrink.append(blocks[:, :units].reshape(2 * units, depth))
        expand.append(blocks[:, units : units + depth].transpose(1, 0, 2).reshape(depth, 2 * units))
        output.append(blocks[:, units + depth : units + depth + width].reshape(2 * width, depth))
        inputs.append(triple[:, :depth].reshape(2, depth, 3, width).transpose(1, 2, 0, 3).reshape(depth, 3, 2 * width))
    small = small.reshape(2, layers, 8, depth)
    both = lambda at, a, b: small[:, :, at, a:b].transpose(1, 0, 2).reshape(layers, 2 * (b - a))
    vector = lambda at: small[0, :, at]
    return (
        layer_output,
        input_rows,
        jnp.stack(inputs),
        both(7, 0, width),
        both(7, 2 * width, 3 * width),
        jnp.stack(output),
        vector(5),
        vector(4),
        vector(3),
        jnp.stack(expand),
        both(6, 0, units),
        jnp.stack(shrink),
        vector(2),
        vector(1),
        vector(0),
    )


def finish_kernel(chips, *refs):
    (blocks, inputs_mine, inputs_theirs, small), refs = refs[:4], refs[4:]
    (blocks_out, inputs_out, small_out), refs = refs[:3], refs[3:]
    (held, held_inputs, *landed), refs = refs[:6], refs[6:]
    (core_inputs, mid_inputs, row_inputs, core_small, mid_small, row_small, sum_small, step_small), refs = refs[:8], refs[8:]
    ring_send, ring_recv, pair_send, pair_recv, step_send, step_recv = refs
    wide, narrow = lax.axis_index("wide"), lax.axis_index("narrow")
    core, chip = lax.rem(wide, 2), wide // 2
    odd = lax.rem(chip, 2)
    place = odd * (chips - 1 - chip // 2) + (1 - odd) * (chip // 2)

    def chip_at(position):
        position = lax.rem(position + chips, chips)
        late = position // (chips // 2)
        return late * (2 * (chips - 1 - position) + 1) + (1 - late) * (2 * position)

    def peer(index, other_core=0, other_narrow=0):
        side = core + other_core * (1 - 2 * core)
        return (index * 2 + side, narrow + other_narrow * (1 - 2 * narrow))

    right, left = peer(chip_at(place + 1)), peer(chip_at(place - 1))
    beside, across = peer(chip, 1, 0), peer(chip, 0, 1)
    steps = chips.bit_length() - 1
    bits = []
    for bit in range(steps):
        flag = lax.rem(chip // 2**bit, 2)
        bits.append(peer(chip + 2**bit * (1 - 2 * flag)))
    barrier = pltpu.get_barrier_semaphore()
    partners = [right, left, beside, across] + bits
    for device in partners:
        pl.semaphore_signal(barrier, inc=1, device_id=device, device_id_type=pl.DeviceIdType.MESH)
    pl.semaphore_wait(barrier, len(partners))

    sent = []

    def push(source, target, send_sem, recv_sem, device):
        copy = pltpu.make_async_remote_copy(source, target, send_sem, recv_sem, device_id=device, device_id_type=pl.DeviceIdType.MESH)
        copy.start()
        sent.append(copy)
        return copy

    class Ring:
        def __init__(self, which, data, out, columns, slots):
            self.which, self.data, self.out, self.columns, self.slots = which, data, out, columns, slots
            self.size = data.shape[0] // chips
            self.now = [None, None]

        def rows(self, index):
            index = lax.rem(index + 2 * chips, chips)
            return pl.ds(pl.multiple_of(index * self.size, 16), self.size)

        def span(self, side):
            at, count = self.columns[side]
            return pl.ds(at, count)

        def start(self):
            for side in range(2):
                self.pass_on(side, 0, self.data.at[self.rows(place), self.span(side)], self.slots[side].at[0])

        def pass_on(self, side, step, source, target):
            self.now[side] = push(source, target, ring_send.at[self.which, side, step], ring_recv.at[self.which, side, step], (right, left)[side])

        def tick(self, step):
            for side in range(2):
                way = 1 - 2 * side
                span = self.span(side)
                self.now[side].wait_recv()
                if step < chips - 1:
                    rows = self.rows(place - way * (step + 1))
                    total = self.data[rows, span].astype(F32) + self.slots[side][step].astype(F32)
                    total = total.astype(BF16)
                    self.data[rows, span] = total
                    if step < chips - 2:
                        self.pass_on(side, step + 1, self.data.at[rows, span], self.slots[side].at[step + 1])
                    else:
                        self.out[core, rows, span] = total
                        self.pass_on(side, step + 1, self.data.at[rows, span], self.out.at[core, rows, span])
                elif step < 2 * chips - 3:
                    rows = self.rows(place - way * (step - chips + 1))
                    where = self.out.at[core, rows, span]
                    self.pass_on(side, step + 1, where, where)

    def fill(target, value):
        target[0 : value.shape[0]] = value
        if value.shape[0] < target.shape[0]:
            target[value.shape[0] :] = jnp.zeros((target.shape[0] - value.shape[0], target.shape[1]), target.dtype)

    fill(held, blocks[...])
    half = held.shape[1] // 2
    first = Ring(0, held, blocks_out, ((0, half), (half, half)), landed[0:2])
    third = held_inputs.shape[1] // 3
    second = Ring(1, held_inputs, inputs_out, ((0, 2 * third), (2 * third, third)), landed[2:4])
    first.start()
    copy_inputs = push(inputs_theirs, core_inputs, pair_send.at[0], pair_recv.at[0], beside)
    copy_small = push(small.at[pl.ds(2, 2)], core_small, pair_send.at[1], pair_recv.at[1], beside)
    copy_small.wait_recv()
    mid_small[...] = small[1] + core_small[1]
    copy_small = push(mid_small, row_small, pair_send.at[2], pair_recv.at[2], across)
    copy_inputs.wait_recv()
    mid_inputs[...] = (inputs_mine[1].astype(F32) + core_inputs[1].astype(F32)).astype(BF16)
    copy_inputs = push(mid_inputs, row_inputs, pair_send.at[3], pair_recv.at[3], across)
    fill(held_inputs, (inputs_mine[0].astype(F32) + core_inputs[0].astype(F32)).astype(BF16))
    ticks = 2 * (chips - 1)
    delay = 3
    small_value = None
    for step in range(ticks + delay):
        if step < ticks:
            first.tick(step)
        if step == 0:
            copy_small.wait_recv()
            small_value = small[0] + core_small[0] + row_small[...]
        if 0 < step <= steps:
            copy_small.wait_recv()
            small_value = small_value + step_small[step - 1]
        if step < steps:
            sum_small[step] = small_value
            copy_small = push(sum_small.at[step], step_small.at[step], step_send.at[step], step_recv.at[step], bits[step])
        if step == steps:
            small_out[core] = small_value
        if step == delay - 1:
            copy_inputs.wait_recv()
            total = held_inputs[0 : row_inputs.shape[0]].astype(F32) + row_inputs[...].astype(F32)
            held_inputs[0 : row_inputs.shape[0]] = total.astype(BF16)
            second.start()
        if step >= delay:
            second.tick(step - delay)
        if step == ticks:
            last = [
                push(blocks_out.at[core], blocks_out.at[core], pair_send.at[4], pair_recv.at[4], beside),
                push(small_out.at[core], small_out.at[core], pair_send.at[5], pair_recv.at[5], beside),
            ]
    last.append(push(inputs_out.at[core], inputs_out.at[core], pair_send.at[6], pair_recv.at[6], beside))
    for copy in last:
        copy.wait_recv()
    for copy in sent:
        copy.wait_send()


def finish_call(blocks, inputs_mine, inputs_theirs, small, wide):
    chips = wide // 2
    size = lambda rows: -(-rows // (16 * chips)) * 16 * chips
    rows, depth = blocks.shape
    input_rows, columns = inputs_mine.shape[1:]
    tall, input_tall = size(rows), size(input_rows)
    steps = chips.bit_length() - 1
    slot = lambda tall, count: pltpu.VMEM((chips - 1, tall // chips, count), BF16)
    small_rows = small.shape[1]
    return pl.pallas_call(
        functools.partial(finish_kernel, chips),
        out_shape=[shaped(BF16, 2, tall, depth), shaped(BF16, 2, input_tall, columns), shaped(F32, 2, small_rows, depth)],
        in_specs=[VM] * 4,
        out_specs=[VM] * 3,
        scratch_shapes=[
            pltpu.VMEM((tall, depth), BF16),
            pltpu.VMEM((input_tall, columns), BF16),
            slot(tall, depth // 2),
            slot(tall, depth // 2),
            slot(input_tall, 2 * columns // 3),
            slot(input_tall, columns // 3),
            pltpu.VMEM((2, input_rows, columns), BF16),
            pltpu.VMEM((input_rows, columns), BF16),
            pltpu.VMEM((input_rows, columns), BF16),
            pltpu.VMEM((2, small_rows, depth), F32),
            pltpu.VMEM((small_rows, depth), F32),
            pltpu.VMEM((small_rows, depth), F32),
            pltpu.VMEM((steps, small_rows, depth), F32),
            pltpu.VMEM((steps, small_rows, depth), F32),
            pltpu.SemaphoreType.DMA((2, 2, 2 * (chips - 1))),
            pltpu.SemaphoreType.DMA((2, 2, 2 * (chips - 1))),
            pltpu.SemaphoreType.DMA((7,)),
            pltpu.SemaphoreType.DMA((7,)),
            pltpu.SemaphoreType.DMA((steps,)),
            pltpu.SemaphoreType.DMA((steps,)),
        ],
        compiler_params=pltpu.CompilerParams(collective_id=0, has_side_effects=True, vmem_limit_bytes=48 * 2**20),
        cost_estimate=cost(10**9, 10**7),
        name="finish",
    )(blocks, inputs_mine, inputs_theirs, small)


def solution(mesh):
    split = P(AXES, None)
    in_specs = (
        split, P(None, None, None, "narrow"), P(None, "narrow"), P(None, "narrow"), P(None, "narrow", None), P(), P(), P(),
        P(None, None, "narrow"), P(None, "narrow"), P(None, "narrow", None), P(), P(), P(), P("wide"), P("wide"), split,
    )
    out_specs = (
        split, split, P(None, None, None, "narrow"), P(None, "narrow"), P(None, "narrow"), P(None, "narrow", None), P(), P(), P(),
        P(None, None, "narrow"), P(None, "narrow"), P(None, "narrow", None), P(), P(), P(),
    )
    return jax.shard_map(local, mesh=mesh, in_specs=in_specs, out_specs=out_specs, check_vma=False)
```

```python
import functools

import jax
import jax.numpy as jnp
from jax import lax
from jax.experimental import pallas as pl
from jax.experimental.pallas import tpu as pltpu
from jax.sharding import PartitionSpec as P

DH = 64
EPSILON = 1e-12
MASKED = -1e9
AXES = ("wide", "narrow")
F32 = jnp.float32
BF16 = jnp.bfloat16
STATES = 17


def dot(a, b):
    return lax.dot_general(a, b, (((1,), (0,)), ((), ())), preferred_element_type=F32)


def dot_rt(a, b):
    return lax.dot_general(a, b, (((1,), (1,)), ((), ())), preferred_element_type=F32)


def dot_lt(a, b):
    return lax.dot_general(a, b, (((0,), (0,)), ((), ())), preferred_element_type=F32)


def lane_halves(shape):
    lane = lax.broadcasted_iota(jnp.int32, shape, len(shape) - 1)
    return lane < DH


def normalise(x):
    centre = x - jnp.mean(x, -1, keepdims=True)
    scale = lax.rsqrt(jnp.mean(centre * centre, -1, keepdims=True) + EPSILON)
    return centre * scale, scale


def gelu_parts(a):
    square = jnp.exp(-0.5 * a * a)
    size = jnp.abs(a)
    t = 1.0 / (1.0 + (0.3275911 * 0.7071067811865476) * size)
    poly = t * (
        0.127414796
        + t * (-0.142248368 + t * (0.7107068705 + t * (-0.7265760135 + t * 0.5307027145)))
    )
    tail = poly * square
    phi = jnp.where(a >= 0, 1.0 - tail, tail)
    return a * phi, phi + a * square * 0.3989422804014327


def ring_size(chips):
    return min(chips, 8)


class Links:
    def __init__(self):
        self.wide, self.narrow = lax.axis_index("wide"), lax.axis_index("narrow")
        self.core = lax.rem(self.wide, 2)
        self.chip = self.wide // 2
        self.bit = lax.rem(self.chip, 2)
        other_core, other_narrow = self.wide + 1 - 2 * self.core, 1 - self.narrow
        self.beside = (other_core, self.narrow)
        self.across = (self.wide, other_narrow)
        self.along = (self.wide + 2 * (1 - 2 * self.bit), self.narrow)
        self.opposite = (other_core, other_narrow)
        self.moved = self.core + self.narrow == 1

    def ring(self, chips):
        self.chips = ring_size(chips)
        self.group = self.chip // self.chips
        at = lax.rem(self.chip, self.chips)
        odd = lax.rem(at, 2)
        self.place = odd * (self.chips - 1 - at // 2) + (1 - odd) * (at // 2)
        self.right, self.left = self.ring_device(1), self.ring_device(-1)
        self.bits = []
        for bit in range(chips.bit_length() - 1):
            side = lax.rem(self.chip // 2**bit, 2)
            self.bits.append((self.wide + 2 ** (bit + 1) * (1 - 2 * side), self.narrow))
        self.further = self.bits[self.chips.bit_length() - 1 :]

    def ring_device(self, offset):
        place = lax.rem(self.place + offset + self.chips, self.chips)
        late = place // (self.chips // 2)
        chip = late * (2 * (self.chips - 1 - place) + 1) + (1 - late) * (2 * place)
        return (2 * (self.group * self.chips + chip) + self.core, self.narrow)

    def greet(self, devices):
        barrier = pltpu.get_barrier_semaphore()
        for device in devices:
            pl.semaphore_signal(barrier, inc=1, device_id=device, device_id_type=pl.DeviceIdType.MESH)
        pl.semaphore_wait(barrier, len(devices))


def remote(source, target, sems, at, device):
    return pltpu.make_async_remote_copy(
        source, target, sems[0].at[at], sems[1].at[at], device_id=device, device_id_type=pl.DeviceIdType.MESH
    )


class Weight:
    def __init__(self, links, number, own, buffer, local_sem, sems):
        self.links, self.number, self.own, self.buffer, self.local_sem, self.sems = links, number, own, buffer, local_sem, sems
        self.half = buffer.shape[1] // 2

    def rows(self, bit):
        return pl.ds(pl.multiple_of(bit * self.half, 16), self.half)

    def local_copies(self):
        core = self.links.core
        return [
            pltpu.make_async_copy(self.own(core, slice(None)), self.buffer.at[0], self.local_sem.at[2 * self.number]),
            pltpu.make_async_copy(self.own(1 - core, slice(None)), self.buffer.at[2], self.local_sem.at[2 * self.number + 1]),
        ]

    def hop(self, kind):
        links, rows = self.links, self.rows(self.links.bit)
        at = 4 * self.number + kind
        if kind == 0:
            return remote(self.own(links.core, rows), self.buffer.at[1, rows], self.sems, at, links.across)
        if kind == 1:
            return remote(self.buffer.at[1, rows], self.buffer.at[1, rows], self.sems, at, links.along)
        if kind == 3:
            rows = self.rows(1 - links.bit)
        return remote(self.buffer.at[1, rows], self.buffer.at[3, rows], self.sems, at, links.beside)

    def start(self):
        self.hop(0).start()

    def start_local(self):
        for copy in self.local_copies():
            copy.start()

    def relay(self):
        self.hop(0).wait_recv()
        self.hop(1).start()
        self.hop(2).start()

    def relay_again(self):
        self.hop(1).wait_recv()
        self.hop(3).start()

    def wait_own(self):
        for copy in self.local_copies():
            copy.wait()

    def wait_fetched(self):
        self.hop(2).wait_recv()
        self.hop(3).wait_recv()

    def wait_sent(self):
        for kind in range(4):
            self.hop(kind).wait_send()


def ordered(step):
    return lax.rem(2 * step, 4) + step // 2


def at_step(step, hooks):
    for number, hook in enumerate(hooks):
        if hook:

            @pl.when(step == number)
            def _(hook=hook):
                for action in hook:
                    action()


def all_forward(layers, *refs):
    (flag, tokens, cotangent, small, vectors, wi_own, wo_own, we_own, ws_own), refs = refs[:9], refs[9:]
    (rows_ref, cotangent_in, flag_in), refs = refs[:3], refs[3:]
    kept = [refs[STATES * layer : STATES * (layer + 1)] for layer in range(layers)]
    refs = refs[STATES * layers :]
    states = [refs[STATES * layer : STATES * (layer + 1)] for layer in range(layers)]
    refs = refs[STATES * layers :]
    tokens_in = states[0][16]
    (save_sem, small_in, acc, rows_low, rows_in, local_sem, send_sem, recv_sem, kv_send, kv_recv, misc_send, misc_recv) = refs
    links = Links()
    core = links.core
    sems = (send_sem, recv_sem)
    units = ws_own.shape[2]
    width = wo_own.shape[2]
    rows = tokens.shape[0]
    weights = []
    for layer in range(layers):
        buffers = states[layer][:4]
        owns = [
            lambda part, rows, layer=layer: wi_own.at[layer, part, rows],
            lambda part, rows, layer=layer: wo_own.at[layer, part, rows],
            lambda part, rows, layer=layer: we_own.at[layer, rows, pl.ds(pl.multiple_of(part * units, 128), units)],
            lambda part, rows, layer=layer: ws_own.at[layer, part, rows],
        ]
        weights.append([Weight(links, 4 * layer + number, owns[number], buffers[number], local_sem, sems) for number in range(4)])
    every = [weight for group in weights for weight in group]
    for weight in every[:4]:
        weight.start_local()
    links.greet([links.across, links.along, links.beside, links.opposite])
    misc = (misc_send, misc_recv)
    swap_tokens = remote(tokens, tokens_in, misc, 0, links.opposite)
    swap_flag = remote(flag, flag_in, misc, 1, links.opposite)
    copy_small = remote(small, small_in, misc, 2, links.across)
    swap_cotangent = remote(cotangent, cotangent_in, misc, 3, links.opposite)
    swap_rows = remote(rows_low, rows_in, misc, 4, links.opposite)
    copy_small.start()

    @pl.when(links.moved)
    def _():
        swap_tokens.start()
        swap_flag.start()

    @pl.when(jnp.logical_not(links.moved))
    def _():
        tokens_in[...] = tokens[...]
        cotangent_in[...] = cotangent[...]
        flag_in[...] = flag[...]

    for weight in every[:4]:
        weight.start()

    @pl.when(links.moved)
    def _():
        swap_cotangent.start()

    for weight in every[4:]:
        weight.start()
        weight.start_local()

    def bias(layer, at, size, index):
        part = core + (index // 2) * (1 - 2 * core)
        place = pl.ds(pl.multiple_of(at + part * size, 128), size)
        return jnp.where(lax.rem(index, 2) == 0, small[layer : layer + 1, place], small_in[layer : layer + 1, place])

    @pl.when(links.moved)
    def _():
        swap_tokens.wait_recv()
        swap_flag.wait_recv()

    copy_small.wait_recv()
    shift = jnp.where(flag_in[0:1, 0:1] < 0.5, 0.0, MASKED)
    acc[...] = tokens_in[...].astype(F32)
    halves = lane_halves((rows, width))

    def save_copy(layer, number):
        return pltpu.make_async_copy(states[layer][number], kept[layer][number], save_sem.at[layer, number])

    def save(layer, *numbers):
        for number in numbers:
            save_copy(layer, number).start()

    for layer in range(layers):
        (wi, wo, we, ws, query_ref, pair_ref, remote_ref, mixed_ref, total_ref, normed_ref, first_ref, first_scale, active_ref, slope_ref, second_ref, second_scale, low_ref) = states[layer]
        vector = lambda at: vectors[layer, at : at + 1]
        wi_go, wo_go, we_go, ws_go = weights[layer]
        later = weights[layer + 1] if layer + 1 < layers else None
        if layer > 0:
            low_ref[...] = acc[...].astype(BF16)

        def exchange(index):
            return remote(pair_ref.at[index], remote_ref.at[index], (kv_send, kv_recv), (layer, index), links.beside)

        def project(step, carry):
            index = ordered(step)
            triple = dot(low_ref[...], wi[index])
            query = (triple[:, :width] + bias(layer, 0, width, index)).astype(BF16)
            query_ref[index] = query * BF16(DH ** (-0.5))
            pair_ref[index, :, :width] = triple[:, width : 2 * width].astype(BF16)
            pair_ref[index, :, width:] = (triple[:, 2 * width :] + bias(layer, 2 * width, width, index)).astype(BF16)
            exchange(index).start()
            return carry

        if layer == 0:
            before_pair = [
                [wi_go.relay],
                [wo_go.relay, wi_go.relay_again],
                [we_go.relay, wo_go.relay_again, wi_go.wait_fetched, lambda: lax.fori_loop(2, 4, project, 0)],
                [ws_go.relay, we_go.relay_again],
            ]
            before_quarter = [[later[0].relay, ws_go.relay_again], [later[1].relay, later[0].relay_again], [we_go.wait_fetched, ws_go.wait_fetched, later[1].relay_again], [later[2].relay]] if later else [[ws_go.relay_again], [], [we_go.wait_fetched, ws_go.wait_fetched], []]
            wi_go.wait_own()
            lax.fori_loop(0, 2, project, 0)
        else:
            before_pair = [[ws_go.relay, we_go.relay_again], [], [ws_go.relay_again], []]
            before_quarter = [[], [], [we_go.wait_fetched, ws_go.wait_fetched], []]
            wi_go.wait_own()
            wi_go.wait_fetched()
            lax.fori_loop(0, 4, project, 0)
        acc[...] += vector(0)
        wo_go.wait_own()
        before_pair[2].append(wo_go.wait_fetched)

        def one_pair(step, carry):
            at_step(step, before_pair)
            index = ordered(step)
            there = lax.rem(index + 2, 4)
            exchange(there).wait_recv()
            queries = query_ref[index]
            key_here, value_here = pair_ref[index, :, :width], pair_ref[index, :, width:]
            key_there, value_there = remote_ref[there, :, :width], remote_ref[there, :, width:]
            mixed, total = [], []
            for part in range(2):
                mask = halves if part == 0 else jnp.logical_not(halves)
                masked = jnp.where(mask, queries, BF16(0))
                here = dot_rt(masked, key_here)
                away = dot_rt(masked, key_there)
                peak = jnp.maximum(jnp.max(here, -1, keepdims=True), jnp.max(away, -1, keepdims=True) + shift)
                here = jnp.exp(here - peak)
                away = jnp.exp(away - (peak - shift))
                weight = jnp.sum(here, -1, keepdims=True) + jnp.sum(away, -1, keepdims=True)
                both = dot(here.astype(BF16), value_here) + dot(away.astype(BF16), value_there)
                mixed.append(both * (1.0 / weight))
                total.append(jnp.broadcast_to(peak + jnp.log(weight), (rows, width)))
            mixed_low = jnp.where(halves, mixed[0], mixed[1]).astype(BF16)
            mixed_ref[index] = mixed_low
            totals = jnp.where(halves, total[0], total[1]).T
            total_ref[index] = jnp.concatenate([totals[0:8], totals[DH : DH + 8]], 0)
            acc[...] += dot(mixed_low, wo[index])
            return carry

        lax.fori_loop(0, 4, one_pair, 0)
        save(layer, 16, 0, 4, 5, 6, 1, 7, 8)
        first, scale = normalise(acc[...])
        first_ref[...] = first
        first_scale[...] = scale
        normed = first * vector(1) + vector(2)
        normed_ref[...] = normed.astype(BF16)
        acc[...] = normed + vector(3)
        save(layer, 9, 10, 11)
        we_go.wait_own()
        ws_go.wait_own()

        def one_quarter(step, carry):
            at_step(step, before_quarter)
            index = ordered(step)
            active, slope = gelu_parts(dot(normed_ref[...], we[index]) + bias(layer, 4 * width, units, index))
            active_low = active.astype(BF16)
            active_ref[index] = active_low
            slope_ref[index] = slope.astype(BF16)
            acc[...] += dot(active_low, ws[index])
            return carry

        lax.fori_loop(0, 4, one_quarter, 0)
        save(layer, 2, 3, 12, 13)
        second, scale = normalise(acc[...])
        second_ref[...] = second
        second_scale[...] = scale
        save(layer, 14, 15)
        acc[...] = second * vector(4) + vector(5)

    rows_low[...] = acc[...].astype(BF16)

    @pl.when(links.moved)
    def _():
        swap_rows.start()
        swap_rows.wait_recv()
        rows_ref[...] = rows_in[...].astype(F32)

    @pl.when(jnp.logical_not(links.moved))
    def _():
        rows_ref[...] = acc[...]

    @pl.when(links.moved)
    def _():
        swap_cotangent.wait_recv()
        for copy in (swap_tokens, swap_flag, swap_cotangent, swap_rows):
            copy.wait_send()

    copy_small.wait_send()
    for weight in every:
        weight.wait_sent()
    for layer in range(layers):
        for number in range(STATES):
            save_copy(layer, number).wait()
    for layer in range(layers):
        pair_ref, remote_ref = states[layer][5:7]
        for index in range(4):
            remote(pair_ref.at[index], remote_ref.at[index], (kv_send, kv_recv), (layer, index), links.beside).wait_send()


def column_sum(x):
    return jnp.sum(x, 0, keepdims=True)


def norm_backward(grad, normed, scale, gain):
    scaled = grad * gain
    return (
        scaled - jnp.mean(scaled, -1, keepdims=True) - normed * jnp.mean(scaled * normed, -1, keepdims=True)
    ) * scale


def backwards(step):
    return 3 - ordered(step)


class Gradient:
    def __init__(self, links, number, mine, theirs, core_in, narrow_in, slots, further_in, out, columns, sems):
        self.links, self.number, self.mine, self.theirs, self.core_in = links, number, mine, theirs, core_in
        self.narrow_in, self.slots, self.further_in, self.out, self.columns, self.sems = narrow_in, slots, further_in, out, columns, sems
        self.size = core_in.shape[1]
        self.piece = mine.shape[1] // links.chips

    def part_copy(self, part):
        return remote(self.theirs.at[part], self.core_in.at[part], self.sems[0], (self.number, part), self.links.beside)

    def narrow_copy(self):
        return remote(self.mine.at[1, pl.ds(0, self.size)], self.narrow_in, self.sems[0], (self.number, 2), self.links.across)

    def share_copy(self):
        place = self.out.at[self.links.core]
        return remote(place, place, self.sems[0], (self.number, 3), self.links.beside)

    def ring_copy(self, side, step):
        links, way = self.links, 1 - 2 * side
        at, count = self.columns[side]
        device = links.right if side == 0 else links.left
        where = (self.number, side, step)
        if step < links.chips - 1:
            source = self.mine.at[0, self.rows(-way * step), pl.ds(at, count)]
            return remote(source, self.slots[side].at[step], self.sems[1], where, device)
        rows = self.rows(-way * (step - links.chips))
        target = self.out.at[links.core, rows, pl.ds(at, count)]
        source = self.mine.at[0, rows, pl.ds(at, count)] if step == links.chips - 1 else target
        return remote(source, target, self.sems[1], where, device)

    def further_copy(self, side, number):
        at, count = self.columns[side]
        source = self.mine.at[0, self.rows(1 - 2 * side), pl.ds(at, count)]
        return remote(source, self.further_in[side].at[number], self.sems[2], (self.number, side, number), self.links.further[number])

    def rows(self, offset):
        index = lax.rem(self.links.place + offset + 2 * self.links.chips, self.links.chips)
        return pl.ds(pl.multiple_of(index * self.piece, 16), self.piece)

    def send(self, part):
        self.part_copy(part).start()

    def middle(self):
        self.part_copy(1).wait_recv()
        total = self.mine[1, 0 : self.size].astype(F32) + self.core_in[1].astype(F32)
        self.mine[1, 0 : self.size] = total.astype(BF16)
        self.narrow_copy().start()

    def settle(self):
        self.part_copy(0).wait_recv()
        self.narrow_copy().wait_recv()
        total = self.mine[0, 0 : self.size].astype(F32) + self.core_in[0].astype(F32) + self.narrow_in[...].astype(F32)
        self.mine[0, 0 : self.size] = total.astype(BF16)
        for side in range(2):
            self.ring_copy(side, 0).start()

    def tick(self, step):
        chips = self.links.chips
        for side in range(2):
            way = 1 - 2 * side
            at, count = self.columns[side]
            self.ring_copy(side, step).wait_recv()
            if step < chips - 1:
                rows = self.rows(-way * (step + 1))
                total = self.mine[0, rows, at : at + count].astype(F32) + self.slots[side][step].astype(F32)
                total = total.astype(BF16)
                self.mine[0, rows, at : at + count] = total
                for number in range(len(self.links.further) if step == chips - 2 else 0):
                    copy = self.further_copy(side, number)
                    copy.start()
                    copy.wait()
                    total = (total.astype(F32) + self.further_in[side][number].astype(F32)).astype(BF16)
                    self.mine[0, rows, at : at + count] = total
                if step == chips - 2:
                    self.out[self.links.core, rows, at : at + count] = total
            if step < 2 * chips - 3:
                self.ring_copy(side, step + 1).start()

    def share(self):
        self.share_copy().start()

    def free_theirs(self):
        for part in range(2):
            self.part_copy(part).wait_send()

    def wait_all(self, theirs_waited):
        self.share_copy().wait_recv()
        self.share_copy().wait_send()
        if not theirs_waited:
            self.free_theirs()
        self.narrow_copy().wait_send()
        for side in range(2):
            for step in range(2 * self.links.chips - 2):
                self.ring_copy(side, step).wait_send()


def all_backward(layers, chips, *refs):
    (flag, vectors, cotangent), refs = refs[:3], refs[3:]
    kept = [refs[STATES * layer : STATES * (layer + 1)] for layer in range(layers)]
    refs = refs[STATES * layers :]
    (rows_ref, small_out), refs = refs[:2], refs[2:]
    outs = [refs[3 * layer : 3 * layer + 3] for layer in range(layers)]
    refs = refs[3 * layers :]
    state, refs = refs[:STATES], refs[STATES:]
    (acc, turned, summed_ref, mixed_grad_ref, inner_ref, query_grad_ref, here_ref, away_ref, rows_low, rows_in), refs = refs[:10], refs[10:]
    away_in, refs = refs[:layers], refs[layers:]
    theirs, refs = refs[:3], refs[3:]
    buffers = [refs[21 * layer : 21 * layer + 21] for layer in range(layers)]
    refs = refs[21 * layers :]
    (small, core_small, mid_small, row_small, sum_small, step_small), refs = refs[:6], refs[6:]
    (load_sem, away_send, away_recv, grad_send, grad_recv, ring_send, ring_recv, misc_send, misc_recv, step_send, step_recv, further_send, further_recv) = refs
    (wi, wo, we, ws, query, pair, remote_pair, mixed, total_ref, normed, first, first_scale, active, slope, second, second_scale, hidden_low) = state
    links = Links()
    links.ring(chips)
    core = links.core
    steps = chips.bit_length() - 1
    bits = links.bits

    def load_copy(layer, number):
        return pltpu.make_async_copy(kept[layer][number], state[number], load_sem.at[number])

    def load(layer, numbers):
        for number in numbers:
            load_copy(layer, number).start()

    def loaded(layer, *numbers):
        for number in numbers:
            load_copy(layer, number).wait()

    block_group = (14, 15, 3, 13, 12, 2, 9, 10, 11, 1, 7)
    pair_group = (4, 5, 6, 8)
    input_group = (16, 0)
    load(layers - 1, block_group + pair_group + input_group)
    links.greet([links.across, links.beside, links.opposite, links.right, links.left] + bits)
    misc = (misc_send, misc_recv)
    gradients = []
    for layer in range(layers):
        group = []
        for kind in range(3):
            mine, core_in, narrow_in, slot_one, slot_two, further_one, further_two = buffers[layer][7 * kind : 7 * kind + 7]
            if kind < 2:
                half = mine.shape[2] // 2
                columns = ((0, half), (half, half))
            else:
                third = mine.shape[2] // 3
                columns = ((0, 2 * third), (2 * third, third))
            group.append(Gradient(
                links, 3 * layer + kind, mine, theirs[kind], core_in, narrow_in, (slot_one, slot_two), (further_one, further_two), outs[layer][kind], columns,
                ((grad_send, grad_recv), (ring_send, ring_recv), (further_send, further_recv)),
            ))
        gradients.append(group)
    rows, width = mixed.shape[1], mixed.shape[2]
    units, depth = ws.shape[1], ws.shape[2]
    halves = lane_halves((rows, width))
    shift = jnp.where(flag[0:1, 0:1] < 0.5, 0.0, MASKED)
    small[...] = jnp.zeros(small.shape, F32)
    half = lax.broadcasted_iota(jnp.int32, (16, width), 1) // DH
    which = lax.broadcasted_iota(jnp.int32, (16, width), 0) // 8
    selector = (half == which).astype(F32)
    acc[...] = cotangent[...].astype(F32)
    for layer in reversed(range(layers)):
        feed, output, inputs = gradients[layer]
        before = gradients[layer + 1] if layer + 1 < layers else None
        vector = lambda at: vectors[layer, at : at + 1]

        def put(gradient, index, at, value):
            @pl.when(index < 2)
            def _():
                gradient.mine[index, at : at + value.shape[0]] = value

            @pl.when(index >= 2)
            def _():
                gradient.theirs[index - 2, at : at + value.shape[0]] = value

        def tick(kind, step):
            return lambda: before[kind].tick(step)

        loaded(layer, 14, 15)
        incoming = acc[...]
        widened = norm_backward(incoming, second[...], second_scale[...], vector(4))
        sums = [column_sum(incoming), column_sum(incoming * second[...]), column_sum(widened)]
        acc[...] = widened
        rows_low[...] = widened.astype(BF16)
        loaded(layer, 9)
        turned[...] = normed[...].T
        loaded(layer, 3, 13, 12, 2)
        if before:
            for gradient in before:
                gradient.free_theirs()
        block_hooks = [[], [functools.partial(feed.send, 1)], [feed.middle], [functools.partial(feed.send, 0)]]
        if before:
            block_hooks[0].append(before[0].settle)
            for number in range(3):
                block_hooks[number + 1].append(tick(0, number))

        def one_quarter(step, carry):
            at_step(step, block_hooks)
            index = backwards(step)
            branch = rows_low[...]
            inner = (dot_rt(branch, ws[index]) * slope[index].astype(F32)).astype(BF16)
            put(feed, index, 0, dot_lt(active[index], branch).astype(BF16))
            put(feed, index, units, dot(turned[...], inner).astype(BF16))
            small[index, 8 * layer + 6 : 8 * layer + 7, 0:units] = column_sum(inner.astype(F32))
            acc[...] += dot_rt(inner, we[index])
            return carry

        lax.fori_loop(0, 4, one_quarter, 0)
        loaded(layer, 10, 11, 1, 7)
        outgoing = acc[...]
        summed = norm_backward(outgoing, first[...], first_scale[...], vector(1))
        sums += [column_sum(outgoing), column_sum(outgoing * first[...]), column_sum(summed)]
        for number, value in enumerate(sums):
            for quarter in range(4):
                small[quarter, 8 * layer + number : 8 * layer + number + 1] = value
        summed_ref[...] = summed
        rows_low[...] = summed.astype(BF16)
        if before:
            before[0].tick(3)
            before[1].settle()

        def one_output(step, carry):
            index = backwards(step)
            mixed_grad = dot_rt(rows_low[...], wo[index]).astype(BF16)
            mixed_grad_ref[index] = mixed_grad
            put(output, index, 0, dot_lt(mixed[index], rows_low[...]).astype(BF16))
            product = mixed_grad.astype(F32) * mixed[index].astype(F32)
            inner_ref[index] = lax.dot_general(
                selector, product, (((1,), (1,)), ((), ())), precision=lax.Precision.HIGHEST, preferred_element_type=F32
            )
            return carry

        lax.fori_loop(0, 4, one_output, 0)
        output.send(0)
        output.send(1)
        if layer > 0:
            load(layer - 1, block_group)
        loaded(layer, *pair_group)
        pair_hooks = [[], [output.middle], [], []]
        if before:
            pair_hooks[0] += [tick(0, 4), before[2].settle]
            pair_hooks[1] += [tick(0, 5), tick(1, 0), tick(2, 0)]
            pair_hooks[2] += [tick(0, 6), tick(1, 1), tick(2, 1)]
            pair_hooks[3] += [tick(0, 7), tick(1, 2), tick(2, 2)]

        def away_copy(there):
            return remote(away_ref.at[there], away_in[layer].at[there], (away_send, away_recv), (layer, there), links.beside)

        if before:
            for there in range(4):
                remote(away_ref.at[there], away_in[layer + 1].at[there], (away_send, away_recv), (layer + 1, there), links.beside).wait_send()

        def one_pair(step, carry):
            at_step(step, pair_hooks)
            there = backwards(step)
            index = lax.rem(there + 2, 4)
            queries, grads = query[index], mixed_grad_ref[index]
            query_turned = None
            for side in range(2):
                source, place = (pair, index) if side == 0 else (remote_pair, there)
                keys, values = source[place, :, :width], source[place, :, width:]
                key_grad = value_grad = None
                for part in range(2):
                    mask = halves if part == 0 else jnp.logical_not(halves)
                    masked_query = jnp.where(mask, queries, BF16(0))
                    masked_grad = jnp.where(mask, grads, BF16(0))
                    masked_key = jnp.where(mask, keys, BF16(0))
                    level = total_ref[index, 8 * part : 8 * part + 1]
                    if side == 1:
                        level = level - shift
                    weights = jnp.exp(dot_rt(keys, masked_query) - level)
                    update = dot(weights.astype(BF16), masked_grad)
                    value_grad = update if value_grad is None else value_grad + update
                    slopes = dot_rt(values, masked_grad) - inner_ref[index, 8 * part : 8 * part + 1]
                    slopes = (weights * slopes).astype(BF16)
                    update = dot(slopes, masked_query)
                    key_grad = update if key_grad is None else key_grad + update
                    update = dot_lt(masked_key, slopes)
                    query_turned = update if query_turned is None else query_turned + update
                if side == 0:
                    here_ref[index, :, :width] = key_grad
                    here_ref[index, :, width:] = value_grad
                else:
                    away_ref[there, :, :width] = key_grad.astype(BF16)
                    away_ref[there, :, width:] = value_grad.astype(BF16)
            away_copy(there).start()
            query_grad_ref[index] = (query_turned * DH ** (-0.5)).T.astype(BF16)
            return carry

        lax.fori_loop(0, 4, one_pair, 0)
        if layer > 0:
            load(layer - 1, pair_group)
        loaded(layer, *input_group)
        turned[...] = hidden_low[...].T
        acc[...] = summed_ref[...]
        input_hooks = [[], [functools.partial(inputs.send, 1)], [inputs.middle], [functools.partial(inputs.send, 0)]]
        if before:
            input_hooks[0] += [tick(0, 8)]
            input_hooks[1] += [tick(1, 3), tick(2, 3)]
            input_hooks[2] += [tick(0, 9)]
            input_hooks[3] += [tick(1, 4), tick(2, 4)]

        def one_input(step, carry):
            at_step(step, input_hooks)
            index = backwards(step)
            away_copy(index).wait_recv()
            pair_grad = (here_ref[index] + away_in[layer][index].astype(F32)).astype(BF16)
            triple = jnp.concatenate([query_grad_ref[index], pair_grad], 1)
            put(inputs, index, 0, dot(turned[...], triple).astype(BF16))
            acc[...] += dot_rt(triple, wi[index])
            small[index, 8 * layer + 7 : 8 * layer + 8, 0 : 3 * width] = column_sum(triple.astype(F32))
            return carry

        lax.fori_loop(0, 4, one_input, 0)
        if layer > 0:
            load(layer - 1, input_group)

    feed, output, inputs = gradients[0]
    rows_low[...] = acc[...].astype(BF16)
    swap_rows = remote(rows_low, rows_in, misc, 0, links.opposite)
    copy_core = remote(small.at[pl.ds(2, 2)], core_small, misc, 1, links.beside)
    copy_row = remote(mid_small, row_small, misc, 2, links.across)
    share_small = remote(small_out.at[core], small_out.at[core], misc, 3, links.beside)

    def step_copy(step):
        return remote(sum_small.at[step], step_small.at[step], (step_send, step_recv), step, bits[step])

    copy_core.start()

    @pl.when(links.moved)
    def _():
        swap_rows.start()

    copy_core.wait_recv()
    mid_small[...] = small[1] + core_small[1]
    copy_row.start()
    ticks = 2 * links.chips - 2
    queues = []
    if layers > 1:
        queues += [(0, gradients[1][0], 10), (0, gradients[1][1], 5), (0, gradients[1][2], 5)]
    feed_at, late_at = 0, 3
    queues += [(feed_at + 1, feed, 0), (late_at + 1, output, 0), (late_at + 1, inputs, 0)]
    for gradient in gradients[2:]:
        pass
    value = None
    for step in range(late_at + 1 + ticks):
        if step == feed_at:
            feed.settle()
        if step == late_at:
            output.settle()
            inputs.settle()
        for start, gradient, done in queues:
            at = step - start + done
            if step >= start and at < ticks:
                gradient.tick(at)
                if at == ticks - 1:
                    gradient.share()
        if step == 1:
            copy_row.wait_recv()
            value = small[0] + core_small[0] + row_small[...]
        if 1 < step <= steps + 1:
            step_copy(step - 2).wait_recv()
            value = value + step_small[step - 2]
        if 1 <= step <= steps:
            sum_small[step - 1] = value
            step_copy(step - 1).start()
        if step == steps + 1:
            small_out[core] = value
            share_small.start()

    @pl.when(links.moved)
    def _():
        swap_rows.wait_recv()
        swap_rows.wait_send()
        rows_ref[...] = rows_in[...].astype(F32)

    @pl.when(jnp.logical_not(links.moved))
    def _():
        rows_ref[...] = acc[...]

    share_small.wait_recv()
    share_small.wait_send()
    copy_core.wait_send()
    copy_row.wait_send()
    for step in range(steps):
        step_copy(step).wait_send()
    for there in range(4):
        remote(away_ref.at[there], away_in[0].at[there], (away_send, away_recv), (0, there), links.beside).wait_send()
    for layer in range(layers):
        for gradient in gradients[layer]:
            gradient.wait_all(layer > 0)


def assemble_kernel(layers, *refs):
    ins, refs = refs[: 3 * layers], refs[3 * layers :]
    (shrink_ref, expand_ref, output_ref, input_ref) = refs
    for layer in range(layers):
        feed, output, inputs = ins[3 * layer : 3 * layer + 3]
        units, depth = expand_ref.shape[2] // 2, expand_ref.shape[1]
        width = output_ref.shape[1] // 2
        for part in range(2):
            shrink_ref[layer, part * units : (part + 1) * units] = feed[part, 0:units].astype(F32)
            expand_ref[layer, :, part * units : (part + 1) * units] = feed[part, units : units + depth].astype(F32)
            output_ref[layer, part * width : (part + 1) * width] = output[part, 0:width].astype(F32)
            for kind in range(3):
                input_ref[kind, layer, :, part * width : (part + 1) * width] = inputs[part, 0:depth, kind * width : (kind + 1) * width].astype(F32)


VM = pl.BlockSpec(memory_space=pltpu.VMEM)
AN = pl.BlockSpec(memory_space=pl.ANY)


def shaped(dtype, *dims):
    return jax.ShapeDtypeStruct(dims, dtype)


def cost(flops, size):
    return pl.CostEstimate(flops=flops, bytes_accessed=size, transcendentals=0)


def local(
    tokens, input_weight, query_bias, value_bias, output_weight, output_bias, first_gain, first_shift,
    expand_weight, expand_bias, shrink_weight, shrink_bias, second_gain, second_shift, lengths, bucket, cotangent,
):
    wide, narrow = lax.axis_size("wide"), lax.axis_size("narrow")
    assert narrow == 2 and wide % 2 == 0
    layers, depth = input_weight.shape[0], input_weight.shape[1]
    rows = tokens.shape[0]
    width = input_weight.shape[3] // 2
    units = expand_weight.shape[2] // 2

    flag = jnp.broadcast_to(bucket, (8, 128)).astype(F32)
    input_own = (
        input_weight.reshape(layers, depth, 3, 2, width).transpose(0, 3, 1, 2, 4).reshape(layers, 2, depth, 3 * width)
    )
    output_own = output_weight.reshape(layers, 2, width, depth)
    shrink_own = shrink_weight.reshape(layers, 2, units, depth)
    small = jnp.concatenate([query_bias, value_bias, expand_bias], 1)
    vectors = jnp.stack(
        [output_bias, first_gain, first_shift, shrink_bias, second_gain, second_shift, output_bias, output_bias], 1
    )
    query_shape = shaped(BF16, 4, rows, width)
    pair_shape = shaped(BF16, 4, rows, 2 * width)
    row_shape = shaped(F32, rows, depth)
    low_shape = shaped(BF16, rows, depth)
    scale_shape = shaped(F32, rows, 1)
    stat_shape = shaped(F32, 4, 16, rows)
    wide_shape = shaped(BF16, 4, rows, units)
    state_shapes = [
        shaped(BF16, 4, depth, 3 * width), shaped(BF16, 4, width, depth), shaped(BF16, 4, depth, units), shaped(BF16, 4, units, depth),
        query_shape, pair_shape, pair_shape, query_shape, stat_shape, low_shape, row_shape, scale_shape, wide_shape, wide_shape, row_shape, scale_shape, low_shape,
    ]
    state_scratch = [pltpu.VMEM(shape.shape, shape.dtype) for shape in state_shapes]
    kept_shapes = state_shapes * layers
    results = pl.pallas_call(
        functools.partial(all_forward, layers),
        out_shape=[row_shape, low_shape, shaped(F32, 8, 128)] + kept_shapes,
        in_specs=[VM] * 5 + [AN] * 4,
        out_specs=[VM] * 3 + [AN] * len(kept_shapes),
        scratch_shapes=state_scratch * layers + [
            pltpu.SemaphoreType.DMA((layers, STATES)),
            pltpu.VMEM(small.shape, F32), pltpu.VMEM((rows, depth), F32), pltpu.VMEM((rows, depth), BF16), pltpu.VMEM((rows, depth), BF16),
            pltpu.SemaphoreType.DMA((8 * layers,)),
            pltpu.SemaphoreType.DMA((16 * layers,)), pltpu.SemaphoreType.DMA((16 * layers,)),
            pltpu.SemaphoreType.DMA((layers, 4)), pltpu.SemaphoreType.DMA((layers, 4)),
            pltpu.SemaphoreType.DMA((5,)), pltpu.SemaphoreType.DMA((5,)),
        ],
        compiler_params=pltpu.CompilerParams(collective_id=1, has_side_effects=True, vmem_limit_bytes=62 * 2**20),
        cost_estimate=cost(10**10, 10**8),
        name="forward",
    )(flag, tokens, cotangent, small, vectors, input_own, output_own, expand_weight, shrink_own)
    layer_output, cotangent, flag = results[:3]
    chips = wide // 2
    ring = ring_size(chips)
    further = (chips // ring).bit_length() - 1
    tall = lambda size: -(-size // (16 * ring)) * 16 * ring
    out_shapes, buffer_scratch, theirs_scratch = [], [], []
    for size, columns, first_columns in ((units + depth, depth, depth // 2), (width, depth, depth // 2), (depth, 3 * width, 2 * width)):
        out_shapes.append(shaped(BF16, 2, tall(size), columns))
        theirs_scratch.append(pltpu.VMEM((2, size, columns), BF16))
        slot = lambda count: pltpu.VMEM((ring - 1, tall(size) // ring, count), BF16)
        more = lambda count: pltpu.VMEM((further, tall(size) // ring, count) if further else (1, 16, 128), BF16)
        buffer_scratch += [
            pltpu.VMEM((2, tall(size), columns), BF16), pltpu.VMEM((2, size, columns), BF16), pltpu.VMEM((size, columns), BF16),
            slot(first_columns), slot(columns - first_columns), more(first_columns), more(columns - first_columns),
        ]
    small_rows = 8 * layers
    steps = chips.bit_length() - 1
    small_scratch = pltpu.VMEM((small_rows, depth), F32)
    ring_sem = pltpu.SemaphoreType.DMA((3 * layers, 2, 2 * ring - 2))
    further_sem = pltpu.SemaphoreType.DMA((3 * layers, 2, max(further, 1)))
    results = pl.pallas_call(
        functools.partial(all_backward, layers, chips),
        out_shape=[row_shape, shaped(F32, 2, small_rows, depth)] + out_shapes * layers,
        in_specs=[VM] * 3 + [AN] * len(kept_shapes),
        out_specs=[VM] * (2 + 3 * layers),
        scratch_shapes=state_scratch + [
            pltpu.VMEM((rows, depth), F32), pltpu.VMEM((depth, rows), BF16), pltpu.VMEM((rows, depth), F32),
            pltpu.VMEM(query_shape.shape, BF16), pltpu.VMEM(stat_shape.shape, F32), pltpu.VMEM(query_shape.shape, BF16),
            pltpu.VMEM(pair_shape.shape, F32), pltpu.VMEM(pair_shape.shape, BF16), pltpu.VMEM((rows, depth), BF16), pltpu.VMEM((rows, depth), BF16),
        ] + [pltpu.VMEM(pair_shape.shape, BF16)] * layers + theirs_scratch + buffer_scratch * layers + [
            pltpu.VMEM((4, small_rows, depth), F32), pltpu.VMEM((2, small_rows, depth), F32), small_scratch, small_scratch,
            pltpu.VMEM((steps, small_rows, depth), F32), pltpu.VMEM((steps, small_rows, depth), F32),
            pltpu.SemaphoreType.DMA((STATES,)),
            pltpu.SemaphoreType.DMA((layers, 4)), pltpu.SemaphoreType.DMA((layers, 4)),
            pltpu.SemaphoreType.DMA((3 * layers, 4)), pltpu.SemaphoreType.DMA((3 * layers, 4)),
            ring_sem, ring_sem,
            pltpu.SemaphoreType.DMA((4,)), pltpu.SemaphoreType.DMA((4,)),
            pltpu.SemaphoreType.DMA((steps,)), pltpu.SemaphoreType.DMA((steps,)), further_sem, further_sem,
        ],
        compiler_params=pltpu.CompilerParams(collective_id=0, has_side_effects=True, vmem_limit_bytes=67043328),
        cost_estimate=cost(10**10, 10**8),
        name="backward",
    )(flag, vectors, cotangent, *results[3:])
    input_rows, small = results[:2]
    shrink_grad, expand_grad, output_grad, input_grad = pl.pallas_call(
        functools.partial(assemble_kernel, layers),
        out_shape=[
            shaped(F32, layers, 2 * units, depth), shaped(F32, layers, depth, 2 * units), shaped(F32, layers, 2 * width, depth),
            shaped(F32, 3, layers, depth, 2 * width),
        ],
        in_specs=[VM] * (3 * layers),
        out_specs=[VM] * 4,
        compiler_params=pltpu.CompilerParams(vmem_limit_bytes=40 * 2**20),
        cost_estimate=cost(10**6, 2 * 10**7),
        name="assemble",
    )(*results[2:])
    small = small.reshape(2, layers, 8, depth)
    both = lambda at, a, b: small[:, :, at, a:b].transpose(1, 0, 2).reshape(layers, 2 * (b - a))
    vector = lambda at: small[0, :, at]
    return (
        layer_output,
        input_rows,
        input_grad.transpose(1, 2, 0, 3),
        both(7, 0, width),
        both(7, 2 * width, 3 * width),
        output_grad,
        vector(5),
        vector(4),
        vector(3),
        expand_grad,
        both(6, 0, units),
        shrink_grad,
        vector(2),
        vector(1),
        vector(0),
    )


def solution(mesh):
    split = P(AXES, None)
    in_specs = (
        split, P(None, None, None, "narrow"), P(None, "narrow"), P(None, "narrow"), P(None, "narrow", None), P(), P(), P(),
        P(None, None, "narrow"), P(None, "narrow"), P(None, "narrow", None), P(), P(), P(), P("wide"), P("wide"), split,
    )
    out_specs = (
        split, split, P(None, None, None, "narrow"), P(None, "narrow"), P(None, "narrow"), P(None, "narrow", None), P(), P(), P(),
        P(None, None, "narrow"), P(None, "narrow"), P(None, "narrow", None), P(), P(), P(),
    )
    return jax.shard_map(local, mesh=mesh, in_specs=in_specs, out_specs=out_specs, check_vma=False)
```

```python
import functools

import jax
import jax.numpy as jnp
from jax import lax
from jax.experimental import pallas as pl
from jax.experimental.pallas import tpu as pltpu
from jax.sharding import PartitionSpec as P

DH = 64
EPSILON = 1e-12
MASKED = -1e9
AXES = ("wide", "narrow")
F32 = jnp.float32
BF16 = jnp.bfloat16
STATES = 17


def dot(a, b):
    return lax.dot_general(a, b, (((1,), (0,)), ((), ())), preferred_element_type=F32)


def dot_rt(a, b):
    return lax.dot_general(a, b, (((1,), (1,)), ((), ())), preferred_element_type=F32)


def dot_lt(a, b):
    return lax.dot_general(a, b, (((0,), (0,)), ((), ())), preferred_element_type=F32)


def lane_halves(shape):
    lane = lax.broadcasted_iota(jnp.int32, shape, len(shape) - 1)
    return lane < DH


def normalise(x):
    centre = x - jnp.mean(x, -1, keepdims=True)
    scale = lax.rsqrt(jnp.mean(centre * centre, -1, keepdims=True) + EPSILON)
    return centre * scale, scale


def gelu_parts(a):
    square = jnp.exp(-0.5 * a * a)
    size = jnp.abs(a)
    t = 1.0 / (1.0 + (0.3275911 * 0.7071067811865476) * size)
    poly = t * (
        0.127414796
        + t * (-0.142248368 + t * (0.7107068705 + t * (-0.7265760135 + t * 0.5307027145)))
    )
    tail = poly * square
    phi = jnp.where(a >= 0, 1.0 - tail, tail)
    return a * phi, phi + a * square * 0.3989422804014327


def ring_size(chips):
    return min(chips, 8)


class Links:
    def __init__(self):
        self.wide, self.narrow = lax.axis_index("wide"), lax.axis_index("narrow")
        self.core = lax.rem(self.wide, 2)
        self.chip = self.wide // 2
        self.bit = lax.rem(self.chip, 2)
        other_core, other_narrow = self.wide + 1 - 2 * self.core, 1 - self.narrow
        self.beside = (other_core, self.narrow)
        self.across = (self.wide, other_narrow)
        self.next_bit = lax.rem(self.chip // 2, 2)
        self.along = (self.wide + 2 * (1 - 2 * self.bit), self.narrow)
        self.along_next = (self.wide + 4 * (1 - 2 * self.next_bit), self.narrow)
        self.opposite = (other_core, other_narrow)
        self.moved = self.core + self.narrow == 1

    def ring(self, chips):
        self.chips = ring_size(chips)
        self.group = self.chip // self.chips
        at = lax.rem(self.chip, self.chips)
        odd = lax.rem(at, 2)
        self.place = odd * (self.chips - 1 - at // 2) + (1 - odd) * (at // 2)
        self.right, self.left = self.ring_device(1), self.ring_device(-1)
        self.bits = []
        for bit in range(chips.bit_length() - 1):
            side = lax.rem(self.chip // 2**bit, 2)
            self.bits.append((self.wide + 2 ** (bit + 1) * (1 - 2 * side), self.narrow))
        self.further = self.bits[self.chips.bit_length() - 1 :]

    def ring_device(self, offset):
        place = lax.rem(self.place + offset + self.chips, self.chips)
        late = place // (self.chips // 2)
        chip = late * (2 * (self.chips - 1 - place) + 1) + (1 - late) * (2 * place)
        return (2 * (self.group * self.chips + chip) + self.core, self.narrow)

    def greet(self, devices):
        barrier = pltpu.get_barrier_semaphore()
        for device in devices:
            pl.semaphore_signal(barrier, inc=1, device_id=device, device_id_type=pl.DeviceIdType.MESH)
        pl.semaphore_wait(barrier, len(devices))


def remote(source, target, sems, at, device):
    return pltpu.make_async_remote_copy(
        source, target, sems[0].at[at], sems[1].at[at], device_id=device, device_id_type=pl.DeviceIdType.MESH
    )


class Weight:
    def __init__(self, links, number, own, parts, buffer, local_sem, sems):
        self.links, self.number, self.own, self.parts = links, number, own, parts
        self.buffer, self.local_sem, self.sems = buffer, local_sem, sems
        self.size = buffer.shape[1] // 4
        self.columns = buffer.shape[2] // parts

    def rows(self, flip, flip_next):
        bit = self.links.bit + flip * (1 - 2 * self.links.bit)
        next_bit = self.links.next_bit + flip_next * (1 - 2 * self.links.next_bit)
        return pl.ds(pl.multiple_of((2 * next_bit + bit) * self.size, 16), self.size)

    def local_copies(self):
        core = self.links.core
        copies = []
        for slot, part in ((0, core), (2, 1 - core)):
            for kind in range(self.parts):
                target = self.buffer.at[slot, :, pl.ds(kind * self.columns, self.columns)]
                copies.append(pltpu.make_async_copy(self.own(part, slice(None), kind), target, self.local_sem.at[self.number, len(copies)]))
        return copies

    def first_hops(self):
        rows = self.rows(0, 0)
        return [
            remote(
                self.own(self.links.core, rows, kind), self.buffer.at[1, rows, pl.ds(kind * self.columns, self.columns)],
                self.sems, (self.number, kind), self.links.across,
            )
            for kind in range(self.parts)
        ]

    def hop(self, kind):
        links = self.links
        at = (self.number, 2 + kind)
        device = links.along if kind == 1 or (kind == 3 and self.number % 2) else links.along_next
        if kind < 3:
            rows = self.rows(0, 0)
        elif kind == 3:
            rows = self.rows(0, 1) if self.number % 2 else self.rows(1, 0)
        else:
            rows = self.rows(kind % 2, (kind - 4) // 2)
        if kind < 4:
            return remote(self.buffer.at[1, rows], self.buffer.at[1, rows], self.sems, at, device)
        return remote(self.buffer.at[1, rows], self.buffer.at[3, rows], self.sems, at, links.beside)

    def start(self):
        for copy in self.first_hops():
            copy.start()

    def start_local(self):
        for copy in self.local_copies():
            copy.start()

    def relay(self):
        for copy in self.first_hops():
            copy.wait_recv()
        for kind in (1, 2, 4):
            self.hop(kind).start()

    def relay_again(self):
        self.hop(1).wait_recv()
        self.hop(2).wait_recv()
        for kind in (3, 5, 6):
            self.hop(kind).start()

    def relay_last(self):
        self.hop(3).wait_recv()
        self.hop(7).start()

    def wait_own(self):
        for copy in self.local_copies():
            copy.wait()

    def wait_fetched(self):
        for kind in range(4, 8):
            self.hop(kind).wait_recv()

    def wait_sent(self):
        for copy in self.first_hops() + [self.hop(kind) for kind in range(1, 8)]:
            copy.wait_send()


def ordered(step):
    return lax.rem(2 * step, 4) + step // 2


def at_step(step, hooks):
    for number, hook in enumerate(hooks):
        if hook:

            @pl.when(step == number)
            def _(hook=hook):
                for action in hook:
                    action()


def all_forward(layers, *refs):
    (flag, tokens, cotangent, query_bias, value_bias, expand_bias), refs = refs[:6], refs[6:]
    gains, refs = refs[:6], refs[6:]
    (wi_own, wo_own, we_own, ws_own), refs = refs[:4], refs[4:]
    (rows_ref, cotangent_in, flag_in), refs = refs[:3], refs[3:]
    kept = [refs[STATES * layer : STATES * (layer + 1)] for layer in range(layers)]
    refs = refs[STATES * layers :]
    states = [refs[STATES * layer : STATES * (layer + 1)] for layer in range(layers)]
    refs = refs[STATES * layers :]
    tokens_in = states[0][16]
    biases = (query_bias, value_bias, expand_bias)
    biases_in, refs = refs[:3], refs[3:]
    (save_sem, acc, rows_low, local_sem, send_sem, recv_sem, kv_send, kv_recv, misc_send, misc_recv) = refs
    links = Links()
    core = links.core
    sems = (send_sem, recv_sem)
    units = ws_own.shape[2]
    width = wo_own.shape[2]
    rows = tokens.shape[0]
    weights = []
    for layer in range(layers):
        buffers = states[layer][:4]

        def lanes(part, count):
            return pl.ds(pl.multiple_of(part * count, 128), count)

        owns = [
            lambda part, rows, kind, layer=layer: wi_own.at[layer, kind, rows, lanes(part, width)],
            lambda part, rows, kind, layer=layer: wo_own.at[layer, part, rows],
            lambda part, rows, kind, layer=layer: we_own.at[layer, rows, lanes(part, units)],
            lambda part, rows, kind, layer=layer: ws_own.at[layer, part, rows],
        ]
        weights.append([
            Weight(links, 4 * layer + number, owns[number], 3 if number == 0 else 1, buffers[number], local_sem, sems)
            for number in range(4)
        ])
    every = [weight for group in weights for weight in group]
    for weight in every[:4]:
        weight.start_local()
    links.greet([links.across, links.along, links.along_next, links.beside, links.opposite])
    misc = (misc_send, misc_recv)
    swap_tokens = remote(tokens, tokens_in, misc, 0, links.opposite)
    swap_flag = remote(flag, flag_in, misc, 1, links.opposite)
    swap_cotangent = remote(cotangent, cotangent_in, misc, 2, links.opposite)
    swap_rows = remote(rows_low, rows_ref, misc, 3, links.opposite)
    copy_biases = [remote(biases[number], biases_in[number], misc, 4 + number, links.across) for number in range(3)]

    @pl.when(links.moved)
    def _():
        swap_flag.start()
        swap_tokens.start()

    for copy in copy_biases:
        copy.start()
    every[0].start()

    @pl.when(links.moved)
    def _():
        for weight in every[1:]:
            weight.start()
        swap_cotangent.start()

    @pl.when(jnp.logical_not(links.moved))
    def _():
        tokens_in[...] = tokens[...]
        cotangent_in[...] = cotangent[...]
        flag_in[...] = flag[...]

    def start_rest():
        @pl.when(jnp.logical_not(links.moved))
        def _():
            for weight in every[1:]:
                weight.start()

        for weight in every[4:]:
            weight.start_local()

    def bias(number, layer, index):
        size = biases[number].shape[1] // 2
        part = core + (index // 2) * (1 - 2 * core)
        place = pl.ds(pl.multiple_of(part * size, 128), size)
        return jnp.where(
            lax.rem(index, 2) == 0, biases[number][layer : layer + 1, place], biases_in[number][layer : layer + 1, place]
        )

    @pl.when(links.moved)
    def _():
        swap_flag.wait_recv()
        swap_tokens.wait_recv()

    for copy in copy_biases:
        copy.wait_recv()
    shift = jnp.where(flag_in[0:1, 0:1] < 0.5, 0.0, MASKED)
    acc[...] = tokens_in[...].astype(F32)
    halves = lane_halves((rows, width))

    def save_copy(layer, number):
        return pltpu.make_async_copy(states[layer][number], kept[layer][number], save_sem.at[layer, number])

    def save(layer, *numbers):
        for number in numbers:
            save_copy(layer, number).start()

    for layer in range(layers):
        (wi, wo, we, ws, query_ref, pair_ref, remote_ref, mixed_ref, total_ref, normed_ref, first_ref, first_scale, active_ref, slope_ref, second_ref, second_scale, low_ref) = states[layer]
        vector = lambda at: gains[at][layer : layer + 1]
        wi_go, wo_go, we_go, ws_go = weights[layer]
        later = weights[layer + 1] if layer + 1 < layers else None
        if layer > 0:
            low_ref[...] = acc[...].astype(BF16)

        def exchange(index):
            return remote(pair_ref.at[index], remote_ref.at[index], (kv_send, kv_recv), (layer, index), links.beside)

        def project(step, carry):
            index = ordered(step)
            triple = dot(low_ref[...], wi[index])
            query = (triple[:, :width] + bias(0, layer, index)).astype(BF16)
            query_ref[index] = query * BF16(DH ** (-0.5))
            pair_ref[index, :, :width] = triple[:, width : 2 * width].astype(BF16)
            pair_ref[index, :, width:] = (triple[:, 2 * width :] + bias(1, layer, index)).astype(BF16)
            exchange(index).start()
            return carry

        def project_rest():
            lax.fori_loop(2, 4, project, 0)

        wi_go.wait_own()
        lax.fori_loop(0, 2, project, 0)
        after_pair = [[], [], [], []]
        if layer == 0:
            before_pair = [
                [],
                [wi_go.relay_again, wo_go.relay],
                [wi_go.relay_last, wo_go.relay_again, we_go.relay, wi_go.wait_fetched, project_rest],
                [wo_go.relay_last, we_go.relay_again, ws_go.relay],
            ]
            after_pair[0] = [start_rest, wi_go.relay]
            before_feed = [we_go.relay_last, ws_go.relay_again, wo_go.wait_fetched]
            before_quarter = [[], [ws_go.relay_last], [we_go.wait_fetched, ws_go.wait_fetched], []]
            if later:
                before_feed += [later[0].relay]
                before_quarter[1] += [later[0].relay_again, later[1].relay]
                before_quarter[2] += [later[2].relay]
                before_quarter[3] += [later[0].relay_last, later[1].relay_again]
        else:
            before_pair = [
                [ws_go.relay, we_go.relay_again, wo_go.relay_last],
                [ws_go.relay_again, we_go.relay_last],
                [ws_go.relay_last, wi_go.wait_fetched, project_rest],
                [],
            ]
            before_feed = [wo_go.wait_fetched]
            before_quarter = [[], [], [we_go.wait_fetched, ws_go.wait_fetched], []]
            if later:
                before_feed += [later[0].relay, later[1].relay]
                before_quarter[2] += [later[0].relay_again, later[1].relay_again, later[2].relay]
                before_quarter[3] += [later[0].relay_last]
        acc[...] += vector(0)

        def one_pair(step, carry):
            at_step(step, before_pair)
            index = ordered(step)
            there = lax.rem(index + 2, 4)
            exchange(there).wait_recv()
            at_step(step, after_pair)
            queries = query_ref[index]
            key_here, value_here = pair_ref[index, :, :width], pair_ref[index, :, width:]
            key_there, value_there = remote_ref[there, :, :width], remote_ref[there, :, width:]
            mixed, total = [], []
            for part in range(2):
                mask = halves if part == 0 else jnp.logical_not(halves)
                masked = jnp.where(mask, queries, BF16(0))
                here = dot_rt(masked, key_here)
                away = dot_rt(masked, key_there)
                peak = jnp.maximum(jnp.max(here, -1, keepdims=True), jnp.max(away, -1, keepdims=True) + shift)
                here = jnp.exp(here - peak)
                away = jnp.exp(away - (peak - shift))
                weight = jnp.sum(here, -1, keepdims=True) + jnp.sum(away, -1, keepdims=True)
                both = dot(here.astype(BF16), value_here) + dot(away.astype(BF16), value_there)
                mixed.append(both * (1.0 / weight))
                total.append(jnp.broadcast_to(peak + jnp.log(weight), (rows, width)))
            mixed_low = jnp.where(halves, mixed[0], mixed[1]).astype(BF16)
            mixed_ref[index] = mixed_low
            totals = jnp.where(halves, total[0], total[1]).T
            total_ref[index] = jnp.concatenate([totals[0:8], totals[DH : DH + 8]], 0)
            return carry

        lax.fori_loop(0, 4, one_pair, 0)
        for action in before_feed:
            action()
        wo_go.wait_own()
        total = acc[...]
        for index in range(4):
            total = total + dot(mixed_ref[index], wo[index])
        acc[...] = total
        save(layer, 16, 0, 4, 5, 6, 1, 7, 8)
        first, scale = normalise(acc[...])
        first_ref[...] = first
        first_scale[...] = scale
        normed = first * vector(1) + vector(2)
        normed_ref[...] = normed.astype(BF16)
        acc[...] = normed + vector(3)
        save(layer, 9, 10, 11)
        we_go.wait_own()
        ws_go.wait_own()

        def one_quarter(step, carry):
            at_step(step, before_quarter)
            index = ordered(step)
            active, slope = gelu_parts(dot(normed_ref[...], we[index]) + bias(2, layer, index))
            active_low = active.astype(BF16)
            active_ref[index] = active_low
            slope_ref[index] = slope.astype(BF16)
            acc[...] += dot(active_low, ws[index])
            return carry

        lax.fori_loop(0, 4, one_quarter, 0)
        save(layer, 2, 3, 12, 13)
        second, scale = normalise(acc[...])
        second_ref[...] = second
        second_scale[...] = scale
        save(layer, 14, 15)
        acc[...] = second * vector(4) + vector(5)

    rows_low[...] = acc[...].astype(BF16)

    @pl.when(links.moved)
    def _():
        swap_rows.start()

    @pl.when(jnp.logical_not(links.moved))
    def _():
        rows_ref[...] = rows_low[...]

    @pl.when(links.moved)
    def _():
        for copy in (swap_cotangent, swap_rows):
            copy.wait_recv()
        for copy in (swap_tokens, swap_flag, swap_cotangent, swap_rows):
            copy.wait_send()

    for copy in copy_biases:
        copy.wait_send()
    for weight in every:
        weight.wait_sent()
    for layer in range(layers):
        for number in range(STATES):
            save_copy(layer, number).wait()
    for layer in range(layers):
        pair_ref, remote_ref = states[layer][5:7]
        for index in range(4):
            remote(pair_ref.at[index], remote_ref.at[index], (kv_send, kv_recv), (layer, index), links.beside).wait_send()


def column_sum(x):
    return jnp.sum(x, 0, keepdims=True)


def norm_backward(grad, normed, scale, gain):
    scaled = grad * gain
    return (
        scaled - jnp.mean(scaled, -1, keepdims=True) - normed * jnp.mean(scaled * normed, -1, keepdims=True)
    ) * scale


def backwards(step):
    return 3 - ordered(step)


GRADIENT_LANES = (
    ((1, 0, 4), (-1, 1, 4), (1, 2, 4), (-1, 3, 4)),
    ((-1, 0, 1),),
    ((1, 0, 3), (-1, 1, 3), (1, 2, 3)),
)


def lanes_of(kind, columns):
    return [(way, at * columns // parts, columns // parts) for way, at, parts in GRADIENT_LANES[kind]]


class Gradient:
    def __init__(self, links, number, mine, theirs, core_in, narrow_in, slots, further_in, out, lanes, sems):
        self.links, self.number, self.mine, self.theirs, self.core_in = links, number, mine, theirs, core_in
        self.narrow_in, self.slots, self.further_in, self.out, self.lanes, self.sems = narrow_in, slots, further_in, out, lanes, sems
        self.size = core_in.shape[1]
        self.piece = mine.shape[1] // links.chips

    def part_copy(self, part):
        return remote(self.theirs.at[part], self.core_in.at[part], self.sems[0], (self.number, part), self.links.beside)

    def narrow_copy(self):
        return remote(self.mine.at[1, pl.ds(0, self.size)], self.narrow_in, self.sems[0], (self.number, 2), self.links.across)

    def share_copy(self):
        place = self.out.at[self.links.core]
        return remote(place, place, self.sems[0], (self.number, 3), self.links.beside)

    def ring_copy(self, lane, step):
        links = self.links
        way, at, count = self.lanes[lane]
        device = links.right if way > 0 else links.left
        where = (self.number, lane, step)
        if step < links.chips - 1:
            source = self.mine.at[0, self.rows(-way * step), pl.ds(at, count)]
            return remote(source, self.slots[lane].at[step], self.sems[1], where, device)
        rows = self.rows(-way * (step - links.chips))
        target = self.out.at[links.core, rows, pl.ds(at, count)]
        source = self.mine.at[0, rows, pl.ds(at, count)] if step == links.chips - 1 else target
        return remote(source, target, self.sems[1], where, device)

    def further_copy(self, lane, number):
        way, at, count = self.lanes[lane]
        source = self.mine.at[0, self.rows(way), pl.ds(at, count)]
        return remote(source, self.further_in[lane].at[number], self.sems[2], (self.number, lane, number), self.links.further[number])

    def rows(self, offset):
        index = lax.rem(self.links.place + offset + 2 * self.links.chips, self.links.chips)
        return pl.ds(pl.multiple_of(index * self.piece, 16), self.piece)

    def send(self, part):
        self.part_copy(part).start()

    def middle(self):
        self.part_copy(1).wait_recv()
        total = self.mine[1, 0 : self.size].astype(F32) + self.core_in[1].astype(F32)
        self.mine[1, 0 : self.size] = total.astype(BF16)
        self.narrow_copy().start()

    def settle(self):
        self.part_copy(0).wait_recv()
        self.narrow_copy().wait_recv()
        total = self.mine[0, 0 : self.size].astype(F32) + self.core_in[0].astype(F32) + self.narrow_in[...].astype(F32)
        self.mine[0, 0 : self.size] = total.astype(BF16)
        for lane in range(len(self.lanes)):
            self.ring_copy(lane, 0).start()

    def tick(self, step):
        chips = self.links.chips
        for lane, (way, at, count) in enumerate(self.lanes):
            self.ring_copy(lane, step).wait_recv()
            if step < chips - 1:
                rows = self.rows(-way * (step + 1))
                total = self.mine[0, rows, at : at + count].astype(F32) + self.slots[lane][step].astype(F32)
                total = total.astype(BF16)
                self.mine[0, rows, at : at + count] = total
                for number in range(len(self.links.further) if step == chips - 2 else 0):
                    copy = self.further_copy(lane, number)
                    copy.start()
                    copy.wait()
                    total = (total.astype(F32) + self.further_in[lane][number].astype(F32)).astype(BF16)
                    self.mine[0, rows, at : at + count] = total
                if step == chips - 2:
                    self.out[self.links.core, rows, at : at + count] = total
            if step < 2 * chips - 3:
                self.ring_copy(lane, step + 1).start()

    def share(self):
        self.share_copy().start()

    def free_theirs(self):
        for part in range(2):
            self.part_copy(part).wait_send()

    def wait_all(self, theirs_waited):
        self.share_copy().wait_recv()
        self.share_copy().wait_send()
        if not theirs_waited:
            self.free_theirs()
        self.narrow_copy().wait_send()
        for lane in range(len(self.lanes)):
            for step in range(2 * self.links.chips - 2):
                self.ring_copy(lane, step).wait_send()


def all_backward(layers, chips, *refs):
    (flag, cotangent), refs = refs[:2], refs[2:]
    gains, refs = refs[:6], refs[6:]
    kept = [refs[STATES * layer : STATES * (layer + 1)] for layer in range(layers)]
    refs = refs[STATES * layers :]
    (rows_ref, small_out), refs = refs[:2], refs[2:]
    outs = [[ref.at[layer] for ref in refs[:3]] for layer in range(layers)]
    refs = refs[3:]
    state, refs = refs[:STATES], refs[STATES:]
    (acc, turned, summed_ref, mixed_grad_ref, inner_ref, query_grad_ref, here_ref, away_ref, rows_low), refs = refs[:9], refs[9:]
    away_in, refs = refs[:layers], refs[layers:]
    theirs, refs = refs[:3], refs[3:]
    buffers = []
    for layer in range(layers):
        group = []
        for lanes in GRADIENT_LANES:
            count = len(lanes)
            group.append((refs[0], refs[1], refs[2], refs[3 : 3 + count], refs[3 + count : 3 + 2 * count]))
            refs = refs[3 + 2 * count :]
        buffers.append(group)
    (small, core_small, mid_small, row_small, sum_small, step_small), refs = refs[:6], refs[6:]
    (load_sem, away_send, away_recv, grad_send, grad_recv, ring_send, ring_recv, misc_send, misc_recv, step_send, step_recv, further_send, further_recv) = refs
    (wi, wo, we, ws, query, pair, remote_pair, mixed, total_ref, normed, first, first_scale, active, slope, second, second_scale, hidden_low) = state
    links = Links()
    links.ring(chips)
    core = links.core
    steps = chips.bit_length() - 1
    bits = links.bits

    def load_copy(layer, number):
        return pltpu.make_async_copy(kept[layer][number], state[number], load_sem.at[number])

    def load(layer, numbers):
        for number in numbers:
            load_copy(layer, number).start()

    def loaded(layer, *numbers):
        for number in numbers:
            load_copy(layer, number).wait()

    block_group = (14, 15, 3, 13, 12, 2, 9, 10, 11, 1, 7)
    pair_group = (4, 5, 6, 8)
    input_group = (16, 0)
    load(layers - 1, block_group + pair_group + input_group)
    links.greet([links.across, links.beside, links.opposite, links.right, links.left] + bits)
    misc = (misc_send, misc_recv)
    gradients = []
    for layer in range(layers):
        group = []
        for kind in range(3):
            mine, core_in, narrow_in, slots, further_in = buffers[layer][kind]
            group.append(Gradient(
                links, 3 * layer + kind, mine, theirs[kind], core_in, narrow_in, slots, further_in, outs[layer][kind],
                lanes_of(kind, mine.shape[2]), ((grad_send, grad_recv), (ring_send, ring_recv), (further_send, further_recv)),
            ))
        gradients.append(group)
    rows, width = mixed.shape[1], mixed.shape[2]
    units, depth = ws.shape[1], ws.shape[2]
    halves = lane_halves((rows, width))
    shift = jnp.where(flag[0:1, 0:1] < 0.5, 0.0, MASKED)
    small[...] = jnp.zeros(small.shape, F32)
    half = lax.broadcasted_iota(jnp.int32, (16, width), 1) // DH
    which = lax.broadcasted_iota(jnp.int32, (16, width), 0) // 8
    selector = (half == which).astype(F32)
    acc[...] = cotangent[...].astype(F32)
    for layer in reversed(range(layers)):
        feed, output, inputs = gradients[layer]
        before = gradients[layer + 1] if layer + 1 < layers else None
        vector = lambda at: gains[at][layer : layer + 1]

        def put(gradient, index, at, value):
            @pl.when(index < 2)
            def _():
                gradient.mine[index, at : at + value.shape[0]] = value

            @pl.when(index >= 2)
            def _():
                gradient.theirs[index - 2, at : at + value.shape[0]] = value

        def tick(kind, step):
            return lambda: before[kind].tick(step)

        loaded(layer, 14, 15)
        incoming = acc[...]
        widened = norm_backward(incoming, second[...], second_scale[...], vector(4))
        sums = [column_sum(incoming), column_sum(incoming * second[...]), column_sum(widened)]
        acc[...] = widened
        rows_low[...] = widened.astype(BF16)
        loaded(layer, 9)
        turned[...] = normed[...].T
        loaded(layer, 3, 13, 12, 2)
        if before:
            for gradient in before:
                gradient.free_theirs()
        block_hooks = [[], [functools.partial(feed.send, 1)], [], [functools.partial(feed.send, 0), feed.middle]]
        if before:
            block_hooks[0].append(before[0].settle)
            block_hooks[1].append(tick(0, 0))
            block_hooks[3].append(tick(0, 1))

        def one_quarter(step, carry):
            at_step(step, block_hooks)
            index = backwards(step)
            branch = rows_low[...]
            inner = (dot_rt(branch, ws[index]) * slope[index].astype(F32)).astype(BF16)
            put(feed, index, 0, dot_lt(active[index], branch).astype(BF16))
            put(feed, index, units, dot(turned[...], inner).astype(BF16))
            small[index, 8 * layer + 6 : 8 * layer + 7, 0:units] = column_sum(inner.astype(F32))
            acc[...] += dot_rt(inner, we[index])
            return carry

        lax.fori_loop(0, 4, one_quarter, 0)
        loaded(layer, 10, 11, 1, 7)
        outgoing = acc[...]
        summed = norm_backward(outgoing, first[...], first_scale[...], vector(1))
        sums += [column_sum(outgoing), column_sum(outgoing * first[...]), column_sum(summed)]
        for number, value in enumerate(sums):
            for quarter in range(4):
                small[quarter, 8 * layer + number : 8 * layer + number + 1] = value
        summed_ref[...] = summed
        rows_low[...] = summed.astype(BF16)
        if before:
            before[0].tick(2)
            before[1].settle()
            before[2].settle()

        def one_output(step, carry):
            index = backwards(step)
            mixed_grad = dot_rt(rows_low[...], wo[index]).astype(BF16)
            mixed_grad_ref[index] = mixed_grad
            put(output, index, 0, dot_lt(mixed[index], rows_low[...]).astype(BF16))
            product = mixed_grad.astype(F32) * mixed[index].astype(F32)
            inner_ref[index] = lax.dot_general(
                selector, product, (((1,), (1,)), ((), ())), precision=lax.Precision.HIGHEST, preferred_element_type=F32
            )
            return carry

        lax.fori_loop(0, 4, one_output, 0)
        output.send(0)
        output.send(1)
        if layer > 0:
            load(layer - 1, block_group)
        loaded(layer, *pair_group)
        pair_hooks = [[], [output.middle], [], []]
        middle_hooks = [[], [], [], []]
        if before:
            both = lambda step: [tick(1, step), tick(2, step)]
            pair_hooks[0] += [tick(0, 3)] + both(0)
            pair_hooks[1] += [tick(0, 4)] + both(1)
            middle_hooks[1] += [tick(0, 5)] + both(2)
            pair_hooks[2] += [tick(0, 6)] + both(3)
            middle_hooks[2] += [tick(0, 7)] + both(4)
            pair_hooks[3] += [tick(0, 8)] + both(5)
            middle_hooks[3] += [tick(0, 9)] + both(6)

        def away_copy(there):
            return remote(away_ref.at[there], away_in[layer].at[there], (away_send, away_recv), (layer, there), links.beside)

        if before:
            for there in range(4):
                remote(away_ref.at[there], away_in[layer + 1].at[there], (away_send, away_recv), (layer + 1, there), links.beside).wait_send()

        def one_pair(step, carry):
            at_step(step, pair_hooks)
            there = backwards(step)
            index = lax.rem(there + 2, 4)
            queries, grads = query[index], mixed_grad_ref[index]
            query_turned = None
            for side in range(2):
                if side == 1:
                    at_step(step, middle_hooks)
                source, place = (pair, index) if side == 0 else (remote_pair, there)
                keys, values = source[place, :, :width], source[place, :, width:]
                key_grad = value_grad = None
                for part in range(2):
                    mask = halves if part == 0 else jnp.logical_not(halves)
                    masked_query = jnp.where(mask, queries, BF16(0))
                    masked_grad = jnp.where(mask, grads, BF16(0))
                    masked_key = jnp.where(mask, keys, BF16(0))
                    level = total_ref[index, 8 * part : 8 * part + 1]
                    if side == 1:
                        level = level - shift
                    weights = jnp.exp(dot_rt(keys, masked_query) - level)
                    update = dot(weights.astype(BF16), masked_grad)
                    value_grad = update if value_grad is None else value_grad + update
                    slopes = dot_rt(values, masked_grad) - inner_ref[index, 8 * part : 8 * part + 1]
                    slopes = (weights * slopes).astype(BF16)
                    update = dot(slopes, masked_query)
                    key_grad = update if key_grad is None else key_grad + update
                    update = dot_lt(masked_key, slopes)
                    query_turned = update if query_turned is None else query_turned + update
                if side == 0:
                    here_ref[index, :, :width] = key_grad
                    here_ref[index, :, width:] = value_grad
                else:
                    away_ref[there, :, :width] = key_grad.astype(BF16)
                    away_ref[there, :, width:] = value_grad.astype(BF16)
            away_copy(there).start()
            query_grad_ref[index] = (query_turned * DH ** (-0.5)).T.astype(BF16)
            return carry

        lax.fori_loop(0, 4, one_pair, 0)
        if layer > 0:
            load(layer - 1, pair_group)
        loaded(layer, *input_group)
        turned[...] = hidden_low[...].T
        acc[...] = summed_ref[...]
        input_hooks = [[], [functools.partial(inputs.send, 1)], [inputs.middle], [functools.partial(inputs.send, 0)]]
        if before:
            feed.settle()
            input_hooks[0] += [tick(0, 10)] + both(7)
            input_hooks[2] += [tick(0, 11)] + both(8)
            input_hooks[3] += [functools.partial(feed.tick, 0)]

        def one_input(step, carry):
            at_step(step, input_hooks)
            index = backwards(step)
            away_copy(index).wait_recv()
            pair_grad = (here_ref[index] + away_in[layer][index].astype(F32)).astype(BF16)
            triple = jnp.concatenate([query_grad_ref[index], pair_grad], 1)
            put(inputs, index, 0, dot(turned[...], triple).astype(BF16))
            acc[...] += dot_rt(triple, wi[index])
            small[index, 8 * layer + 7 : 8 * layer + 8, 0 : 3 * width] = column_sum(triple.astype(F32))
            return carry

        lax.fori_loop(0, 4, one_input, 0)
        if layer > 0:
            load(layer - 1, input_group)

    feed, output, inputs = gradients[0]
    rows_low[...] = acc[...].astype(BF16)
    swap_rows = remote(rows_low, rows_ref, misc, 0, links.opposite)
    copy_core = remote(small.at[pl.ds(2, 2)], core_small, misc, 1, links.beside)
    copy_row = remote(mid_small, row_small, misc, 2, links.across)
    share_small = remote(small_out.at[core], small_out.at[core], misc, 3, links.beside)

    def step_copy(step):
        return remote(sum_small.at[step], step_small.at[step], (step_send, step_recv), step, bits[step])

    copy_core.start()
    copy_core.wait_recv()
    mid_small[...] = small[1] + core_small[1]
    copy_row.start()

    @pl.when(links.moved)
    def _():
        swap_rows.start()

    ticks = 2 * links.chips - 2
    queues = []
    if layers > 1:
        queues += [(0, gradients[1][0], 12), (0, gradients[1][1], 9), (0, gradients[1][2], 9)]
    late_at, small_at = 3, 4
    started = 1
    if layers == 1:
        feed.settle()
        started = 0
    queues += [(0, feed, started), (1, output, 0), (late_at + 1, inputs, 0)]
    value = None
    for step in range(late_at + 1 + ticks):
        if step == 0:
            output.settle()
        if step == late_at:
            inputs.settle()
        for start, gradient, done in queues:
            at = step - start + done
            if step >= start and at < ticks:
                gradient.tick(at)
                if at == ticks - 1:
                    gradient.share()
        if step == small_at:
            copy_row.wait_recv()
            value = small[0] + core_small[0] + row_small[...]
        if small_at < step <= small_at + steps:
            step_copy(step - small_at - 1).wait_recv()
            value = value + step_small[step - small_at - 1]
        if small_at <= step < small_at + steps:
            sum_small[step - small_at] = value
            step_copy(step - small_at).start()
        if step == small_at + steps:
            small_out[core] = value
            share_small.start()

    @pl.when(links.moved)
    def _():
        swap_rows.wait_recv()
        swap_rows.wait_send()

    @pl.when(jnp.logical_not(links.moved))
    def _():
        rows_ref[...] = rows_low[...]

    share_small.wait_recv()
    share_small.wait_send()
    copy_core.wait_send()
    copy_row.wait_send()
    for step in range(steps):
        step_copy(step).wait_send()
    for there in range(4):
        remote(away_ref.at[there], away_in[0].at[there], (away_send, away_recv), (0, there), links.beside).wait_send()
    for layer in range(layers):
        for gradient in gradients[layer]:
            gradient.wait_all(layer > 0)


def assemble_kernel(layers, *refs):
    (feed, output, inputs, small, out_rows, in_rows), refs = refs[:6], refs[6:]
    (shrink_ref, expand_ref, output_ref, input_ref, out_rows_ref, in_rows_ref), refs = refs[:6], refs[6:]
    vector_refs, (expand_bias_ref, query_bias_ref, value_bias_ref) = refs[:6], refs[6:]
    units, depth, width = shrink_ref.shape[1], shrink_ref.shape[2], output_ref.shape[1]
    shrink_ref[0] = feed[0, 0, 0:units].astype(F32)
    expand_ref[0] = feed[0, 0, units : units + depth].astype(F32)
    output_ref[0] = output[0, 0, 0:width].astype(F32)
    for kind in range(3):
        input_ref[0, kind] = inputs[0, 0, 0:depth, kind * width : (kind + 1) * width].astype(F32)
    out_rows_ref[...] = out_rows[...].astype(F32)
    in_rows_ref[...] = in_rows[...].astype(F32)

    @pl.when(pl.program_id(0) + pl.program_id(1) == 0)
    def _():
        for layer in range(layers):
            for number in range(6):
                vector_refs[number][layer : layer + 1] = small[0, 8 * layer + number : 8 * layer + number + 1]
            for part in range(2):
                row = slice(8 * layer + 6, 8 * layer + 7)
                expand_bias_ref[layer : layer + 1, part * units : (part + 1) * units] = small[part, row, 0:units]
                row = slice(8 * layer + 7, 8 * layer + 8)
                query_bias_ref[layer : layer + 1, part * width : (part + 1) * width] = small[part, row, 0:width]
                value_bias_ref[layer : layer + 1, part * width : (part + 1) * width] = small[part, row, 2 * width : 3 * width]


VM = pl.BlockSpec(memory_space=pltpu.VMEM)
AN = pl.BlockSpec(memory_space=pl.ANY)


def shaped(dtype, *dims):
    return jax.ShapeDtypeStruct(dims, dtype)


def cost(flops, size):
    return pl.CostEstimate(flops=flops, bytes_accessed=size, transcendentals=0)


def local(
    tokens, input_weight, query_bias, value_bias, output_weight, output_bias, first_gain, first_shift,
    expand_weight, expand_bias, shrink_weight, shrink_bias, second_gain, second_shift, lengths, bucket, cotangent,
):
    wide, narrow = lax.axis_size("wide"), lax.axis_size("narrow")
    assert narrow == 2 and wide % 2 == 0
    layers, depth = input_weight.shape[0], input_weight.shape[1]
    rows = tokens.shape[0]
    width = input_weight.shape[3] // 2
    units = expand_weight.shape[2] // 2

    flag = jnp.broadcast_to(bucket, (8, 128)).astype(F32)
    input_own = input_weight.transpose(0, 2, 1, 3)
    output_own = output_weight.reshape(layers, 2, width, depth)
    shrink_own = shrink_weight.reshape(layers, 2, units, depth)
    gains = (output_bias, first_gain, first_shift, shrink_bias, second_gain, second_shift)
    biases = (query_bias, value_bias, expand_bias)
    query_shape = shaped(BF16, 4, rows, width)
    pair_shape = shaped(BF16, 4, rows, 2 * width)
    row_shape = shaped(F32, rows, depth)
    low_shape = shaped(BF16, rows, depth)
    scale_shape = shaped(F32, rows, 1)
    stat_shape = shaped(F32, 4, 16, rows)
    wide_shape = shaped(BF16, 4, rows, units)
    state_shapes = [
        shaped(BF16, 4, depth, 3 * width), shaped(BF16, 4, width, depth), shaped(BF16, 4, depth, units), shaped(BF16, 4, units, depth),
        query_shape, pair_shape, pair_shape, query_shape, stat_shape, low_shape, row_shape, scale_shape, wide_shape, wide_shape, row_shape, scale_shape, low_shape,
    ]
    state_scratch = [pltpu.VMEM(shape.shape, shape.dtype) for shape in state_shapes]
    kept_shapes = state_shapes * layers
    results = pl.pallas_call(
        functools.partial(all_forward, layers),
        out_shape=[low_shape, low_shape, shaped(F32, 8, 128)] + kept_shapes,
        in_specs=[VM] * 12 + [AN] * 4,
        out_specs=[VM] * 3 + [AN] * len(kept_shapes),
        scratch_shapes=state_scratch * layers + [pltpu.VMEM(bias.shape, F32) for bias in biases] + [
            pltpu.SemaphoreType.DMA((layers, STATES)),
            pltpu.VMEM((rows, depth), F32), pltpu.VMEM((rows, depth), BF16),
            pltpu.SemaphoreType.DMA((4 * layers, 6)),
            pltpu.SemaphoreType.DMA((4 * layers, 10)), pltpu.SemaphoreType.DMA((4 * layers, 10)),
            pltpu.SemaphoreType.DMA((layers, 4)), pltpu.SemaphoreType.DMA((layers, 4)),
            pltpu.SemaphoreType.DMA((7,)), pltpu.SemaphoreType.DMA((7,)),
        ],
        compiler_params=pltpu.CompilerParams(collective_id=1, has_side_effects=True, vmem_limit_bytes=62 * 2**20),
        cost_estimate=cost(10**10, 10**8),
        name="forward",
    )(flag, tokens, cotangent, *biases, *gains, input_own, output_own, expand_weight, shrink_own)
    out_rows, cotangent, flag = results[:3]
    chips = wide // 2
    ring = ring_size(chips)
    further = (chips // ring).bit_length() - 1
    tall = lambda size: -(-size // (16 * ring)) * 16 * ring
    out_shapes, buffer_scratch, theirs_scratch = [], [], []
    for kind, (size, columns) in enumerate(((units + depth, depth), (width, depth), (depth, 3 * width))):
        out_shapes.append(shaped(BF16, layers, 2, tall(size), columns))
        theirs_scratch.append(pltpu.VMEM((2, size, columns), BF16))
        slot = lambda count: pltpu.VMEM((ring - 1, tall(size) // ring, count), BF16)
        more = lambda count: pltpu.VMEM((further, tall(size) // ring, count) if further else (1, 16, 128), BF16)
        buffer_scratch += [
            pltpu.VMEM((2, tall(size), columns), BF16), pltpu.VMEM((2, size, columns), BF16), pltpu.VMEM((size, columns), BF16),
        ]
        lanes = lanes_of(kind, columns)
        buffer_scratch += [slot(count) for way, at, count in lanes] + [more(count) for way, at, count in lanes]
    small_rows = 8 * layers
    steps = chips.bit_length() - 1
    small_scratch = pltpu.VMEM((small_rows, depth), F32)
    ring_sem = pltpu.SemaphoreType.DMA((3 * layers, 4, 2 * ring - 2))
    further_sem = pltpu.SemaphoreType.DMA((3 * layers, 4, max(further, 1)))
    results = pl.pallas_call(
        functools.partial(all_backward, layers, chips),
        out_shape=[low_shape, shaped(F32, 2, small_rows, depth)] + out_shapes,
        in_specs=[VM] * 8 + [AN] * len(kept_shapes),
        out_specs=[VM] * 5,
        scratch_shapes=state_scratch + [
            pltpu.VMEM((rows, depth), F32), pltpu.VMEM((depth, rows), BF16), pltpu.VMEM((rows, depth), F32),
            pltpu.VMEM(query_shape.shape, BF16), pltpu.VMEM(stat_shape.shape, F32), pltpu.VMEM(query_shape.shape, BF16),
            pltpu.VMEM(pair_shape.shape, F32), pltpu.VMEM(pair_shape.shape, BF16), pltpu.VMEM((rows, depth), BF16),
        ] + [pltpu.VMEM(pair_shape.shape, BF16)] * layers + theirs_scratch + buffer_scratch * layers + [
            pltpu.VMEM((4, small_rows, depth), F32), pltpu.VMEM((2, small_rows, depth), F32), small_scratch, small_scratch,
            pltpu.VMEM((steps, small_rows, depth), F32), pltpu.VMEM((steps, small_rows, depth), F32),
            pltpu.SemaphoreType.DMA((STATES,)),
            pltpu.SemaphoreType.DMA((layers, 4)), pltpu.SemaphoreType.DMA((layers, 4)),
            pltpu.SemaphoreType.DMA((3 * layers, 4)), pltpu.SemaphoreType.DMA((3 * layers, 4)),
            ring_sem, ring_sem,
            pltpu.SemaphoreType.DMA((4,)), pltpu.SemaphoreType.DMA((4,)),
            pltpu.SemaphoreType.DMA((steps,)), pltpu.SemaphoreType.DMA((steps,)), further_sem, further_sem,
        ],
        compiler_params=pltpu.CompilerParams(collective_id=0, has_side_effects=True, vmem_limit_bytes=67043328),
        cost_estimate=cost(10**10, 10**8),
        name="backward",
    )(flag, cotangent, *gains, *results[3:])
    in_rows, small = results[:2]
    whole = lambda *dims: pl.BlockSpec(dims, lambda layer, part: (0,) * len(dims))
    piece = lambda shape: pl.BlockSpec((1, 1) + shape.shape[2:], lambda layer, part: (layer, part, 0, 0))
    strip = pl.BlockSpec((rows // (2 * layers), depth), lambda layer, part: (2 * layer + part, 0))
    upright = lambda size: pl.BlockSpec((1, size, depth), lambda layer, part: (layer, part, 0))
    vector_shape = shaped(F32, layers, depth)
    outs = pl.pallas_call(
        functools.partial(assemble_kernel, layers),
        grid=(layers, 2),
        out_shape=[
            shaped(F32, layers, 2 * units, depth), shaped(F32, layers, depth, 2 * units), shaped(F32, layers, 2 * width, depth),
            shaped(F32, layers, 3, depth, 2 * width), row_shape, row_shape,
        ] + [vector_shape] * 6 + [shaped(F32, layers, 2 * units), shaped(F32, layers, 2 * width), shaped(F32, layers, 2 * width)],
        in_specs=[piece(shape) for shape in out_shapes] + [whole(2, small_rows, depth), strip, strip],
        out_specs=[
            upright(units), pl.BlockSpec((1, depth, units), lambda layer, part: (layer, 0, part)), upright(width),
            pl.BlockSpec((1, 3, depth, width), lambda layer, part: (layer, 0, 0, part)), strip, strip,
        ] + [whole(layers, depth)] * 6 + [whole(layers, 2 * units), whole(layers, 2 * width), whole(layers, 2 * width)],
        compiler_params=pltpu.CompilerParams(vmem_limit_bytes=40 * 2**20),
        cost_estimate=cost(10**6, 2 * 10**7),
        name="assemble",
    )(*results[2:], small, out_rows, in_rows)
    shrink_grad, expand_grad, output_grad, input_grad, layer_output, input_rows = outs[:6]
    second_shift_grad, second_gain_grad, shrink_bias_grad, first_shift_grad, first_gain_grad, output_bias_grad = outs[6:12]
    expand_bias_grad, query_bias_grad, value_bias_grad = outs[12:]
    return (
        layer_output,
        input_rows,
        input_grad.transpose(0, 2, 1, 3),
        query_bias_grad,
        value_bias_grad,
        output_grad,
        output_bias_grad,
        first_gain_grad,
        first_shift_grad,
        expand_grad,
        expand_bias_grad,
        shrink_grad,
        shrink_bias_grad,
        second_gain_grad,
        second_shift_grad,
    )


def solution(mesh):
    split = P(AXES, None)
    in_specs = (
        split, P(None, None, None, "narrow"), P(None, "narrow"), P(None, "narrow"), P(None, "narrow", None), P(), P(), P(),
        P(None, None, "narrow"), P(None, "narrow"), P(None, "narrow", None), P(), P(), P(), P("wide"), P("wide"), split,
    )
    out_specs = (
        split, split, P(None, None, None, "narrow"), P(None, "narrow"), P(None, "narrow"), P(None, "narrow", None), P(), P(), P(),
        P(None, None, "narrow"), P(None, "narrow"), P(None, "narrow", None), P(), P(), P(),
    )
    return jax.shard_map(local, mesh=mesh, in_specs=in_specs, out_specs=out_specs, check_vma=False)
```

```python
import functools

import jax
import jax.numpy as jnp
from jax import lax
from jax.experimental import pallas as pl
from jax.experimental.pallas import tpu as pltpu
from jax.sharding import PartitionSpec as P

DH = 64
EPSILON = 1e-12
MASKED = -1e9
AXES = ("wide", "narrow")
F32 = jnp.float32
BF16 = jnp.bfloat16
STATES = 17
KINDS = 5


def dot(a, b):
    return lax.dot_general(a, b, (((1,), (0,)), ((), ())), preferred_element_type=F32)


def dot_rt(a, b):
    return lax.dot_general(a, b, (((1,), (1,)), ((), ())), preferred_element_type=F32)


def dot_lt(a, b):
    return lax.dot_general(a, b, (((0,), (0,)), ((), ())), preferred_element_type=F32)


def lane_halves(shape):
    lane = lax.broadcasted_iota(jnp.int32, shape, len(shape) - 1)
    return lane < DH


def normalise(x):
    centre = x - jnp.mean(x, -1, keepdims=True)
    scale = lax.rsqrt(jnp.mean(centre * centre, -1, keepdims=True) + EPSILON)
    return centre * scale, scale


def gelu_parts(a):
    square = jnp.exp(-0.5 * a * a)
    size = jnp.abs(a)
    t = 1.0 / (1.0 + (0.3275911 * 0.7071067811865476) * size)
    poly = t * (
        0.127414796
        + t * (-0.142248368 + t * (0.7107068705 + t * (-0.7265760135 + t * 0.5307027145)))
    )
    tail = poly * square
    phi = jnp.where(a >= 0, 1.0 - tail, tail)
    return a * phi, phi + a * square * 0.3989422804014327


class Links:
    def __init__(self):
        self.wide, self.narrow = lax.axis_index("wide"), lax.axis_index("narrow")
        self.core = lax.rem(self.wide, 2)
        self.chip = self.wide // 2
        self.bit = lax.rem(self.chip, 2)
        other_core, other_narrow = self.wide + 1 - 2 * self.core, 1 - self.narrow
        self.beside = (other_core, self.narrow)
        self.across = (self.wide, other_narrow)
        self.next_bit = lax.rem(self.chip // 2, 2)
        self.along = (self.wide + 2 * (1 - 2 * self.bit), self.narrow)
        self.along_next = (self.wide + 4 * (1 - 2 * self.next_bit), self.narrow)
        self.opposite = (other_core, other_narrow)
        self.moved = self.core + self.narrow == 1

    def plane(self, chips):
        assert chips % 8 == 0
        self.line = lax.rem(self.chip // 2, 4)
        self.line_peers = []
        for offset in range(1, 4):
            there = lax.rem(self.line + offset, 4)
            self.line_peers.append((self.wide + 4 * (there - self.line), self.narrow))
        self.bits = []
        for bit in range(chips.bit_length() - 1):
            side = lax.rem(self.chip // 2**bit, 2)
            self.bits.append((self.wide + 2 ** (bit + 1) * (1 - 2 * side), self.narrow))
        self.further = self.bits[3:]

    def greet(self, devices):
        barrier = pltpu.get_barrier_semaphore()
        for device in devices:
            pl.semaphore_signal(barrier, inc=1, device_id=device, device_id_type=pl.DeviceIdType.MESH)
        pl.semaphore_wait(barrier, len(devices))


def remote(source, target, sems, at, device):
    return pltpu.make_async_remote_copy(
        source, target, sems[0].at[at], sems[1].at[at], device_id=device, device_id_type=pl.DeviceIdType.MESH
    )


class Weight:
    def __init__(self, links, number, own, parts, buffer, local_sem, sems):
        self.links, self.number, self.own, self.parts = links, number, own, parts
        self.buffer, self.local_sem, self.sems = buffer, local_sem, sems
        self.size = buffer.shape[1] // 4
        self.columns = buffer.shape[2] // parts

    def rows(self, flip, flip_next):
        bit = self.links.bit + flip * (1 - 2 * self.links.bit)
        next_bit = self.links.next_bit + flip_next * (1 - 2 * self.links.next_bit)
        return pl.ds(pl.multiple_of((2 * next_bit + bit) * self.size, 16), self.size)

    def local_copies(self):
        core = self.links.core
        copies = []
        for slot, part in ((0, core), (2, 1 - core)):
            for kind in range(self.parts):
                target = self.buffer.at[slot, :, pl.ds(kind * self.columns, self.columns)]
                copies.append(pltpu.make_async_copy(self.own(part, slice(None), kind), target, self.local_sem.at[self.number, len(copies)]))
        return copies

    def first_hops(self):
        rows = self.rows(0, 0)
        return [
            remote(
                self.own(self.links.core, rows, kind), self.buffer.at[1, rows, pl.ds(kind * self.columns, self.columns)],
                self.sems, (self.number, kind), self.links.across,
            )
            for kind in range(self.parts)
        ]

    def hop(self, kind):
        links = self.links
        at = (self.number, 2 + kind)
        device = links.along if kind == 1 or (kind == 3 and self.number % 2) else links.along_next
        if kind < 3:
            rows = self.rows(0, 0)
        elif kind == 3:
            rows = self.rows(0, 1) if self.number % 2 else self.rows(1, 0)
        else:
            rows = self.rows(kind % 2, (kind - 4) // 2)
        if kind < 4:
            return remote(self.buffer.at[1, rows], self.buffer.at[1, rows], self.sems, at, device)
        return remote(self.buffer.at[1, rows], self.buffer.at[3, rows], self.sems, at, links.beside)

    def start(self):
        for copy in self.first_hops():
            copy.start()

    def start_local(self):
        for copy in self.local_copies():
            copy.start()

    def relay(self):
        for copy in self.first_hops():
            copy.wait_recv()
        for kind in (1, 2, 4):
            self.hop(kind).start()

    def relay_again(self):
        self.hop(1).wait_recv()
        self.hop(2).wait_recv()
        for kind in (3, 5, 6):
            self.hop(kind).start()

    def relay_last(self):
        self.hop(3).wait_recv()
        self.hop(7).start()

    def wait_own(self):
        for copy in self.local_copies():
            copy.wait()

    def wait_fetched(self):
        for kind in range(4, 8):
            self.hop(kind).wait_recv()

    def wait_sent(self):
        for copy in self.first_hops() + [self.hop(kind) for kind in range(1, 8)]:
            copy.wait_send()


def ordered(step):
    return lax.rem(2 * step, 4) + step // 2


def at_step(step, hooks):
    for number, hook in enumerate(hooks):
        if hook:

            @pl.when(step == number)
            def _(hook=hook):
                for action in hook:
                    action()


def all_forward(layers, *refs):
    (flag, tokens, cotangent, query_bias, value_bias, expand_bias), refs = refs[:6], refs[6:]
    gains, refs = refs[:6], refs[6:]
    (wi_own, wo_own, we_own, ws_own), refs = refs[:4], refs[4:]
    (rows_low, cotangent_in, flag_in), refs = refs[:3], refs[3:]
    kept = [refs[STATES * layer : STATES * (layer + 1)] for layer in range(layers)]
    refs = refs[STATES * layers :]
    states = [refs[STATES * layer : STATES * (layer + 1)] for layer in range(layers)]
    refs = refs[STATES * layers :]
    tokens_in = states[0][16]
    biases = (query_bias, value_bias, expand_bias)
    biases_in, refs = refs[:3], refs[3:]
    (save_sem, acc, local_sem, send_sem, recv_sem, kv_send, kv_recv, misc_send, misc_recv) = refs
    links = Links()
    core = links.core
    sems = (send_sem, recv_sem)
    units = ws_own.shape[2]
    width = wo_own.shape[2]
    rows = tokens.shape[0]
    weights = []
    for layer in range(layers):
        buffers = states[layer][:4]

        def lanes(part, count):
            return pl.ds(pl.multiple_of(part * count, 128), count)

        owns = [
            lambda part, rows, kind, layer=layer: wi_own.at[layer, kind, rows, lanes(part, width)],
            lambda part, rows, kind, layer=layer: wo_own.at[layer, part, rows],
            lambda part, rows, kind, layer=layer: we_own.at[layer, rows, lanes(part, units)],
            lambda part, rows, kind, layer=layer: ws_own.at[layer, part, rows],
        ]
        weights.append([
            Weight(links, 4 * layer + number, owns[number], 3 if number == 0 else 1, buffers[number], local_sem, sems)
            for number in range(4)
        ])
    every = [weight for group in weights for weight in group]
    for weight in every[:4]:
        weight.start_local()
    links.greet([links.across, links.along, links.along_next, links.beside, links.opposite])
    misc = (misc_send, misc_recv)
    swap_tokens = remote(tokens, tokens_in, misc, 0, links.opposite)
    swap_flag = remote(flag, flag_in, misc, 1, links.opposite)
    swap_cotangent = remote(cotangent, cotangent_in, misc, 2, links.opposite)
    copy_biases = [remote(biases[number], biases_in[number], misc, 4 + number, links.across) for number in range(3)]

    for copy in copy_biases:
        copy.start()
    every[0].start()

    @pl.when(links.moved)
    def _():
        swap_flag.start()
        swap_tokens.start()
        for weight in every[1:]:
            weight.start()
        swap_cotangent.start()

    @pl.when(jnp.logical_not(links.moved))
    def _():
        tokens_in[...] = tokens[...]
        cotangent_in[...] = cotangent[...]
        flag_in[...] = flag[...]

    def start_rest():
        @pl.when(jnp.logical_not(links.moved))
        def _():
            for weight in every[1:]:
                weight.start()

        for weight in every[4:]:
            weight.start_local()

    def bias(number, layer, index):
        size = biases[number].shape[1] // 2
        part = core + (index // 2) * (1 - 2 * core)
        place = pl.ds(pl.multiple_of(part * size, 128), size)
        return jnp.where(
            lax.rem(index, 2) == 0, biases[number][layer : layer + 1, place], biases_in[number][layer : layer + 1, place]
        )

    for copy in copy_biases:
        copy.wait_recv()
    every[0].relay()
    every[0].relay_again()

    @pl.when(links.moved)
    def _():
        swap_flag.wait_recv()
        swap_tokens.wait_recv()

    shift = jnp.where(flag_in[0:1, 0:1] < 0.5, 0.0, MASKED)
    acc[...] = tokens_in[...].astype(F32)
    halves = lane_halves((rows, width))

    def save_copy(layer, number):
        return pltpu.make_async_copy(states[layer][number], kept[layer][number], save_sem.at[layer, number])

    def save(layer, *numbers):
        for number in numbers:
            save_copy(layer, number).start()

    for layer in range(layers):
        (wi, wo, we, ws, query_ref, pair_ref, remote_ref, mixed_ref, total_ref, normed_ref, first_ref, first_scale, active_ref, slope_ref, second_ref, second_scale, low_ref) = states[layer]
        vector = lambda at: gains[at][layer : layer + 1]
        wi_go, wo_go, we_go, ws_go = weights[layer]
        later = weights[layer + 1] if layer + 1 < layers else None
        if layer > 0:
            low_ref[...] = acc[...].astype(BF16)

        def exchange(index):
            return remote(pair_ref.at[index], remote_ref.at[index], (kv_send, kv_recv), (layer, index), links.beside)

        def project(step, carry):
            index = ordered(step)
            triple = dot(low_ref[...], wi[index])
            query = (triple[:, :width] + bias(0, layer, index)).astype(BF16)
            query_ref[index] = query * BF16(DH ** (-0.5))
            pair_ref[index, :, :width] = triple[:, width : 2 * width].astype(BF16)
            pair_ref[index, :, width:] = (triple[:, 2 * width :] + bias(1, layer, index)).astype(BF16)
            exchange(index).start()
            return carry

        def project_rest():
            lax.fori_loop(2, 4, project, 0)

        wi_go.wait_own()
        lax.fori_loop(0, 2, project, 0)
        after_pair = [[], [], [], []]
        if layer == 0:
            before_pair = [
                [wi_go.relay_last],
                [wo_go.relay, we_go.relay],
                [wo_go.relay_again, we_go.relay_again, ws_go.relay, wi_go.wait_fetched, project_rest, wo_go.relay_last, wo_go.wait_fetched],
                [ws_go.relay_again, we_go.relay_last],
            ]
            after_pair[0] = [start_rest]
            before_feed = [ws_go.relay_last]
            before_quarter = [[], [], [we_go.wait_fetched, ws_go.wait_fetched], []]
            if later:
                before_feed += [later[0].relay, later[1].relay]
                before_quarter[1] += [later[2].relay]
                before_quarter[2] += [later[0].relay_again, later[1].relay_again]
                before_quarter[3] += [later[3].relay]
        else:
            before_pair = [
                [wi_go.relay_last, wo_go.relay_last, we_go.relay_again],
                [ws_go.relay_again, we_go.relay_last],
                [ws_go.relay_last, wi_go.wait_fetched, project_rest, wo_go.wait_fetched],
                [],
            ]
            before_feed = []
            before_quarter = [[], [], [we_go.wait_fetched, ws_go.wait_fetched], []]
            if later:
                before_feed += [later[0].relay, later[1].relay]
                before_quarter[1] += [later[2].relay]
                before_quarter[2] += [later[0].relay_again, later[1].relay_again]
                before_quarter[3] += [later[3].relay]
        acc[...] += vector(0)

        def one_pair(step, carry):
            at_step(step, before_pair)
            index = ordered(step)
            there = lax.rem(index + 2, 4)
            exchange(there).wait_recv()
            at_step(step, after_pair)
            queries = query_ref[index]
            key_here, value_here = pair_ref[index, :, :width], pair_ref[index, :, width:]
            key_there, value_there = remote_ref[there, :, :width], remote_ref[there, :, width:]
            mixed, total = [], []
            for part in range(2):
                mask = halves if part == 0 else jnp.logical_not(halves)
                masked = jnp.where(mask, queries, BF16(0))
                here = dot_rt(masked, key_here)
                away = dot_rt(masked, key_there)
                peak = jnp.maximum(jnp.max(here, -1, keepdims=True), jnp.max(away, -1, keepdims=True) + shift)
                here = jnp.exp(here - peak)
                away = jnp.exp(away - (peak - shift))
                weight = jnp.sum(here, -1, keepdims=True) + jnp.sum(away, -1, keepdims=True)
                both = dot(here.astype(BF16), value_here) + dot(away.astype(BF16), value_there)
                mixed.append(both * (1.0 / weight))
                total.append(jnp.broadcast_to(peak + jnp.log(weight), (rows, width)))
            mixed_low = jnp.where(halves, mixed[0], mixed[1]).astype(BF16)
            mixed_ref[index] = mixed_low
            totals = jnp.where(halves, total[0], total[1]).T
            total_ref[index] = jnp.concatenate([totals[0:8], totals[DH : DH + 8]], 0)
            acc[...] += dot(mixed_low, wo[index])
            return carry

        wo_go.wait_own()
        lax.fori_loop(0, 4, one_pair, 0)
        for action in before_feed:
            action()
        save(layer, 16, 0, 4, 5, 6, 1, 7, 8)
        first, scale = normalise(acc[...])
        first_ref[...] = first
        first_scale[...] = scale
        normed = first * vector(1) + vector(2)
        normed_ref[...] = normed.astype(BF16)
        acc[...] = normed + vector(3)
        save(layer, 9, 10, 11)
        we_go.wait_own()
        ws_go.wait_own()

        def one_quarter(step, carry):
            at_step(step, before_quarter)
            index = ordered(step)
            active, slope = gelu_parts(dot(normed_ref[...], we[index]) + bias(2, layer, index))
            active_low = active.astype(BF16)
            active_ref[index] = active_low
            slope_ref[index] = slope.astype(BF16)
            acc[...] += dot(active_low, ws[index])
            return carry

        lax.fori_loop(0, 4, one_quarter, 0)
        save(layer, 2, 3, 12, 13)
        second, scale = normalise(acc[...])
        second_ref[...] = second
        second_scale[...] = scale
        save(layer, 14, 15)
        acc[...] = second * vector(4) + vector(5)

    rows_low[...] = acc[...].astype(BF16)

    @pl.when(links.moved)
    def _():
        swap_cotangent.wait_recv()
        for copy in (swap_tokens, swap_flag, swap_cotangent):
            copy.wait_send()

    for copy in copy_biases:
        copy.wait_send()
    for weight in every:
        weight.wait_sent()
    for layer in range(layers):
        for number in range(STATES):
            save_copy(layer, number).wait()
    for layer in range(layers):
        pair_ref, remote_ref = states[layer][5:7]
        for index in range(4):
            remote(pair_ref.at[index], remote_ref.at[index], (kv_send, kv_recv), (layer, index), links.beside).wait_send()


def column_sum(x):
    return jnp.sum(x, 0, keepdims=True)


def norm_backward(grad, normed, scale, gain):
    scaled = grad * gain
    return (
        scaled - jnp.mean(scaled, -1, keepdims=True) - normed * jnp.mean(scaled * normed, -1, keepdims=True)
    ) * scale


def backwards(step):
    return 3 - ordered(step)


class Gradient:
    def __init__(self, links, number, mine, theirs, core_in, narrow_in, pair_in, line_in, further_in, out, sems):
        self.links, self.number, self.mine, self.theirs, self.core_in = links, number, mine, theirs, core_in
        self.narrow_in, self.pair_in, self.line_in, self.further_in, self.out, self.sems = narrow_in, pair_in, line_in, further_in, out, sems
        self.size = core_in.shape[1]
        self.piece = mine.shape[1] // 8

    def copy(self, source, target, at, device):
        return remote(source, target, self.sems, (self.number, at), device)

    def part_copy(self, part):
        return self.copy(self.theirs.at[part], self.core_in.at[part], part, self.links.beside)

    def narrow_copy(self):
        return self.copy(self.mine.at[1, pl.ds(0, self.size)], self.narrow_in, 2, self.links.across)

    def share_copy(self):
        place = self.out.at[self.links.core]
        return self.copy(place, place, 3, self.links.beside)

    def half_rows(self, other):
        bit = self.links.bit + other * (1 - 2 * self.links.bit)
        return pl.ds(pl.multiple_of(bit * 4 * self.piece, 16), 4 * self.piece)

    def piece_rows(self, offset):
        index = 4 * self.links.bit + lax.rem(self.links.line + offset, 4)
        return pl.ds(pl.multiple_of(index * self.piece, 16), self.piece)

    def pair_copy(self):
        return self.copy(self.mine.at[0, self.half_rows(1)], self.pair_in, 4, self.links.along)

    def line_copy(self, offset):
        device = self.links.line_peers[offset - 1]
        return self.copy(self.mine.at[0, self.piece_rows(offset)], self.line_in.at[offset - 1], 4 + offset, device)

    def line_back(self, offset):
        place = self.out.at[self.links.core, self.piece_rows(0)]
        return self.copy(place, place, 7 + offset, self.links.line_peers[offset - 1])

    def pair_back(self):
        place = self.out.at[self.links.core, self.half_rows(0)]
        return self.copy(place, place, 11, self.links.along)

    def further_copy(self, number):
        place = self.mine.at[0, self.piece_rows(0)]
        return self.copy(place, self.further_in.at[number], 12 + number, self.links.further[number])

    def send(self, part):
        self.part_copy(part).start()

    def middle(self):
        self.part_copy(1).wait_recv()
        self.mine[1, 0 : self.size] = add(self.mine[1, 0 : self.size], self.core_in[1])
        self.narrow_copy().start()

    def settle(self):
        self.part_copy(0).wait_recv()
        self.narrow_copy().wait_recv()
        self.mine[0, 0 : self.size] = add(self.mine[0, 0 : self.size], self.core_in[0], self.narrow_in[...])
        self.pair_copy().start()

    def cross(self):
        self.pair_copy().wait_recv()
        rows = self.half_rows(0)
        self.mine[0, rows] = add(self.mine[0, rows], self.pair_in[...])
        for offset in range(1, 4):
            self.line_copy(offset).start()

    def spread(self):
        for offset in range(1, 4):
            self.line_copy(offset).wait_recv()
        rows = self.piece_rows(0)
        total = add(self.mine[0, rows], self.line_in[0], self.line_in[1], self.line_in[2])
        for number in range(len(self.links.further)):
            self.mine[0, rows] = total
            copy = self.further_copy(number)
            copy.start()
            copy.wait()
            total = add(total, self.further_in[number])
        self.out[self.links.core, rows] = total
        for offset in range(1, 4):
            self.line_back(offset).start()

    def widen(self):
        for offset in range(1, 4):
            self.line_back(offset).wait_recv()
        self.pair_back().start()

    def share(self):
        self.pair_back().wait_recv()
        self.share_copy().start()

    def free_theirs(self):
        for part in range(2):
            self.part_copy(part).wait_send()

    def wait_all(self, theirs_waited):
        self.share_copy().wait_recv()
        if not theirs_waited:
            self.free_theirs()
        copies = [self.share_copy(), self.narrow_copy(), self.pair_copy(), self.pair_back()]
        for offset in range(1, 4):
            copies += [self.line_copy(offset), self.line_back(offset)]
        for copy in copies:
            copy.wait_send()


def add(*terms):
    total = terms[0].astype(F32)
    for term in terms[1:]:
        total = total + term.astype(F32)
    return total.astype(BF16)


def all_backward(layers, chips, *refs):
    (flag, cotangent, out_low), refs = refs[:3], refs[3:]
    gains, refs = refs[:6], refs[6:]
    kept = [refs[STATES * layer : STATES * (layer + 1)] for layer in range(layers)]
    refs = refs[STATES * layers :]
    (out_rows, rows_ref, small_out), refs = refs[:3], refs[3:]
    outs = [[ref.at[layer] for ref in refs[:KINDS]] for layer in range(layers)]
    refs = refs[KINDS:]
    state, refs = refs[:STATES], refs[STATES:]
    (acc, turned, summed_ref, mixed_grad_ref, inner_ref, query_grad_ref, here_ref, away_ref, rows_low, rows_back), refs = refs[:10], refs[10:]
    away_in, refs = refs[:layers], refs[layers:]
    theirs, refs = refs[:KINDS], refs[KINDS:]
    buffers = []
    for layer in range(layers):
        buffers.append([refs[6 * kind : 6 * kind + 6] for kind in range(KINDS)])
        refs = refs[6 * KINDS :]
    (small, core_small, mid_small, row_small, sum_small, step_small), refs = refs[:6], refs[6:]
    (load_sem, away_send, away_recv, grad_send, grad_recv, misc_send, misc_recv, step_send, step_recv) = refs
    (wi, wo, we, ws, query, pair, remote_pair, mixed, total_ref, normed, first, first_scale, active, slope, second, second_scale, hidden_low) = state
    links = Links()
    links.plane(chips)
    core = links.core
    steps = chips.bit_length() - 1
    bits = links.bits

    def load_copy(layer, number):
        return pltpu.make_async_copy(kept[layer][number], state[number], load_sem.at[number])

    def load(layer, numbers):
        for number in numbers:
            load_copy(layer, number).start()

    def loaded(layer, *numbers):
        for number in numbers:
            load_copy(layer, number).wait()

    block_group = (14, 15, 3, 13, 12, 2, 9, 10, 11, 1, 7)
    pair_group = (4, 5, 6, 8)
    input_group = (16, 0)
    load(layers - 1, block_group + pair_group + input_group)
    links.greet([links.across, links.beside, links.opposite] + links.line_peers + bits)
    misc = (misc_send, misc_recv)
    gradients = []
    for layer in range(layers):
        group = []
        for kind in range(KINDS):
            mine, core_in, narrow_in, pair_in, line_in, further_in = buffers[layer][kind]
            group.append(Gradient(
                links, KINDS * layer + kind, mine, theirs[kind], core_in, narrow_in, pair_in, line_in, further_in,
                outs[layer][kind], (grad_send, grad_recv),
            ))
        gradients.append(group)
    rows, width = mixed.shape[1], mixed.shape[2]
    units, depth = ws.shape[1], ws.shape[2]
    halves = lane_halves((rows, width))
    shift = jnp.where(flag[0:1, 0:1] < 0.5, 0.0, MASKED)
    small[...] = jnp.zeros(small.shape, F32)
    half = lax.broadcasted_iota(jnp.int32, (16, width), 1) // DH
    which = lax.broadcasted_iota(jnp.int32, (16, width), 0) // 8
    selector = (half == which).astype(F32)
    acc[...] = cotangent[...].astype(F32)
    swap_rows = remote(rows_back, rows_ref, misc, 0, links.opposite)
    swap_out = remote(out_low, out_rows, misc, 4, links.opposite)

    @pl.when(links.moved)
    def _():
        swap_out.start()

    @pl.when(jnp.logical_not(links.moved))
    def _():
        out_rows[...] = out_low[...]

    for layer in reversed(range(layers)):
        shrink, expand, output, input_one, input_two = gradients[layer]
        before = gradients[layer + 1] if layer + 1 < layers else None
        vector = lambda at: gains[at][layer : layer + 1]

        def put(gradient, index, at, value):
            @pl.when(index < 2)
            def _():
                gradient.mine[index, at : at + value.shape[0]] = value

            @pl.when(index >= 2)
            def _():
                gradient.theirs[index - 2, at : at + value.shape[0]] = value

        def act(name, *which):
            return [getattr(gradient, name) for gradient in which]

        loaded(layer, 14, 15)
        incoming = acc[...]
        widened = norm_backward(incoming, second[...], second_scale[...], vector(4))
        sums = [column_sum(incoming), column_sum(incoming * second[...]), column_sum(widened)]
        acc[...] = widened
        rows_low[...] = widened.astype(BF16)
        loaded(layer, 9)
        turned[...] = normed[...].T
        loaded(layer, 3, 13, 12, 2)
        if before:
            for gradient in before:
                gradient.free_theirs()
        partly = lambda part, *which: [functools.partial(gradient.send, part) for gradient in which]
        block_hooks = [[], partly(1, shrink, expand), [], partly(0, shrink, expand) + act("middle", shrink, expand)]
        if before:
            block_hooks[0] += act("cross", before[0]) + act("settle", before[1])

        def one_quarter(step, carry):
            at_step(step, block_hooks)
            index = backwards(step)
            branch = rows_low[...]
            inner = (dot_rt(branch, ws[index]) * slope[index].astype(F32)).astype(BF16)
            put(shrink, index, 0, dot_lt(active[index], branch).astype(BF16))
            put(expand, index, 0, dot(turned[...], inner).astype(BF16))
            small[index, 8 * layer + 6 : 8 * layer + 7, 0:units] = column_sum(inner.astype(F32))
            acc[...] += dot_rt(inner, we[index])
            return carry

        lax.fori_loop(0, 4, one_quarter, 0)
        loaded(layer, 10, 11, 1, 7)
        outgoing = acc[...]
        summed = norm_backward(outgoing, first[...], first_scale[...], vector(1))
        sums += [column_sum(outgoing), column_sum(outgoing * first[...]), column_sum(summed)]
        for number, value in enumerate(sums):
            for quarter in range(4):
                small[quarter, 8 * layer + number : 8 * layer + number + 1] = value
        summed_ref[...] = summed
        rows_low[...] = summed.astype(BF16)
        if before:
            before[0].spread()
            before[1].cross()
            before[2].settle()

        def one_output(step, carry):
            index = backwards(step)
            mixed_grad = dot_rt(rows_low[...], wo[index]).astype(BF16)
            mixed_grad_ref[index] = mixed_grad
            put(output, index, 0, dot_lt(mixed[index], rows_low[...]).astype(BF16))
            product = mixed_grad.astype(F32) * mixed[index].astype(F32)
            inner_ref[index] = lax.dot_general(
                selector, product, (((1,), (1,)), ((), ())), precision=lax.Precision.HIGHEST, preferred_element_type=F32
            )
            return carry

        lax.fori_loop(0, 4, one_output, 0)
        output.send(0)
        output.send(1)
        if layer > 0:
            load(layer - 1, block_group)
        loaded(layer, *pair_group)
        pair_hooks = [[], [output.middle], [], []]
        if before:
            pair_hooks[0] += act("settle", before[3], before[4])
            pair_hooks[1] += act("cross", before[2]) + act("widen", before[0])
            pair_hooks[2] += act("spread", before[1], before[2])
            pair_hooks[3] += act("cross", before[3], before[4])
        pair_hooks[3] += act("settle", shrink)

        def away_copy(there):
            return remote(away_ref.at[there], away_in[layer].at[there], (away_send, away_recv), (layer, there), links.beside)

        if before:
            for there in range(4):
                remote(away_ref.at[there], away_in[layer + 1].at[there], (away_send, away_recv), (layer + 1, there), links.beside).wait_send()

        def one_pair(step, carry):
            at_step(step, pair_hooks)
            there = backwards(step)
            index = lax.rem(there + 2, 4)
            queries, grads = query[index], mixed_grad_ref[index]
            query_turned = None
            for side in range(2):
                source, place = (pair, index) if side == 0 else (remote_pair, there)
                keys, values = source[place, :, :width], source[place, :, width:]
                key_grad = value_grad = None
                for part in range(2):
                    mask = halves if part == 0 else jnp.logical_not(halves)
                    masked_query = jnp.where(mask, queries, BF16(0))
                    masked_grad = jnp.where(mask, grads, BF16(0))
                    masked_key = jnp.where(mask, keys, BF16(0))
                    level = total_ref[index, 8 * part : 8 * part + 1]
                    if side == 1:
                        level = level - shift
                    weights = jnp.exp(dot_rt(keys, masked_query) - level)
                    update = dot(weights.astype(BF16), masked_grad)
                    value_grad = update if value_grad is None else value_grad + update
                    slopes = dot_rt(values, masked_grad) - inner_ref[index, 8 * part : 8 * part + 1]
                    slopes = (weights * slopes).astype(BF16)
                    update = dot(slopes, masked_query)
                    key_grad = update if key_grad is None else key_grad + update
                    update = dot_lt(masked_key, slopes)
                    query_turned = update if query_turned is None else query_turned + update
                if side == 0:
                    here_ref[index, :, :width] = key_grad
                    here_ref[index, :, width:] = value_grad
                else:
                    away_ref[there, :, :width] = key_grad.astype(BF16)
                    away_ref[there, :, width:] = value_grad.astype(BF16)
            away_copy(there).start()
            query_grad_ref[index] = (query_turned * DH ** (-0.5)).T.astype(BF16)
            return carry

        lax.fori_loop(0, 4, one_pair, 0)
        if layer > 0:
            load(layer - 1, pair_group)
        loaded(layer, *input_group)
        turned[...] = hidden_low[...].T
        acc[...] = summed_ref[...]
        input_hooks = [[], partly(1, input_one, input_two), [], act("middle", input_one, input_two) + partly(0, input_one, input_two)]
        if before:
            input_hooks[0] += act("share", before[0])
            input_hooks[2] += act("widen", before[1], before[2])

        def one_input(step, carry):
            at_step(step, input_hooks)
            index = backwards(step)
            away_copy(index).wait_recv()
            pair_grad = (here_ref[index] + away_in[layer][index].astype(F32)).astype(BF16)
            triple = jnp.concatenate([query_grad_ref[index], pair_grad], 1)
            update = dot(turned[...], triple).astype(BF16)
            put(input_one, index, 0, update[: depth // 2])
            put(input_two, index, 0, update[depth // 2 :])
            acc[...] += dot_rt(triple, wi[index])
            small[index, 8 * layer + 7 : 8 * layer + 8, 0 : 3 * width] = column_sum(triple.astype(F32))
            return carry

        lax.fori_loop(0, 4, one_input, 0)
        if layer > 0:
            load(layer - 1, input_group)

    shrink, expand, output, input_one, input_two = gradients[0]
    rows_back[...] = acc[...].astype(BF16)
    copy_core = remote(small.at[pl.ds(2, 2)], core_small, misc, 1, links.beside)
    copy_row = remote(mid_small, row_small, misc, 2, links.across)
    share_small = remote(small_out.at[core], small_out.at[core], misc, 3, links.beside)

    def step_copy(step):
        return remote(sum_small.at[step], step_small.at[step], (step_send, step_recv), step, bits[step])

    copy_core.start()
    copy_core.wait_recv()
    mid_small[...] = small[1] + core_small[1]
    copy_row.start()

    @pl.when(links.moved)
    def _():
        swap_rows.start()

    plan = [(shrink, "cross"), (expand, "settle")]
    if layers > 1:
        shrink_two, expand_two, output_two, input_three, input_four = gradients[1]
        plan = [(input_three, "spread"), (input_four, "spread")] + plan + [(expand_two, "share"), (output_two, "share")]
    plan += [(output, "settle"), (shrink, "spread")]
    if layers > 1:
        plan += [(input_three, "widen"), (input_four, "widen")]
    plan += [
        (expand, "cross"), (output, "cross"), (input_one, "settle"), (shrink, "widen"), (expand, "spread"), (output, "spread"),
        (input_one, "cross"), (input_two, "settle"),
    ]
    if layers > 1:
        plan += [(input_three, "share"), (input_four, "share")]
    plan += [
        None, (shrink, "share"), (expand, "widen"), (input_one, "spread"), (input_two, "cross"), None, (output, "widen"),
        (input_one, "widen"), None, (expand, "share"), (input_two, "spread"), (output, "share"), None, (input_one, "share"), (input_two, "widen"),
    ]
    plan += [None] * (steps - 3) + [(input_two, "share")]
    step, value = 0, None
    for entry in plan:
        if entry:
            getattr(entry[0], entry[1])()
            continue
        if step == 0:
            copy_row.wait_recv()
            value = small[0] + core_small[0] + row_small[...]
        else:
            step_copy(step - 1).wait_recv()
            value = value + step_small[step - 1]
        if step < steps:
            sum_small[step] = value
            step_copy(step).start()
        else:
            small_out[core] = value
            share_small.start()
        step += 1
    assert step == steps + 1

    @pl.when(links.moved)
    def _():
        for copy in (swap_rows, swap_out):
            copy.wait_recv()
            copy.wait_send()

    @pl.when(jnp.logical_not(links.moved))
    def _():
        rows_ref[...] = rows_back[...]

    share_small.wait_recv()
    share_small.wait_send()
    copy_core.wait_send()
    copy_row.wait_send()
    for step in range(steps):
        step_copy(step).wait_send()
    for there in range(4):
        remote(away_ref.at[there], away_in[0].at[there], (away_send, away_recv), (0, there), links.beside).wait_send()
    for layer in range(layers):
        for gradient in gradients[layer]:
            gradient.wait_all(layer > 0)


def assemble_kernel(layers, *refs):
    (shrink, expand, output, input_one, input_two, small, out_rows, in_rows), refs = refs[:8], refs[8:]
    (shrink_ref, expand_ref, output_ref, input_ref, out_rows_ref, in_rows_ref), refs = refs[:6], refs[6:]
    vector_refs, (expand_bias_ref, query_bias_ref, value_bias_ref) = refs[:6], refs[6:]
    units, depth, width = shrink_ref.shape[1], shrink_ref.shape[2], output_ref.shape[1]
    shrink_ref[0] = shrink[0, 0, 0:units].astype(F32)
    expand_ref[0] = expand[0, 0, 0:depth].astype(F32)
    output_ref[0] = output[0, 0, 0:width].astype(F32)
    for kind in range(3):
        columns = slice(kind * width, (kind + 1) * width)
        input_ref[0, kind, 0 : depth // 2] = input_one[0, 0, 0 : depth // 2, columns].astype(F32)
        input_ref[0, kind, depth // 2 :] = input_two[0, 0, 0 : depth // 2, columns].astype(F32)
    out_rows_ref[...] = out_rows[...].astype(F32)
    in_rows_ref[...] = in_rows[...].astype(F32)

    @pl.when(pl.program_id(0) + pl.program_id(1) == 0)
    def _():
        for layer in range(layers):
            for number in range(6):
                vector_refs[number][layer : layer + 1] = small[0, 8 * layer + number : 8 * layer + number + 1]
            for part in range(2):
                row = slice(8 * layer + 6, 8 * layer + 7)
                expand_bias_ref[layer : layer + 1, part * units : (part + 1) * units] = small[part, row, 0:units]
                row = slice(8 * layer + 7, 8 * layer + 8)
                query_bias_ref[layer : layer + 1, part * width : (part + 1) * width] = small[part, row, 0:width]
                value_bias_ref[layer : layer + 1, part * width : (part + 1) * width] = small[part, row, 2 * width : 3 * width]


VM = pl.BlockSpec(memory_space=pltpu.VMEM)
AN = pl.BlockSpec(memory_space=pl.ANY)


def shaped(dtype, *dims):
    return jax.ShapeDtypeStruct(dims, dtype)


def cost(flops, size):
    return pl.CostEstimate(flops=flops, bytes_accessed=size, transcendentals=0)


def local(
    tokens, input_weight, query_bias, value_bias, output_weight, output_bias, first_gain, first_shift,
    expand_weight, expand_bias, shrink_weight, shrink_bias, second_gain, second_shift, lengths, bucket, cotangent,
):
    wide, narrow = lax.axis_size("wide"), lax.axis_size("narrow")
    assert narrow == 2 and wide % 2 == 0
    layers, depth = input_weight.shape[0], input_weight.shape[1]
    rows = tokens.shape[0]
    width = input_weight.shape[3] // 2
    units = expand_weight.shape[2] // 2

    flag = jnp.broadcast_to(bucket, (8, 128)).astype(F32)
    input_own = input_weight.transpose(0, 2, 1, 3)
    output_own = output_weight.reshape(layers, 2, width, depth)
    shrink_own = shrink_weight.reshape(layers, 2, units, depth)
    gains = (output_bias, first_gain, first_shift, shrink_bias, second_gain, second_shift)
    biases = (query_bias, value_bias, expand_bias)
    query_shape = shaped(BF16, 4, rows, width)
    pair_shape = shaped(BF16, 4, rows, 2 * width)
    row_shape = shaped(F32, rows, depth)
    low_shape = shaped(BF16, rows, depth)
    scale_shape = shaped(F32, rows, 1)
    stat_shape = shaped(F32, 4, 16, rows)
    wide_shape = shaped(BF16, 4, rows, units)
    state_shapes = [
        shaped(BF16, 4, depth, 3 * width), shaped(BF16, 4, width, depth), shaped(BF16, 4, depth, units), shaped(BF16, 4, units, depth),
        query_shape, pair_shape, pair_shape, query_shape, stat_shape, low_shape, row_shape, scale_shape, wide_shape, wide_shape, row_shape, scale_shape, low_shape,
    ]
    state_scratch = [pltpu.VMEM(shape.shape, shape.dtype) for shape in state_shapes]
    kept_shapes = state_shapes * layers
    results = pl.pallas_call(
        functools.partial(all_forward, layers),
        out_shape=[low_shape, low_shape, shaped(F32, 8, 128)] + kept_shapes,
        in_specs=[VM] * 12 + [AN] * 4,
        out_specs=[VM] * 3 + [AN] * len(kept_shapes),
        scratch_shapes=state_scratch * layers + [pltpu.VMEM(bias.shape, F32) for bias in biases] + [
            pltpu.SemaphoreType.DMA((layers, STATES)),
            pltpu.VMEM((rows, depth), F32),
            pltpu.SemaphoreType.DMA((4 * layers, 6)),
            pltpu.SemaphoreType.DMA((4 * layers, 10)), pltpu.SemaphoreType.DMA((4 * layers, 10)),
            pltpu.SemaphoreType.DMA((layers, 4)), pltpu.SemaphoreType.DMA((layers, 4)),
            pltpu.SemaphoreType.DMA((7,)), pltpu.SemaphoreType.DMA((7,)),
        ],
        compiler_params=pltpu.CompilerParams(collective_id=1, has_side_effects=True, vmem_limit_bytes=62 * 2**20),
        cost_estimate=cost(10**10, 10**8),
        name="forward",
    )(flag, tokens, cotangent, *biases, *gains, input_own, output_own, expand_weight, shrink_own)
    out_low, cotangent, flag = results[:3]
    chips = wide // 2
    further = (chips // 8).bit_length() - 1
    tall = lambda size: -(-size // 128) * 128
    out_shapes, buffer_scratch, theirs_scratch = [], [], []
    for size, columns in ((units, depth), (depth, units), (width, depth), (depth // 2, 3 * width), (depth // 2, 3 * width)):
        out_shapes.append(shaped(BF16, layers, 2, tall(size), columns))
        theirs_scratch.append(pltpu.VMEM((2, size, columns), BF16))
        piece = tall(size) // 8
        buffer_scratch += [
            pltpu.VMEM((2, tall(size), columns), BF16), pltpu.VMEM((2, size, columns), BF16), pltpu.VMEM((size, columns), BF16),
            pltpu.VMEM((4 * piece, columns), BF16), pltpu.VMEM((3, piece, columns), BF16),
            pltpu.VMEM((further, piece, columns) if further else (1, 16, 128), BF16),
        ]
    small_rows = 8 * layers
    steps = chips.bit_length() - 1
    small_scratch = pltpu.VMEM((small_rows, depth), F32)
    grad_sem = pltpu.SemaphoreType.DMA((KINDS * layers, 12 + further))
    results = pl.pallas_call(
        functools.partial(all_backward, layers, chips),
        out_shape=[low_shape, low_shape, shaped(F32, 2, small_rows, depth)] + out_shapes,
        in_specs=[VM] * 9 + [AN] * len(kept_shapes),
        out_specs=[VM] * (3 + KINDS),
        scratch_shapes=state_scratch + [
            pltpu.VMEM((rows, depth), F32), pltpu.VMEM((depth, rows), BF16), pltpu.VMEM((rows, depth), F32),
            pltpu.VMEM(query_shape.shape, BF16), pltpu.VMEM(stat_shape.shape, F32), pltpu.VMEM(query_shape.shape, BF16),
            pltpu.VMEM(pair_shape.shape, F32), pltpu.VMEM(pair_shape.shape, BF16), pltpu.VMEM((rows, depth), BF16), pltpu.VMEM((rows, depth), BF16),
        ] + [pltpu.VMEM(pair_shape.shape, BF16)] * layers + theirs_scratch + buffer_scratch * layers + [
            pltpu.VMEM((4, small_rows, depth), F32), pltpu.VMEM((2, small_rows, depth), F32), small_scratch, small_scratch,
            pltpu.VMEM((steps, small_rows, depth), F32), pltpu.VMEM((steps, small_rows, depth), F32),
            pltpu.SemaphoreType.DMA((STATES,)),
            pltpu.SemaphoreType.DMA((layers, 4)), pltpu.SemaphoreType.DMA((layers, 4)),
            grad_sem, grad_sem,
            pltpu.SemaphoreType.DMA((5,)), pltpu.SemaphoreType.DMA((5,)),
            pltpu.SemaphoreType.DMA((steps,)), pltpu.SemaphoreType.DMA((steps,)),
        ],
        compiler_params=pltpu.CompilerParams(collective_id=0, has_side_effects=True, vmem_limit_bytes=67043328),
        cost_estimate=cost(10**10, 10**8),
        name="backward",
    )(flag, cotangent, out_low, *gains, *results[3:])
    out_rows, in_rows, small = results[:3]
    whole = lambda *dims: pl.BlockSpec(dims, lambda layer, part: (0,) * len(dims))
    piece = lambda shape: pl.BlockSpec((1, 1) + shape.shape[2:], lambda layer, part: (layer, part, 0, 0))
    strip = pl.BlockSpec((rows // (2 * layers), depth), lambda layer, part: (2 * layer + part, 0))
    upright = lambda size: pl.BlockSpec((1, size, depth), lambda layer, part: (layer, part, 0))
    vector_shape = shaped(F32, layers, depth)
    outs = pl.pallas_call(
        functools.partial(assemble_kernel, layers),
        grid=(layers, 2),
        out_shape=[
            shaped(F32, layers, 2 * units, depth), shaped(F32, layers, depth, 2 * units), shaped(F32, layers, 2 * width, depth),
            shaped(F32, layers, 3, depth, 2 * width), row_shape, row_shape,
        ] + [vector_shape] * 6 + [shaped(F32, layers, 2 * units), shaped(F32, layers, 2 * width), shaped(F32, layers, 2 * width)],
        in_specs=[piece(shape) for shape in out_shapes] + [whole(2, small_rows, depth), strip, strip],
        out_specs=[
            upright(units), pl.BlockSpec((1, depth, units), lambda layer, part: (layer, 0, part)), upright(width),
            pl.BlockSpec((1, 3, depth, width), lambda layer, part: (layer, 0, 0, part)), strip, strip,
        ] + [whole(layers, depth)] * 6 + [whole(layers, 2 * units), whole(layers, 2 * width), whole(layers, 2 * width)],
        compiler_params=pltpu.CompilerParams(vmem_limit_bytes=40 * 2**20),
        cost_estimate=cost(10**6, 2 * 10**7),
        name="assemble",
    )(*results[3:], small, out_rows, in_rows)
    shrink_grad, expand_grad, output_grad, input_grad, layer_output, input_rows = outs[:6]
    second_shift_grad, second_gain_grad, shrink_bias_grad, first_shift_grad, first_gain_grad, output_bias_grad = outs[6:12]
    expand_bias_grad, query_bias_grad, value_bias_grad = outs[12:]
    return (
        layer_output,
        input_rows,
        input_grad.transpose(0, 2, 1, 3),
        query_bias_grad,
        value_bias_grad,
        output_grad,
        output_bias_grad,
        first_gain_grad,
        first_shift_grad,
        expand_grad,
        expand_bias_grad,
        shrink_grad,
        shrink_bias_grad,
        second_gain_grad,
        second_shift_grad,
    )


def solution(mesh):
    split = P(AXES, None)
    in_specs = (
        split, P(None, None, None, "narrow"), P(None, "narrow"), P(None, "narrow"), P(None, "narrow", None), P(), P(), P(),
        P(None, None, "narrow"), P(None, "narrow"), P(None, "narrow", None), P(), P(), P(), P("wide"), P("wide"), split,
    )
    out_specs = (
        split, split, P(None, None, None, "narrow"), P(None, "narrow"), P(None, "narrow"), P(None, "narrow", None), P(), P(), P(),
        P(None, None, "narrow"), P(None, "narrow"), P(None, "narrow", None), P(), P(), P(),
    )
    return jax.shard_map(local, mesh=mesh, in_specs=in_specs, out_specs=out_specs, check_vma=False)
```

```python
import functools
import itertools

import jax
import jax.numpy as jnp
from jax import lax
from jax.experimental import pallas as pl
from jax.experimental.pallas import tpu as pltpu
from jax.sharding import PartitionSpec as P

DH = 64
EPSILON = 1e-12
MASKED = -1e9
AXES = ("wide", "narrow")
F32 = jnp.float32
BF16 = jnp.bfloat16
STATES = 17
KINDS = 5


def dot(a, b):
    return lax.dot_general(a, b, (((1,), (0,)), ((), ())), preferred_element_type=F32)


def dot_rt(a, b):
    return lax.dot_general(a, b, (((1,), (1,)), ((), ())), preferred_element_type=F32)


def dot_lt(a, b):
    return lax.dot_general(a, b, (((0,), (0,)), ((), ())), preferred_element_type=F32)


def lane_halves(shape):
    lane = lax.broadcasted_iota(jnp.int32, shape, len(shape) - 1)
    return lane < DH


def normalise(x):
    centre = x - jnp.mean(x, -1, keepdims=True)
    scale = lax.rsqrt(jnp.mean(centre * centre, -1, keepdims=True) + EPSILON)
    return centre * scale, scale


def gelu_parts(a):
    square = jnp.exp(-0.5 * a * a)
    size = jnp.abs(a)
    t = 1.0 / (1.0 + (0.3275911 * 0.7071067811865476) * size)
    poly = t * (
        0.127414796
        + t * (-0.142248368 + t * (0.7107068705 + t * (-0.7265760135 + t * 0.5307027145)))
    )
    tail = poly * square
    phi = jnp.where(a >= 0, 1.0 - tail, tail)
    return a * phi, phi + a * square * 0.3989422804014327


class Links:
    def __init__(self):
        self.wide, self.narrow = lax.axis_index("wide"), lax.axis_index("narrow")
        self.core = lax.rem(self.wide, 2)
        self.chip = self.wide // 2
        self.bit = lax.rem(self.chip, 2)
        other_core, other_narrow = self.wide + 1 - 2 * self.core, 1 - self.narrow
        self.beside = (other_core, self.narrow)
        self.across = (self.wide, other_narrow)
        self.next_bit = lax.rem(self.chip // 2, 2)
        self.along = (self.wide + 2 * (1 - 2 * self.bit), self.narrow)
        self.along_next = (self.wide + 4 * (1 - 2 * self.next_bit), self.narrow)
        self.opposite = (other_core, other_narrow)
        self.moved = self.core + self.narrow == 1

    def plane(self, chips):
        assert chips % 8 == 0
        self.line = lax.rem(self.chip // 2, 4)
        self.line_peers = []
        for offset in range(1, 4):
            there = lax.rem(self.line + offset, 4)
            self.line_peers.append((self.wide + 4 * (there - self.line), self.narrow))
        self.bits = []
        for bit in range(chips.bit_length() - 1):
            side = lax.rem(self.chip // 2**bit, 2)
            self.bits.append((self.wide + 2 ** (bit + 1) * (1 - 2 * side), self.narrow))
        self.further = self.bits[3:]

    def greet(self, devices):
        barrier = pltpu.get_barrier_semaphore()
        for device in devices:
            pl.semaphore_signal(barrier, inc=1, device_id=device, device_id_type=pl.DeviceIdType.MESH)
        pl.semaphore_wait(barrier, len(devices))


def remote(source, target, sems, at, device):
    return pltpu.make_async_remote_copy(
        source, target, sems[0].at[at], sems[1].at[at], device_id=device, device_id_type=pl.DeviceIdType.MESH
    )


class Weight:
    def __init__(self, links, number, own, parts, buffer, local_sem, sems):
        self.links, self.number, self.own, self.parts = links, number, own, parts
        self.buffer, self.local_sem, self.sems = buffer, local_sem, sems
        self.size = buffer.shape[1] // 4
        self.columns = buffer.shape[2] // parts

    def rows(self, flip, flip_next):
        bit = self.links.bit + flip * (1 - 2 * self.links.bit)
        next_bit = self.links.next_bit + flip_next * (1 - 2 * self.links.next_bit)
        return pl.ds(pl.multiple_of((2 * next_bit + bit) * self.size, 16), self.size)

    def local_copies(self):
        core = self.links.core
        copies = []
        for slot, part in ((0, core), (2, 1 - core)):
            for kind in range(self.parts):
                target = self.buffer.at[slot, :, pl.ds(kind * self.columns, self.columns)]
                copies.append(pltpu.make_async_copy(self.own(part, slice(None), kind), target, self.local_sem.at[self.number, len(copies)]))
        return copies

    def first_hops(self):
        rows = self.rows(0, 0)
        return [
            remote(
                self.own(self.links.core, rows, kind), self.buffer.at[1, rows, pl.ds(kind * self.columns, self.columns)],
                self.sems, (self.number, kind), self.links.across,
            )
            for kind in range(self.parts)
        ]

    def hop(self, kind):
        links = self.links
        at = (self.number, 2 + kind)
        device = links.along if kind == 1 or (kind == 3 and self.number % 2) else links.along_next
        if kind < 3:
            rows = self.rows(0, 0)
        elif kind == 3:
            rows = self.rows(0, 1) if self.number % 2 else self.rows(1, 0)
        else:
            rows = self.rows(kind % 2, (kind - 4) // 2)
        if kind < 4:
            return remote(self.buffer.at[1, rows], self.buffer.at[1, rows], self.sems, at, device)
        return remote(self.buffer.at[1, rows], self.buffer.at[3, rows], self.sems, at, links.beside)

    def start(self):
        for copy in self.first_hops():
            copy.start()

    def start_local(self):
        for copy in self.local_copies():
            copy.start()

    def relay(self):
        for copy in self.first_hops():
            copy.wait_recv()
        for kind in (1, 2, 4):
            self.hop(kind).start()

    def relay_again(self):
        self.hop(1).wait_recv()
        self.hop(2).wait_recv()
        for kind in (3, 5, 6):
            self.hop(kind).start()

    def relay_last(self):
        self.hop(3).wait_recv()
        self.hop(7).start()

    def wait_own(self):
        for copy in self.local_copies():
            copy.wait()

    def wait_fetched(self):
        for kind in range(4, 8):
            self.hop(kind).wait_recv()

    def wait_sent(self):
        for copy in self.first_hops() + [self.hop(kind) for kind in range(1, 8)]:
            copy.wait_send()


def ordered(step):
    return lax.rem(2 * step, 4) + step // 2


def at_step(step, hooks):
    for number, hook in enumerate(hooks):
        if hook:

            @pl.when(step == number)
            def _(hook=hook):
                for action in hook:
                    action()


def all_forward(layers, *refs):
    (flag, tokens, cotangent, query_bias, value_bias, expand_bias), refs = refs[:6], refs[6:]
    gains, refs = refs[:6], refs[6:]
    (wi_own, wo_own, we_own, ws_own), refs = refs[:4], refs[4:]
    (rows_out, cotangent_out, flag_out), refs = refs[:3], refs[3:]
    kept = [refs[STATES * layer : STATES * (layer + 1)] for layer in range(layers)]
    refs = refs[STATES * layers :]
    states = [refs[STATES * layer : STATES * (layer + 1)] for layer in range(layers)]
    refs = refs[STATES * layers :]
    tokens_in = states[0][16]
    biases = (query_bias, value_bias, expand_bias)
    biases_in, refs = refs[:3], refs[3:]
    (save_sem, pass_sem, rows_low, cotangent_in, flag_in, acc, local_sem, send_sem, recv_sem, kv_send, kv_recv, misc_send, misc_recv) = refs
    links = Links()
    core = links.core
    sems = (send_sem, recv_sem)
    units = ws_own.shape[2]
    width = wo_own.shape[2]
    rows = tokens.shape[0]
    weights = []
    for layer in range(layers):
        buffers = states[layer][:4]

        def lanes(part, count):
            return pl.ds(pl.multiple_of(part * count, 128), count)

        owns = [
            lambda part, rows, kind, layer=layer: wi_own.at[layer, kind, rows, lanes(part, width)],
            lambda part, rows, kind, layer=layer: wo_own.at[layer, part, rows],
            lambda part, rows, kind, layer=layer: we_own.at[layer, rows, lanes(part, units)],
            lambda part, rows, kind, layer=layer: ws_own.at[layer, part, rows],
        ]
        weights.append([
            Weight(links, 4 * layer + number, owns[number], 3 if number == 0 else 1, buffers[number], local_sem, sems)
            for number in range(4)
        ])
    every = [weight for group in weights for weight in group]
    for weight in every[:4]:
        weight.start_local()
    links.greet([links.across, links.along, links.along_next, links.beside, links.opposite])
    misc = (misc_send, misc_recv)
    swap_tokens = remote(tokens, tokens_in, misc, 0, links.opposite)
    swap_flag = remote(flag, flag_in, misc, 1, links.opposite)
    swap_cotangent = remote(cotangent, cotangent_in, misc, 2, links.opposite)
    copy_biases = [remote(biases[number], biases_in[number], misc, 4 + number, links.across) for number in range(3)]

    for copy in copy_biases:
        copy.start()
    every[0].start()
    every[1].start()

    @pl.when(links.moved)
    def _():
        swap_flag.start()
        swap_tokens.start()
        for weight in every[2:]:
            weight.start()
        swap_cotangent.start()

    @pl.when(jnp.logical_not(links.moved))
    def _():
        tokens_in[...] = tokens[...]
        flag_in[...] = flag[...]

    def start_rest():
        @pl.when(jnp.logical_not(links.moved))
        def _():
            for weight in every[2:]:
                weight.start()

        for weight in every[4:]:
            weight.start_local()

    def bias(number, layer, index):
        size = biases[number].shape[1] // 2
        part = core + (index // 2) * (1 - 2 * core)
        place = pl.ds(pl.multiple_of(part * size, 128), size)
        return jnp.where(
            lax.rem(index, 2) == 0, biases[number][layer : layer + 1, place], biases_in[number][layer : layer + 1, place]
        )

    for copy in copy_biases:
        copy.wait_recv()
    every[0].relay()
    every[1].relay()
    every[0].relay_again()
    every[1].relay_again()

    @pl.when(links.moved)
    def _():
        swap_flag.wait_recv()
        swap_tokens.wait_recv()

    shift = jnp.where(flag_in[0:1, 0:1] < 0.5, 0.0, MASKED)
    acc[...] = tokens_in[...].astype(F32)
    halves = lane_halves((rows, width))

    def save_copy(layer, number):
        return pltpu.make_async_copy(states[layer][number], kept[layer][number], save_sem.at[layer, number])

    def save(layer, *numbers):
        for number in numbers:
            save_copy(layer, number).start()

    pass_rows = pltpu.make_async_copy(rows_low, rows_out, pass_sem.at[0])
    pass_flag = pltpu.make_async_copy(flag_in, flag_out, pass_sem.at[1])
    pass_far = pltpu.make_async_copy(cotangent_in, cotangent_out, pass_sem.at[2])
    pass_near = pltpu.make_async_copy(cotangent, cotangent_out, pass_sem.at[2])
    pass_flag.start()

    @pl.when(jnp.logical_not(links.moved))
    def _():
        pass_near.start()

    def pass_cotangent():
        @pl.when(links.moved)
        def _():
            swap_cotangent.wait_recv()
            pass_far.start()

    for layer in range(layers):
        (wi, wo, we, ws, query_ref, pair_ref, remote_ref, mixed_ref, total_ref, normed_ref, first_ref, first_scale, active_ref, slope_ref, second_ref, second_scale, low_ref) = states[layer]
        vector = lambda at: gains[at][layer : layer + 1]
        wi_go, wo_go, we_go, ws_go = weights[layer]
        later = weights[layer + 1] if layer + 1 < layers else None
        if layer > 0:
            low_ref[...] = acc[...].astype(BF16)

        def exchange(index):
            return remote(pair_ref.at[index], remote_ref.at[index], (kv_send, kv_recv), (layer, index), links.beside)

        def project(step, carry):
            index = ordered(step)
            triple = dot(low_ref[...], wi[index])
            query = (triple[:, :width] + bias(0, layer, index)).astype(BF16)
            query_ref[index] = query * BF16(DH ** (-0.5))
            pair_ref[index, :, :width] = triple[:, width : 2 * width].astype(BF16)
            pair_ref[index, :, width:] = (triple[:, 2 * width :] + bias(1, layer, index)).astype(BF16)
            exchange(index).start()
            return carry

        def project_rest():
            lax.fori_loop(2, 4, project, 0)

        wi_go.wait_own()
        if layer == 0:
            start_rest()
        lax.fori_loop(0, 2, project, 0)
        after_pair = [[], [], [], []]
        if layer == 0:
            before_pair = [
                [],
                [wi_go.relay_last, wo_go.relay_last, we_go.relay],
                [ws_go.relay, wi_go.wait_fetched, wo_go.wait_fetched, project_rest, we_go.relay_again],
                [ws_go.relay_again],
            ]
            before_feed = [we_go.relay_last]
            before_quarter = [[], [ws_go.relay_last], [we_go.wait_fetched, ws_go.wait_fetched], []]
            if later:
                before_feed += [later[0].relay, later[1].relay]
                before_quarter[1] += [later[2].relay]
                before_quarter[2] += [later[0].relay_again, later[1].relay_again]
                before_quarter[3] += [later[3].relay]
        else:
            before_pair = [
                [wi_go.relay_last, wo_go.relay_last, we_go.relay_again],
                [ws_go.relay_again, we_go.relay_last],
                [ws_go.relay_last, wi_go.wait_fetched, project_rest, wo_go.wait_fetched],
                [],
            ]
            before_feed = []
            before_quarter = [[], [], [we_go.wait_fetched, ws_go.wait_fetched], []]
            if later:
                before_feed += [later[0].relay, later[1].relay]
                before_quarter[1] += [later[2].relay]
                before_quarter[2] += [later[0].relay_again, later[1].relay_again]
                before_quarter[3] += [later[3].relay]
        before_quarter[3] += [functools.partial(save, layer, 2, 3)]
        if not later:
            before_quarter[3] += [pass_cotangent]
        acc[...] += vector(0)

        def one_pair(step, carry):
            at_step(step, before_pair)
            index = ordered(step)
            there = lax.rem(index + 2, 4)
            exchange(there).wait_recv()
            at_step(step, after_pair)
            queries = query_ref[index]
            key_here, value_here = pair_ref[index, :, :width], pair_ref[index, :, width:]
            key_there, value_there = remote_ref[there, :, :width], remote_ref[there, :, width:]
            mixed, total = [], []
            for part in range(2):
                mask = halves if part == 0 else jnp.logical_not(halves)
                masked = jnp.where(mask, queries, BF16(0))
                here = dot_rt(masked, key_here)
                away = dot_rt(masked, key_there)
                peak = jnp.maximum(jnp.max(here, -1, keepdims=True), jnp.max(away, -1, keepdims=True) + shift)
                here = jnp.exp(here - peak)
                away = jnp.exp(away - (peak - shift))
                weight = jnp.sum(here, -1, keepdims=True) + jnp.sum(away, -1, keepdims=True)
                both = dot(here.astype(BF16), value_here) + dot(away.astype(BF16), value_there)
                mixed.append(both * (1.0 / weight))
                total.append(jnp.broadcast_to(peak + jnp.log(weight), (rows, width)))
            mixed_low = jnp.where(halves, mixed[0], mixed[1]).astype(BF16)
            mixed_ref[index] = mixed_low
            totals = jnp.where(halves, total[0], total[1]).T
            total_ref[index] = jnp.concatenate([totals[0:8], totals[DH : DH + 8]], 0)
            acc[...] += dot(mixed_low, wo[index])
            return carry

        wo_go.wait_own()
        lax.fori_loop(0, 4, one_pair, 0)
        for action in before_feed:
            action()
        save(layer, 16, 0, 4, 5, 6, 1, 7, 8)
        first, scale = normalise(acc[...])
        first_ref[...] = first
        first_scale[...] = scale
        normed = first * vector(1) + vector(2)
        normed_ref[...] = normed.astype(BF16)
        acc[...] = normed + vector(3)
        save(layer, 9, 10, 11)
        we_go.wait_own()
        ws_go.wait_own()

        def one_quarter(step, carry):
            at_step(step, before_quarter)
            index = ordered(step)
            active, slope = gelu_parts(dot(normed_ref[...], we[index]) + bias(2, layer, index))
            active_low = active.astype(BF16)
            active_ref[index] = active_low
            slope_ref[index] = slope.astype(BF16)
            acc[...] += dot(active_low, ws[index])
            return carry

        lax.fori_loop(0, 4, one_quarter, 0)
        save(layer, 12, 13)
        second, scale = normalise(acc[...])
        second_ref[...] = second
        second_scale[...] = scale
        save(layer, 14, 15)
        acc[...] = second * vector(4) + vector(5)

    rows_low[...] = acc[...].astype(BF16)
    pass_rows.start()

    @pl.when(links.moved)
    def _():
        pass_far.wait()
        for copy in (swap_tokens, swap_flag, swap_cotangent):
            copy.wait_send()

    for copy in copy_biases:
        copy.wait_send()
    for weight in every:
        weight.wait_sent()
    for layer in range(layers):
        for number in range(STATES):
            save_copy(layer, number).wait()
    pass_rows.wait()
    pass_flag.wait()

    @pl.when(jnp.logical_not(links.moved))
    def _():
        pass_near.wait()

    for layer in range(layers):
        pair_ref, remote_ref = states[layer][5:7]
        for index in range(4):
            remote(pair_ref.at[index], remote_ref.at[index], (kv_send, kv_recv), (layer, index), links.beside).wait_send()


def column_sum(x):
    return jnp.sum(x, 0, keepdims=True)


def norm_backward(grad, normed, scale, gain):
    scaled = grad * gain
    return (
        scaled - jnp.mean(scaled, -1, keepdims=True) - normed * jnp.mean(scaled * normed, -1, keepdims=True)
    ) * scale


def backwards(step):
    return 3 - ordered(step)


def late_sum(layer, kind):
    return False


class Gradient:
    def __init__(self, links, number, late, mine, theirs, core_in, narrow_in, pair_in, line_in, further_in, out, sems):
        self.links, self.number, self.mine, self.theirs, self.core_in = links, number, mine, theirs, core_in
        self.narrow_in, self.pair_in, self.line_in, self.further_in, self.out, self.sems = narrow_in, pair_in, line_in, further_in, out, sems
        self.size = core_in.shape[1]
        self.piece = mine.shape[1] // 8
        self.late = late
        self.kept = (0, 1) if late else (0,)

    def copy(self, source, target, at, device):
        return remote(source, target, self.sems, (self.number, at), device)

    def part_copy(self, part):
        return self.copy(self.theirs.at[part], self.core_in.at[part], part, self.links.beside)

    def narrow_copy(self):
        rows = self.piece_rows(0) if self.late else pl.ds(0, self.size)
        return self.copy(self.mine.at[1, rows], self.narrow_in, 2, self.links.across)

    def share_copy(self):
        place = self.out.at[self.links.core]
        return self.copy(place, place, 3, self.links.beside)

    def half_rows(self, other):
        bit = self.links.bit + other * (1 - 2 * self.links.bit)
        return pl.ds(pl.multiple_of(bit * 4 * self.piece, 16), 4 * self.piece)

    def piece_rows(self, offset):
        index = 4 * self.links.bit + lax.rem(self.links.line + offset, 4)
        return pl.ds(pl.multiple_of(index * self.piece, 16), self.piece)

    def pair_copy(self, part):
        return self.copy(self.mine.at[part, self.half_rows(1)], self.pair_in.at[part], 12 + part, self.links.along)

    def line_copy(self, part, offset):
        device = self.links.line_peers[offset - 1]
        source = self.mine.at[part, self.piece_rows(offset)]
        return self.copy(source, self.line_in.at[part, offset - 1], 13 + 3 * part + offset, device)

    def line_back(self, offset):
        place = self.out.at[self.links.core, self.piece_rows(0)]
        return self.copy(place, place, 7 + offset, self.links.line_peers[offset - 1])

    def pair_back(self):
        place = self.out.at[self.links.core, self.half_rows(0)]
        return self.copy(place, place, 11, self.links.along)

    def further_copy(self, number):
        place = self.mine.at[0, self.piece_rows(0)]
        return self.copy(place, self.further_in.at[number], 20 + number, self.links.further[number])

    def send(self, part):
        self.part_copy(part).start()

    def middle(self):
        if not self.late:
            self.part_copy(1).wait_recv()
            self.mine[1, 0 : self.size] = add(self.mine[1, 0 : self.size], self.core_in[1])
            self.narrow_copy().start()

    def settle(self):
        if self.late:
            for part in range(2):
                self.part_copy(part).wait_recv()
                self.mine[part, 0 : self.size] = add(self.mine[part, 0 : self.size], self.core_in[part])
                self.pair_copy(part).start()
        else:
            self.part_copy(0).wait_recv()
            self.narrow_copy().wait_recv()
            self.mine[0, 0 : self.size] = add(self.mine[0, 0 : self.size], self.core_in[0], self.narrow_in[...])
            self.pair_copy(0).start()

    def cross(self):
        rows = self.half_rows(0)
        for part in self.kept:
            self.pair_copy(part).wait_recv()
            self.mine[part, rows] = add(self.mine[part, rows], self.pair_in[part])
            for offset in range(1, 4):
                self.line_copy(part, offset).start()

    def spread(self):
        rows = self.piece_rows(0)
        for part in reversed(self.kept):
            for offset in range(1, 4):
                self.line_copy(part, offset).wait_recv()
            total = add(self.mine[part, rows], self.line_in[part, 0], self.line_in[part, 1], self.line_in[part, 2])
            if self.late:
                self.mine[part, rows] = total
                if part == 1:
                    self.narrow_copy().start()
        if not self.late:
            self.spread_total(total)

    def fold(self):
        self.narrow_copy().wait_recv()
        self.spread_total(add(self.mine[0, self.piece_rows(0)], self.narrow_in[...]))

    def spread_total(self, total):
        rows = self.piece_rows(0)
        for number in range(len(self.links.further)):
            self.mine[0, rows] = total
            copy = self.further_copy(number)
            copy.start()
            copy.wait()
            total = add(total, self.further_in[number])
        self.out[self.links.core, rows] = total
        for offset in range(1, 4):
            self.line_back(offset).start()

    def widen(self):
        for offset in range(1, 4):
            self.line_back(offset).wait_recv()
        self.pair_back().start()

    def share(self):
        self.pair_back().wait_recv()
        self.share_copy().start()

    def free_theirs(self):
        for part in range(2):
            self.part_copy(part).wait_send()

    def wait_all(self, theirs_waited):
        self.share_copy().wait_recv()
        if not theirs_waited:
            self.free_theirs()
        copies = [self.share_copy(), self.narrow_copy(), self.pair_back()]
        for offset in range(1, 4):
            copies.append(self.line_back(offset))
            copies += [self.line_copy(part, offset) for part in self.kept]
        copies += [self.pair_copy(part) for part in self.kept]
        for copy in copies:
            copy.wait_send()


def add(*terms):
    total = terms[0].astype(F32)
    for term in terms[1:]:
        total = total + term.astype(F32)
    return total.astype(BF16)


def all_backward(layers, chips, *refs):
    passed, refs = refs[:3], refs[3:]
    gains, refs = refs[:6], refs[6:]
    kept = [refs[STATES * layer : STATES * (layer + 1)] for layer in range(layers)]
    refs = refs[STATES * layers :]
    (out_rows, rows_ref, small_out), refs = refs[:3], refs[3:]
    outs = [[ref.at[layer] for ref in refs[:KINDS]] for layer in range(layers)]
    refs = refs[KINDS:]
    state, refs = refs[:STATES], refs[STATES:]
    (acc, turned, summed_ref, mixed_grad_ref, inner_ref, query_grad_ref, here_ref, away_ref, rows_low, rows_back), refs = refs[:10], refs[10:]
    away_in, refs = refs[:layers], refs[layers:]
    theirs, refs = refs[:KINDS], refs[KINDS:]
    buffers = []
    for layer in range(layers):
        buffers.append([refs[6 * kind : 6 * kind + 6] for kind in range(KINDS)])
        refs = refs[6 * KINDS :]
    (small, core_small, mid_small, row_small, sum_small, step_small), refs = refs[:6], refs[6:]
    (out_low, cotangent, flag, pass_sem, load_sem, away_send, away_recv, grad_send, grad_recv, misc_send, misc_recv, step_send, step_recv) = refs
    (wi, wo, we, ws, query, pair, remote_pair, mixed, total_ref, normed, first, first_scale, active, slope, second, second_scale, hidden_low) = state
    links = Links()
    links.plane(chips)
    core = links.core
    steps = chips.bit_length() - 1
    bits = links.bits

    def load_copy(layer, number):
        return pltpu.make_async_copy(kept[layer][number], state[number], load_sem.at[number])

    def load(layer, numbers):
        for number in numbers:
            load_copy(layer, number).start()

    def loaded(layer, *numbers):
        for number in numbers:
            load_copy(layer, number).wait()

    block_group = (14, 15, 3, 13, 12, 2, 9, 10, 11, 1, 7)
    pair_group = (4, 5, 6, 8)
    input_group = (16, 0)
    passes = [pltpu.make_async_copy(passed[number], (out_low, cotangent, flag)[number], pass_sem.at[number]) for number in range(3)]
    passes[1].start()
    passes[2].start()
    load(layers - 1, block_group[:7])
    links.greet([links.across, links.beside, links.opposite] + links.line_peers + bits)
    misc = (misc_send, misc_recv)
    gradients = []
    for layer in range(layers):
        group = []
        for kind in range(KINDS):
            mine, core_in, narrow_in, pair_in, line_in, further_in = buffers[layer][kind]
            group.append(Gradient(
                links, KINDS * layer + kind, late_sum(layer, kind), mine, theirs[kind], core_in, narrow_in, pair_in, line_in, further_in,
                outs[layer][kind], (grad_send, grad_recv),
            ))
        gradients.append(group)
    rows, width = mixed.shape[1], mixed.shape[2]
    units, depth = ws.shape[1], ws.shape[2]
    halves = lane_halves((rows, width))
    passes[2].wait()
    shift = jnp.where(flag[0:1, 0:1] < 0.5, 0.0, MASKED)
    small[...] = jnp.zeros(small.shape, F32)
    half = lax.broadcasted_iota(jnp.int32, (16, width), 1) // DH
    which = lax.broadcasted_iota(jnp.int32, (16, width), 0) // 8
    selector = (half == which).astype(F32)
    passes[1].wait()
    acc[...] = cotangent[...].astype(F32)
    passes[0].start()
    load(layers - 1, block_group[7:] + pair_group + input_group)
    swap_rows = remote(rows_back, rows_ref, misc, 0, links.opposite)
    swap_out = remote(out_low, out_rows, misc, 4, links.opposite)

    def start_out():
        passes[0].wait()

        @pl.when(links.moved)
        def _():
            swap_out.start()

        @pl.when(jnp.logical_not(links.moved))
        def _():
            out_rows[...] = out_low[...]

    for layer in reversed(range(layers)):
        shrink, expand, output, input_one, input_two = gradients[layer]
        before = gradients[layer + 1] if layer + 1 < layers else None
        vector = lambda at: gains[at][layer : layer + 1]

        def put(gradient, index, at, value):
            @pl.when(index < 2)
            def _():
                gradient.mine[index, at : at + value.shape[0]] = value

            @pl.when(index >= 2)
            def _():
                gradient.theirs[index - 2, at : at + value.shape[0]] = value

        def act(name, *which):
            return [getattr(gradient, name) for gradient in which]

        loaded(layer, 14, 15)
        incoming = acc[...]
        widened = norm_backward(incoming, second[...], second_scale[...], vector(4))
        sums = [column_sum(incoming), column_sum(incoming * second[...]), column_sum(widened)]
        acc[...] = widened
        rows_low[...] = widened.astype(BF16)
        loaded(layer, 9)
        turned[...] = normed[...].T
        loaded(layer, 3, 13, 12, 2)
        if before:
            for gradient in before:
                gradient.free_theirs()
        partly = lambda part, *which: [functools.partial(gradient.send, part) for gradient in which]
        block_hooks = [[], partly(1, shrink, expand), [], partly(0, shrink, expand) + act("middle", shrink, expand)]
        if before:
            block_hooks[0] += act("cross", before[0])
            block_hooks[2] += act("settle", before[1])

        def one_quarter(step, carry):
            at_step(step, block_hooks)
            index = backwards(step)
            branch = rows_low[...]
            inner = (dot_rt(branch, ws[index]) * slope[index].astype(F32)).astype(BF16)
            put(shrink, index, 0, dot_lt(active[index], branch).astype(BF16))
            put(expand, index, 0, dot(turned[...], inner).astype(BF16))
            small[index, 8 * layer + 6 : 8 * layer + 7, 0:units] = column_sum(inner.astype(F32))
            acc[...] += dot_rt(inner, we[index])
            return carry

        lax.fori_loop(0, 4, one_quarter, 0)
        loaded(layer, 10, 11, 1, 7)
        outgoing = acc[...]
        summed = norm_backward(outgoing, first[...], first_scale[...], vector(1))
        sums += [column_sum(outgoing), column_sum(outgoing * first[...]), column_sum(summed)]
        for number, value in enumerate(sums):
            for quarter in range(4):
                small[quarter, 8 * layer + number : 8 * layer + number + 1] = value
        summed_ref[...] = summed
        rows_low[...] = summed.astype(BF16)
        if before:
            before[0].spread()
            before[2].settle()
        if shrink.late:
            shrink.settle()

        def one_output(step, carry):
            index = backwards(step)
            mixed_grad = dot_rt(rows_low[...], wo[index]).astype(BF16)
            mixed_grad_ref[index] = mixed_grad
            put(output, index, 0, dot_lt(mixed[index], rows_low[...]).astype(BF16))
            product = mixed_grad.astype(F32) * mixed[index].astype(F32)
            inner_ref[index] = lax.dot_general(
                selector, product, (((1,), (1,)), ((), ())), precision=lax.Precision.HIGHEST, preferred_element_type=F32
            )
            return carry

        lax.fori_loop(0, 4, one_output, 0)
        output.send(0)
        output.send(1)
        if layer > 0:
            load(layer - 1, block_group)
        loaded(layer, *pair_group)
        pair_hooks = [[], [output.middle], [], []]
        if before:
            pair_hooks[0] += act("settle", before[3], before[4]) + act("cross", before[1])
            pair_hooks[1] += act("cross", before[2])
            pair_hooks[2] += act("widen", before[0]) + act("cross", before[3], before[4])
            pair_hooks[3] += act("spread", before[1], before[2])
        else:
            pair_hooks[3] += act("settle", shrink)

        def away_copy(there):
            return remote(away_ref.at[there], away_in[layer].at[there], (away_send, away_recv), (layer, there), links.beside)

        if before:
            for there in range(4):
                remote(away_ref.at[there], away_in[layer + 1].at[there], (away_send, away_recv), (layer + 1, there), links.beside).wait_send()

        def one_pair(step, carry):
            at_step(step, pair_hooks)
            there = backwards(step)
            index = lax.rem(there + 2, 4)
            queries, grads = query[index], mixed_grad_ref[index]
            query_turned = None
            for side in range(2):
                source, place = (pair, index) if side == 0 else (remote_pair, there)
                keys, values = source[place, :, :width], source[place, :, width:]
                key_grad = value_grad = None
                for part in range(2):
                    mask = halves if part == 0 else jnp.logical_not(halves)
                    masked_query = jnp.where(mask, queries, BF16(0))
                    masked_grad = jnp.where(mask, grads, BF16(0))
                    masked_key = jnp.where(mask, keys, BF16(0))
                    level = total_ref[index, 8 * part : 8 * part + 1]
                    if side == 1:
                        level = level - shift
                    weights = jnp.exp(dot_rt(keys, masked_query) - level)
                    update = dot(weights.astype(BF16), masked_grad)
                    value_grad = update if value_grad is None else value_grad + update
                    slopes = dot_rt(values, masked_grad) - inner_ref[index, 8 * part : 8 * part + 1]
                    slopes = (weights * slopes).astype(BF16)
                    update = dot(slopes, masked_query)
                    key_grad = update if key_grad is None else key_grad + update
                    update = dot_lt(masked_key, slopes)
                    query_turned = update if query_turned is None else query_turned + update
                if side == 0:
                    here_ref[index, :, :width] = key_grad
                    here_ref[index, :, width:] = value_grad
                else:
                    away_ref[there, :, :width] = key_grad.astype(BF16)
                    away_ref[there, :, width:] = value_grad.astype(BF16)
            away_copy(there).start()
            query_grad_ref[index] = (query_turned * DH ** (-0.5)).T.astype(BF16)
            return carry

        lax.fori_loop(0, 4, one_pair, 0)
        if layer > 0:
            load(layer - 1, pair_group)
        loaded(layer, *input_group)
        turned[...] = hidden_low[...].T
        acc[...] = summed_ref[...]
        input_hooks = [[], partly(1, input_one, input_two), [], act("middle", input_one, input_two) + partly(0, input_one, input_two)]
        if before:
            input_hooks[0] += act("settle", shrink)
            input_hooks[3] += act("share", before[0])

        def one_input(step, carry):
            at_step(step, input_hooks)
            index = backwards(step)
            away_copy(index).wait_recv()
            pair_grad = (here_ref[index] + away_in[layer][index].astype(F32)).astype(BF16)
            triple = jnp.concatenate([query_grad_ref[index], pair_grad], 1)
            update = dot(turned[...], triple).astype(BF16)
            put(input_one, index, 0, update[: depth // 2])
            put(input_two, index, 0, update[depth // 2 :])
            acc[...] += dot_rt(triple, wi[index])
            small[index, 8 * layer + 7 : 8 * layer + 8, 0 : 3 * width] = column_sum(triple.astype(F32))
            return carry

        lax.fori_loop(0, 4, one_input, 0)
        if layer > 0:
            load(layer - 1, input_group)

    shrink, expand, output, input_one, input_two = gradients[0]
    rows_back[...] = acc[...].astype(BF16)
    copy_core = remote(small.at[pl.ds(2, 2)], core_small, misc, 1, links.beside)
    copy_row = remote(mid_small, row_small, misc, 2, links.across)
    share_small = remote(small_out.at[core], small_out.at[core], misc, 3, links.beside)

    def step_copy(step):
        return remote(sum_small.at[step], step_small.at[step], (step_send, step_recv), step, bits[step])

    copy_core.start()
    copy_core.wait_recv()
    mid_small[...] = small[1] + core_small[1]
    copy_row.start()

    assert layers == 2
    shrink_two, expand_two, output_two, input_three, input_four = gradients[1]
    plan = [
        (expand_two, "widen"), (output_two, "widen"), (input_three, "spread"), (input_four, "spread"), (shrink, "cross"),
        (expand, "settle"), (expand_two, "share"), (output_two, "share"), (input_three, "widen"), (input_four, "widen"),
        (shrink, "spread"), (output, "settle"), (expand, "cross"), (input_one, "settle"), (input_two, "settle"), (output, "cross"),
        (input_three, "share"), (input_four, "share"), None, (input_one, "cross"), (shrink, "widen"), (expand, "spread"),
        (input_two, "cross"), (output, "spread"), None, (input_one, "spread"), (shrink, "share"), (input_two, "spread"),
        (expand, "widen"), (input_one, "widen"), None, (output, "widen"), (input_two, "widen"), (expand, "share"), (output, "share"),
    ]
    plan += [None] * (steps - 2) + [(input_one, "share"), (input_two, "share")]
    def start_rows():
        @pl.when(links.moved)
        def _():
            swap_rows.start()

    step, value = 0, None
    for entry in plan:
        if entry:
            getattr(entry[0], entry[1])()
            if entry == (input_one, "settle"):
                start_out()
                start_rows()
            continue
        if step == 0:
            copy_row.wait_recv()
            value = small[0] + core_small[0] + row_small[...]
        else:
            step_copy(step - 1).wait_recv()
            value = value + step_small[step - 1]
        if step < steps:
            sum_small[step] = value
            step_copy(step).start()
        else:
            small_out[core] = value
            share_small.start()
        step += 1
    assert step == steps + 1

    @pl.when(links.moved)
    def _():
        for copy in (swap_rows, swap_out):
            copy.wait_recv()
            copy.wait_send()

    @pl.when(jnp.logical_not(links.moved))
    def _():
        rows_ref[...] = rows_back[...]

    share_small.wait_recv()
    share_small.wait_send()
    copy_core.wait_send()
    copy_row.wait_send()
    for step in range(steps):
        step_copy(step).wait_send()
    for there in range(4):
        remote(away_ref.at[there], away_in[0].at[there], (away_send, away_recv), (0, there), links.beside).wait_send()
    for layer in range(layers):
        for gradient in gradients[layer]:
            gradient.wait_all(layer > 0)


def assemble_kernel(layers, *refs):
    (shrink, expand, output, input_one, input_two, small, out_rows, in_rows), refs = refs[:8], refs[8:]
    (shrink_ref, expand_ref, output_ref, input_ref, out_rows_ref, in_rows_ref), refs = refs[:6], refs[6:]
    vector_refs, (expand_bias_ref, query_bias_ref, value_bias_ref) = refs[:6], refs[6:]
    units, depth, width = shrink_ref.shape[1], shrink_ref.shape[2], output_ref.shape[1]
    shrink_ref[0] = shrink[0, 0, 0:units].astype(F32)
    expand_ref[0] = expand[0, 0, 0:depth].astype(F32)
    output_ref[0] = output[0, 0, 0:width].astype(F32)
    for kind in range(3):
        columns = slice(kind * width, (kind + 1) * width)
        input_ref[0, kind, 0 : depth // 2] = input_one[0, 0, 0 : depth // 2, columns].astype(F32)
        input_ref[0, kind, depth // 2 :] = input_two[0, 0, 0 : depth // 2, columns].astype(F32)
    out_rows_ref[...] = out_rows[...].astype(F32)
    in_rows_ref[...] = in_rows[...].astype(F32)

    @pl.when(pl.program_id(0) + pl.program_id(1) == 0)
    def _():
        for layer in range(layers):
            for number in range(6):
                vector_refs[number][layer : layer + 1] = small[0, 8 * layer + number : 8 * layer + number + 1]
            for part in range(2):
                row = slice(8 * layer + 6, 8 * layer + 7)
                expand_bias_ref[layer : layer + 1, part * units : (part + 1) * units] = small[part, row, 0:units]
                row = slice(8 * layer + 7, 8 * layer + 8)
                query_bias_ref[layer : layer + 1, part * width : (part + 1) * width] = small[part, row, 0:width]
                value_bias_ref[layer : layer + 1, part * width : (part + 1) * width] = small[part, row, 2 * width : 3 * width]


VM = pl.BlockSpec(memory_space=pltpu.VMEM)
AN = pl.BlockSpec(memory_space=pl.ANY)


def shaped(dtype, *dims):
    return jax.ShapeDtypeStruct(dims, dtype)


def cost(flops, size):
    return pl.CostEstimate(flops=flops, bytes_accessed=size, transcendentals=0)


def local(
    tokens, input_weight, query_bias, value_bias, output_weight, output_bias, first_gain, first_shift,
    expand_weight, expand_bias, shrink_weight, shrink_bias, second_gain, second_shift, lengths, bucket, cotangent,
):
    wide, narrow = lax.axis_size("wide"), lax.axis_size("narrow")
    assert narrow == 2 and wide % 2 == 0
    layers, depth = input_weight.shape[0], input_weight.shape[1]
    rows = tokens.shape[0]
    width = input_weight.shape[3] // 2
    units = expand_weight.shape[2] // 2

    flag = jnp.broadcast_to(bucket, (8, 128)).astype(F32)
    input_own = input_weight.transpose(0, 2, 1, 3)
    output_own = output_weight.reshape(layers, 2, width, depth)
    shrink_own = shrink_weight.reshape(layers, 2, units, depth)
    gains = (output_bias, first_gain, first_shift, shrink_bias, second_gain, second_shift)
    biases = (query_bias, value_bias, expand_bias)
    query_shape = shaped(BF16, 4, rows, width)
    pair_shape = shaped(BF16, 4, rows, 2 * width)
    row_shape = shaped(F32, rows, depth)
    low_shape = shaped(BF16, rows, depth)
    scale_shape = shaped(F32, rows, 1)
    stat_shape = shaped(F32, 4, 16, rows)
    wide_shape = shaped(BF16, 4, rows, units)
    state_shapes = [
        shaped(BF16, 4, depth, 3 * width), shaped(BF16, 4, width, depth), shaped(BF16, 4, depth, units), shaped(BF16, 4, units, depth),
        query_shape, pair_shape, pair_shape, query_shape, stat_shape, low_shape, row_shape, scale_shape, wide_shape, wide_shape, row_shape, scale_shape, low_shape,
    ]
    state_scratch = [pltpu.VMEM(shape.shape, shape.dtype) for shape in state_shapes]
    kept_shapes = state_shapes * layers
    results = pl.pallas_call(
        functools.partial(all_forward, layers),
        out_shape=[low_shape, low_shape, shaped(F32, 8, 128)] + kept_shapes,
        in_specs=[VM] * 12 + [AN] * 4,
        out_specs=[AN] * (3 + len(kept_shapes)),
        scratch_shapes=state_scratch * layers + [pltpu.VMEM(bias.shape, F32) for bias in biases] + [
            pltpu.SemaphoreType.DMA((layers, STATES)), pltpu.SemaphoreType.DMA((3,)),
            pltpu.VMEM((rows, depth), BF16), pltpu.VMEM((rows, depth), BF16), pltpu.VMEM((8, 128), F32),
            pltpu.VMEM((rows, depth), F32),
            pltpu.SemaphoreType.DMA((4 * layers, 6)),
            pltpu.SemaphoreType.DMA((4 * layers, 10)), pltpu.SemaphoreType.DMA((4 * layers, 10)),
            pltpu.SemaphoreType.DMA((layers, 4)), pltpu.SemaphoreType.DMA((layers, 4)),
            pltpu.SemaphoreType.DMA((7,)), pltpu.SemaphoreType.DMA((7,)),
        ],
        compiler_params=pltpu.CompilerParams(collective_id=1, has_side_effects=True, vmem_limit_bytes=62 * 2**20),
        cost_estimate=cost(10**10, 10**8),
        name="forward",
    )(flag, tokens, cotangent, *biases, *gains, input_own, output_own, expand_weight, shrink_own)
    chips = wide // 2
    further = (chips // 8).bit_length() - 1
    tall = lambda size: -(-size // 128) * 128
    sizes = ((units, depth), (depth, units), (width, depth), (depth // 2, 3 * width), (depth // 2, 3 * width))
    out_shapes = [shaped(BF16, layers, 2, tall(size), columns) for size, columns in sizes]
    theirs_scratch = [pltpu.VMEM((2, size, columns), BF16) for size, columns in sizes]
    buffer_scratch = []
    for layer, (kind, (size, columns)) in itertools.product(range(layers), enumerate(sizes)):
        piece = tall(size) // 8
        late = late_sum(layer, kind)
        kept = 2 if late else 1
        buffer_scratch += [
            pltpu.VMEM((2, tall(size), columns), BF16), pltpu.VMEM((2, size, columns), BF16), pltpu.VMEM((piece if late else size, columns), BF16),
            pltpu.VMEM((kept, 4 * piece, columns), BF16), pltpu.VMEM((kept, 3, piece, columns), BF16),
            pltpu.VMEM((further, piece, columns) if further else (1, 16, 128), BF16),
        ]
    small_rows = 8 * layers
    steps = chips.bit_length() - 1
    small_scratch = pltpu.VMEM((small_rows, depth), F32)
    grad_sem = pltpu.SemaphoreType.DMA((KINDS * layers, 20 + further))
    results = pl.pallas_call(
        functools.partial(all_backward, layers, chips),
        out_shape=[low_shape, low_shape, shaped(F32, 2, small_rows, depth)] + out_shapes,
        in_specs=[AN] * 3 + [VM] * 6 + [AN] * len(kept_shapes),
        out_specs=[VM] * (3 + KINDS),
        scratch_shapes=state_scratch + [
            pltpu.VMEM((rows, depth), F32), pltpu.VMEM((depth, rows), BF16), pltpu.VMEM((rows, depth), F32),
            pltpu.VMEM(query_shape.shape, BF16), pltpu.VMEM(stat_shape.shape, F32), pltpu.VMEM(query_shape.shape, BF16),
            pltpu.VMEM(pair_shape.shape, F32), pltpu.VMEM(pair_shape.shape, BF16), pltpu.VMEM((rows, depth), BF16), pltpu.VMEM((rows, depth), BF16),
        ] + [pltpu.VMEM(pair_shape.shape, BF16)] * layers + theirs_scratch + buffer_scratch + [
            pltpu.VMEM((4, small_rows, depth), F32), pltpu.VMEM((2, small_rows, depth), F32), small_scratch, small_scratch,
            pltpu.VMEM((steps, small_rows, depth), F32), pltpu.VMEM((steps, small_rows, depth), F32),
            pltpu.VMEM((rows, depth), BF16), pltpu.VMEM((rows, depth), BF16), pltpu.VMEM((8, 128), F32), pltpu.SemaphoreType.DMA((3,)),
            pltpu.SemaphoreType.DMA((STATES,)),
            pltpu.SemaphoreType.DMA((layers, 4)), pltpu.SemaphoreType.DMA((layers, 4)),
            grad_sem, grad_sem,
            pltpu.SemaphoreType.DMA((5,)), pltpu.SemaphoreType.DMA((5,)),
            pltpu.SemaphoreType.DMA((steps,)), pltpu.SemaphoreType.DMA((steps,)),
        ],
        compiler_params=pltpu.CompilerParams(collective_id=0, has_side_effects=True, vmem_limit_bytes=67043328),
        cost_estimate=cost(10**10, 10**8),
        name="backward",
    )(*results[:3], *gains, *results[3:])
    out_rows, in_rows, small = results[:3]
    whole = lambda *dims: pl.BlockSpec(dims, lambda layer, part: (0,) * len(dims))
    piece = lambda shape: pl.BlockSpec((1, 1) + shape.shape[2:], lambda layer, part: (layer, part, 0, 0))
    strip = pl.BlockSpec((rows // (2 * layers), depth), lambda layer, part: (2 * layer + part, 0))
    upright = lambda size: pl.BlockSpec((1, size, depth), lambda layer, part: (layer, part, 0))
    vector_shape = shaped(F32, layers, depth)
    outs = pl.pallas_call(
        functools.partial(assemble_kernel, layers),
        grid=(layers, 2),
        out_shape=[
            shaped(F32, layers, 2 * units, depth), shaped(F32, layers, depth, 2 * units), shaped(F32, layers, 2 * width, depth),
            shaped(F32, layers, 3, depth, 2 * width), row_shape, row_shape,
        ] + [vector_shape] * 6 + [shaped(F32, layers, 2 * units), shaped(F32, layers, 2 * width), shaped(F32, layers, 2 * width)],
        in_specs=[piece(shape) for shape in out_shapes] + [whole(2, small_rows, depth), strip, strip],
        out_specs=[
            upright(units), pl.BlockSpec((1, depth, units), lambda layer, part: (layer, 0, part)), upright(width),
            pl.BlockSpec((1, 3, depth, width), lambda layer, part: (layer, 0, 0, part)), strip, strip,
        ] + [whole(layers, depth)] * 6 + [whole(layers, 2 * units), whole(layers, 2 * width), whole(layers, 2 * width)],
        compiler_params=pltpu.CompilerParams(vmem_limit_bytes=67043328),
        cost_estimate=cost(10**6, 2 * 10**7),
        name="assemble",
    )(*results[3:], small, out_rows, in_rows)
    shrink_grad, expand_grad, output_grad, input_grad, layer_output, input_rows = outs[:6]
    second_shift_grad, second_gain_grad, shrink_bias_grad, first_shift_grad, first_gain_grad, output_bias_grad = outs[6:12]
    expand_bias_grad, query_bias_grad, value_bias_grad = outs[12:]
    return (
        layer_output,
        input_rows,
        input_grad.transpose(0, 2, 1, 3),
        query_bias_grad,
        value_bias_grad,
        output_grad,
        output_bias_grad,
        first_gain_grad,
        first_shift_grad,
        expand_grad,
        expand_bias_grad,
        shrink_grad,
        shrink_bias_grad,
        second_gain_grad,
        second_shift_grad,
    )


def solution(mesh):
    split = P(AXES, None)
    in_specs = (
        split, P(None, None, None, "narrow"), P(None, "narrow"), P(None, "narrow"), P(None, "narrow", None), P(), P(), P(),
        P(None, None, "narrow"), P(None, "narrow"), P(None, "narrow", None), P(), P(), P(), P("wide"), P("wide"), split,
    )
    out_specs = (
        split, split, P(None, None, None, "narrow"), P(None, "narrow"), P(None, "narrow"), P(None, "narrow", None), P(), P(), P(),
        P(None, None, "narrow"), P(None, "narrow"), P(None, "narrow", None), P(), P(), P(),
    )
    return jax.shard_map(local, mesh=mesh, in_specs=in_specs, out_specs=out_specs, check_vma=False)
```

```python
import functools
import itertools

import jax
import jax.numpy as jnp
from jax import lax
from jax.experimental import pallas as pl
from jax.experimental.pallas import tpu as pltpu
from jax.sharding import PartitionSpec as P

DH = 64
EPSILON = 1e-12
MASKED = -1e9
AXES = ("wide", "narrow")
F32 = jnp.float32
BF16 = jnp.bfloat16
STATES = 17
KINDS = 5


def dot(a, b):
    return lax.dot_general(a, b, (((1,), (0,)), ((), ())), preferred_element_type=F32)


def dot_rt(a, b):
    return lax.dot_general(a, b, (((1,), (1,)), ((), ())), preferred_element_type=F32)


def dot_lt(a, b):
    return lax.dot_general(a, b, (((0,), (0,)), ((), ())), preferred_element_type=F32)


def lane_halves(shape):
    lane = lax.broadcasted_iota(jnp.int32, shape, len(shape) - 1)
    return lane < DH


def normalise(x):
    centre = x - jnp.mean(x, -1, keepdims=True)
    scale = lax.rsqrt(jnp.mean(centre * centre, -1, keepdims=True) + EPSILON)
    return centre * scale, scale


def gelu_parts(a):
    square = jnp.exp(-0.5 * a * a)
    size = jnp.abs(a)
    t = 1.0 / (1.0 + (0.3275911 * 0.7071067811865476) * size)
    poly = t * (
        0.127414796
        + t * (-0.142248368 + t * (0.7107068705 + t * (-0.7265760135 + t * 0.5307027145)))
    )
    tail = poly * square
    phi = jnp.where(a >= 0, 1.0 - tail, tail)
    return a * phi, phi + a * square * 0.3989422804014327


class Links:
    def __init__(self):
        self.wide, self.narrow = lax.axis_index("wide"), lax.axis_index("narrow")
        self.core = lax.rem(self.wide, 2)
        self.chip = self.wide // 2
        self.bit = lax.rem(self.chip, 2)
        other_core, other_narrow = self.wide + 1 - 2 * self.core, 1 - self.narrow
        self.beside = (other_core, self.narrow)
        self.across = (self.wide, other_narrow)
        self.next_bit = lax.rem(self.chip // 2, 2)
        self.along = (self.wide + 2 * (1 - 2 * self.bit), self.narrow)
        self.along_next = (self.wide + 4 * (1 - 2 * self.next_bit), self.narrow)
        self.opposite = (other_core, other_narrow)
        self.moved = self.core + self.narrow == 1

    def plane(self, chips):
        assert chips % 8 == 0
        self.line = lax.rem(self.chip // 2, 4)
        self.line_peers = []
        for offset in range(1, 4):
            there = lax.rem(self.line + offset, 4)
            self.line_peers.append((self.wide + 4 * (there - self.line), self.narrow))
        self.bits = []
        for bit in range(chips.bit_length() - 1):
            side = lax.rem(self.chip // 2**bit, 2)
            self.bits.append((self.wide + 2 ** (bit + 1) * (1 - 2 * side), self.narrow))
        self.further = self.bits[3:]

    def greet(self, devices):
        self.greeted = len(devices)
        for device in devices:
            pl.semaphore_signal(pltpu.get_barrier_semaphore(), inc=1, device_id=device, device_id_type=pl.DeviceIdType.MESH)

    def wait_greetings(self):
        pl.semaphore_wait(pltpu.get_barrier_semaphore(), self.greeted)


def remote(source, target, sems, at, device):
    return pltpu.make_async_remote_copy(
        source, target, sems[0].at[at], sems[1].at[at], device_id=device, device_id_type=pl.DeviceIdType.MESH
    )


class Weight:
    def __init__(self, links, number, own, parts, buffer, local_sem, sems):
        self.links, self.number, self.own, self.parts = links, number, own, parts
        self.buffer, self.local_sem, self.sems = buffer, local_sem, sems
        self.size = buffer.shape[1] // 4
        self.columns = buffer.shape[2] // parts

    def rows(self, flip, flip_next):
        bit = self.links.bit + flip * (1 - 2 * self.links.bit)
        next_bit = self.links.next_bit + flip_next * (1 - 2 * self.links.next_bit)
        return pl.ds(pl.multiple_of((2 * next_bit + bit) * self.size, 16), self.size)

    def local_copies(self):
        core = self.links.core
        copies = []
        for slot, part in ((0, core), (2, 1 - core)):
            for kind in range(self.parts):
                target = self.buffer.at[slot, :, pl.ds(kind * self.columns, self.columns)]
                at = 12 * (self.number // 4) + (0 if self.parts > 1 else 4 + 2 * (self.number % 4)) + len(copies)
                copies.append(pltpu.make_async_copy(self.own(part, slice(None), kind), target, self.local_sem.at[at]))
        return copies

    def place(self, at):
        return 34 * (self.number // 4) + (at if self.parts > 1 else 8 * (self.number % 4) + 2 + at)

    def first_hops(self):
        rows = self.rows(0, 0)
        return [
            remote(
                self.own(self.links.core, rows, kind), self.buffer.at[1, rows, pl.ds(kind * self.columns, self.columns)],
                self.sems, self.place(kind), self.links.across,
            )
            for kind in range(self.parts)
        ]

    def hop(self, kind):
        links = self.links
        at = self.place(self.parts - 1 + kind)
        device = links.along if kind == 1 or (kind == 3 and self.number % 2) else links.along_next
        if kind < 3:
            rows = self.rows(0, 0)
        elif kind == 3:
            rows = self.rows(0, 1) if self.number % 2 else self.rows(1, 0)
        else:
            rows = self.rows(kind % 2, (kind - 4) // 2)
        if kind < 4:
            return remote(self.buffer.at[1, rows], self.buffer.at[1, rows], self.sems, at, device)
        return remote(self.buffer.at[1, rows], self.buffer.at[3, rows], self.sems, at, links.beside)

    def start(self):
        for copy in self.first_hops():
            copy.start()

    def start_local(self):
        for copy in self.local_copies():
            copy.start()

    def relay(self):
        for copy in self.first_hops():
            copy.wait_recv()
        for kind in (1, 2, 4):
            self.hop(kind).start()

    def relay_again(self):
        self.hop(1).wait_recv()
        self.hop(2).wait_recv()
        for kind in (3, 5, 6):
            self.hop(kind).start()

    def relay_last(self):
        self.hop(3).wait_recv()
        self.hop(7).start()

    def wait_own(self):
        for copy in self.local_copies():
            copy.wait()

    def wait_fetched(self):
        for kind in range(4, 8):
            self.hop(kind).wait_recv()

    def wait_sent(self):
        for copy in self.first_hops() + [self.hop(kind) for kind in range(1, 8)]:
            copy.wait_send()


def ordered(step):
    return lax.rem(2 * step, 4) + step // 2


def at_step(step, hooks):
    for number, hook in enumerate(hooks):
        if hook:

            @pl.when(step == number)
            def _(hook=hook):
                for action in hook:
                    action()


def all_forward(layers, *refs):
    (bucket, tokens, cotangent, query_bias, value_bias, expand_bias), refs = refs[:6], refs[6:]
    gains, refs = refs[:6], refs[6:]
    (wi_own, wo_own, we_own, ws_own), refs = refs[:4], refs[4:]
    (rows_out, cotangent_out, flag_out), refs = refs[:3], refs[3:]
    kept = [refs[STATES * layer : STATES * (layer + 1)] for layer in range(layers)]
    refs = refs[STATES * layers :]
    states = [refs[STATES * layer : STATES * (layer + 1)] for layer in range(layers)]
    refs = refs[STATES * layers :]
    tokens_in = states[0][16]
    biases = (query_bias, value_bias, expand_bias)
    biases_in, refs = refs[:3], refs[3:]
    (save_sem, pass_sem, rows_low, cotangent_in, flag_in, flag_own, acc, local_sem, send_sem, recv_sem, kv_send, kv_recv, misc_send, misc_recv) = refs
    links = Links()
    core = links.core
    sems = (send_sem, recv_sem)
    units = ws_own.shape[2]
    width = wo_own.shape[2]
    rows = tokens.shape[0]
    weights = []
    for layer in range(layers):
        buffers = states[layer][:4]

        def lanes(part, count):
            return pl.ds(pl.multiple_of(part * count, 128), count)

        owns = [
            lambda part, rows, kind, layer=layer: wi_own.at[layer, kind, rows, lanes(part, width)],
            lambda part, rows, kind, layer=layer: wo_own.at[layer, part, rows],
            lambda part, rows, kind, layer=layer: we_own.at[layer, rows, lanes(part, units)],
            lambda part, rows, kind, layer=layer: ws_own.at[layer, part, rows],
        ]
        weights.append([
            Weight(links, 4 * layer + number, owns[number], 3 if number == 0 else 1, buffers[number], local_sem, sems)
            for number in range(4)
        ])
    every = [weight for group in weights for weight in group]
    links.greet([links.across, links.along, links.along_next, links.beside, links.opposite])
    fill_tokens = pltpu.make_async_copy(tokens, tokens_in, pass_sem.at[2])

    @pl.when(jnp.logical_not(links.moved))
    def _():
        fill_tokens.start()

    for weight in every[:4]:
        weight.start_local()
    flag = flag_own
    flag[...] = jnp.full(flag.shape, bucket[0], jnp.int32).astype(F32)
    links.wait_greetings()
    misc = (misc_send, misc_recv)
    swap_tokens = remote(tokens, tokens_in, misc, 0, links.opposite)
    swap_flag = remote(flag, flag_in, misc, 1, links.opposite)
    swap_cotangent = remote(cotangent, cotangent_in, misc, 2, links.opposite)
    copy_biases = [remote(biases[number], biases_in[number], misc, 3 + number, links.across) for number in range(3)]

    for copy in copy_biases:
        copy.start()
    every[0].start()
    every[1].start()

    @pl.when(links.moved)
    def _():
        swap_flag.start()
        swap_tokens.start()
        for weight in every[2:]:
            weight.start()
        swap_cotangent.start()

    @pl.when(jnp.logical_not(links.moved))
    def _():
        fill_tokens.wait()
        flag_in[...] = flag[...]

    def start_rest():
        @pl.when(jnp.logical_not(links.moved))
        def _():
            for weight in every[2:]:
                weight.start()

        for weight in every[4:]:
            weight.start_local()

    def bias(number, layer, index):
        size = biases[number].shape[1] // 2
        part = core + (index // 2) * (1 - 2 * core)
        place = pl.ds(pl.multiple_of(part * size, 128), size)
        return jnp.where(
            lax.rem(index, 2) == 0, biases[number][layer : layer + 1, place], biases_in[number][layer : layer + 1, place]
        )

    for copy in copy_biases:
        copy.wait_recv()
    every[0].relay()
    every[1].relay()
    every[0].relay_again()
    every[1].relay_again()

    @pl.when(links.moved)
    def _():
        swap_flag.wait_recv()
        swap_tokens.wait_recv()

    shift = jnp.where(flag_in[0:1, 0:1] < 0.5, 0.0, MASKED)
    acc[...] = tokens_in[...].astype(F32)
    halves = lane_halves((rows, width))

    def save_copy(layer, number):
        return pltpu.make_async_copy(states[layer][number], kept[layer][number], save_sem.at[layer, number])

    def save(layer, *numbers):
        for number in numbers:
            save_copy(layer, number).start()

    pass_rows = pltpu.make_async_copy(rows_low, rows_out, pass_sem.at[0])
    pass_flag = pltpu.make_async_copy(flag_in, flag_out, pass_sem.at[1])
    pass_far = pltpu.make_async_copy(cotangent_in, cotangent_out, pass_sem.at[2])
    pass_flag.start()

    def pass_cotangent():
        @pl.when(links.moved)
        def _():
            swap_cotangent.wait_recv()
            pass_far.start()

    for layer in range(layers):
        (wi, wo, we, ws, query_ref, pair_ref, remote_ref, mixed_ref, total_ref, normed_ref, first_ref, first_scale, active_ref, slope_ref, second_ref, second_scale, low_ref) = states[layer]
        vector = lambda at: gains[at][layer : layer + 1]
        wi_go, wo_go, we_go, ws_go = weights[layer]
        later = weights[layer + 1] if layer + 1 < layers else None
        if layer > 0:
            low_ref[...] = acc[...].astype(BF16)

        def exchange(index):
            return remote(pair_ref.at[index], remote_ref.at[index], (kv_send, kv_recv), (layer, index), links.beside)

        def project(step, carry):
            index = ordered(step)
            triple = dot(low_ref[...], wi[index])
            query = (triple[:, :width] + bias(0, layer, index)).astype(BF16)
            query_ref[index] = query * BF16(DH ** (-0.5))
            pair_ref[index, :, :width] = triple[:, width : 2 * width].astype(BF16)
            pair_ref[index, :, width:] = (triple[:, 2 * width :] + bias(1, layer, index)).astype(BF16)
            exchange(index).start()
            return carry

        def project_rest():
            lax.fori_loop(2, 4, project, 0)

        wi_go.wait_own()
        if layer == 0:
            start_rest()
        lax.fori_loop(0, 2, project, 0)
        after_pair = [[], [], [], []]
        if layer == 0:
            before_pair = [
                [],
                [wi_go.relay_last, wo_go.relay_last, we_go.relay],
                [ws_go.relay, wi_go.wait_fetched, wo_go.wait_fetched, project_rest, we_go.relay_again],
                [ws_go.relay_again],
            ]
            before_feed = [we_go.relay_last]
            before_quarter = [[], [ws_go.relay_last], [we_go.wait_fetched, ws_go.wait_fetched], []]
            if later:
                before_feed += [later[0].relay, later[1].relay]
                before_quarter[1] += [later[2].relay]
                before_quarter[2] += [later[0].relay_again, later[1].relay_again]
                before_quarter[3] += [later[3].relay]
        else:
            before_pair = [
                [wi_go.relay_last, wo_go.relay_last, we_go.relay_again],
                [ws_go.relay_again, we_go.relay_last],
                [ws_go.relay_last, wi_go.wait_fetched, project_rest, wo_go.wait_fetched],
                [],
            ]
            before_feed = []
            before_quarter = [[], [], [we_go.wait_fetched, ws_go.wait_fetched], []]
            if later:
                before_feed += [later[0].relay, later[1].relay]
                before_quarter[1] += [later[2].relay]
                before_quarter[2] += [later[0].relay_again, later[1].relay_again]
                before_quarter[3] += [later[3].relay]
        before_quarter[3] += [functools.partial(save, layer, 2, 3)]
        if not later:
            before_quarter[3] += [pass_cotangent]
        acc[...] += vector(0)

        def one_pair(step, carry):
            at_step(step, before_pair)
            index = ordered(step)
            there = lax.rem(index + 2, 4)
            exchange(there).wait_recv()
            at_step(step, after_pair)
            queries = query_ref[index]
            key_here, value_here = pair_ref[index, :, :width], pair_ref[index, :, width:]
            key_there, value_there = remote_ref[there, :, :width], remote_ref[there, :, width:]
            mixed, total = [], []
            for part in range(2):
                mask = halves if part == 0 else jnp.logical_not(halves)
                masked = jnp.where(mask, queries, BF16(0))
                here = dot_rt(masked, key_here)
                away = dot_rt(masked, key_there)
                peak = jnp.maximum(jnp.max(here, -1, keepdims=True), jnp.max(away, -1, keepdims=True) + shift)
                here = jnp.exp(here - peak)
                away = jnp.exp(away - (peak - shift))
                weight = jnp.sum(here, -1, keepdims=True) + jnp.sum(away, -1, keepdims=True)
                both = dot(here.astype(BF16), value_here) + dot(away.astype(BF16), value_there)
                mixed.append(both * (1.0 / weight))
                total.append(jnp.broadcast_to(peak + jnp.log(weight), (rows, width)))
            mixed_low = jnp.where(halves, mixed[0], mixed[1]).astype(BF16)
            mixed_ref[index] = mixed_low
            totals = jnp.where(halves, total[0], total[1]).T
            total_ref[index] = jnp.concatenate([totals[0:8], totals[DH : DH + 8]], 0)
            acc[...] += dot(mixed_low, wo[index])
            return carry

        wo_go.wait_own()
        lax.fori_loop(0, 4, one_pair, 0)
        for action in before_feed:
            action()
        save(layer, 16, 0, 4, 5, 6, 1, 7, 8)
        first, scale = normalise(acc[...])
        first_ref[...] = first
        first_scale[...] = scale
        normed = first * vector(1) + vector(2)
        normed_ref[...] = normed.astype(BF16)
        acc[...] = normed + vector(3)
        save(layer, 9, 10, 11)
        we_go.wait_own()
        ws_go.wait_own()

        def one_quarter(step, carry):
            at_step(step, before_quarter)
            index = ordered(step)
            active, slope = gelu_parts(dot(normed_ref[...], we[index]) + bias(2, layer, index))
            active_low = active.astype(BF16)
            active_ref[index] = active_low
            slope_ref[index] = slope.astype(BF16)
            acc[...] += dot(active_low, ws[index])
            return carry

        lax.fori_loop(0, 4, one_quarter, 0)
        save(layer, 12, 13)
        second, scale = normalise(acc[...])
        second_ref[...] = second
        second_scale[...] = scale
        save(layer, 14, 15)
        acc[...] = second * vector(4) + vector(5)

    rows_low[...] = acc[...].astype(BF16)
    pass_rows.start()

    @pl.when(links.moved)
    def _():
        pass_far.wait()
        for copy in (swap_tokens, swap_flag, swap_cotangent):
            copy.wait_send()

    for copy in copy_biases:
        copy.wait_send()
    for weight in every:
        weight.wait_sent()
    for layer in range(layers):
        for number in range(STATES):
            save_copy(layer, number).wait()
    pass_rows.wait()
    pass_flag.wait()

    for layer in range(layers):
        pair_ref, remote_ref = states[layer][5:7]
        for index in range(4):
            remote(pair_ref.at[index], remote_ref.at[index], (kv_send, kv_recv), (layer, index), links.beside).wait_send()


def column_sum(x):
    return jnp.sum(x, 0, keepdims=True)


def norm_backward(grad, normed, scale, gain):
    scaled = grad * gain
    return (
        scaled - jnp.mean(scaled, -1, keepdims=True) - normed * jnp.mean(scaled * normed, -1, keepdims=True)
    ) * scale


def backwards(step):
    return 3 - ordered(step)


class Gradient:
    def __init__(self, links, number, mine, theirs, core_in, narrow_in, pair_in, line_in, further_in, out, result, result_sem, sems):
        self.result, self.result_sem, self.collected = result, result_sem, False
        self.links, self.number, self.mine, self.theirs, self.core_in = links, number, mine, theirs, core_in
        self.narrow_in, self.pair_in, self.line_in, self.further_in, self.out, self.sems = narrow_in, pair_in, line_in, further_in, out, sems
        self.size = core_in.shape[1]
        self.piece = mine.shape[1] // 8

    def copy(self, source, target, at, device):
        return remote(source, target, self.sems, (self.number, at), device)

    def part_copy(self, part):
        return self.copy(self.theirs.at[part], self.core_in.at[part], part, self.links.beside)

    def narrow_copy(self):
        return self.copy(self.mine.at[1, pl.ds(0, self.size)], self.narrow_in, 2, self.links.across)

    def share_copy(self):
        place = self.out.at[self.links.core]
        return self.copy(place, place, 3, self.links.beside)

    def half_rows(self, other):
        bit = self.links.bit + other * (1 - 2 * self.links.bit)
        return pl.ds(pl.multiple_of(bit * 4 * self.piece, 16), 4 * self.piece)

    def piece_rows(self, offset):
        index = 4 * self.links.bit + lax.rem(self.links.line + offset, 4)
        return pl.ds(pl.multiple_of(index * self.piece, 16), self.piece)

    def pair_copy(self):
        return self.copy(self.mine.at[0, self.half_rows(1)], self.pair_in, 4, self.links.along)

    def line_copy(self, offset):
        device = self.links.line_peers[offset - 1]
        return self.copy(self.mine.at[0, self.piece_rows(offset)], self.line_in.at[offset - 1], 4 + offset, device)

    def line_back(self, offset):
        place = self.out.at[self.links.core, self.piece_rows(0)]
        return self.copy(place, place, 7 + offset, self.links.line_peers[offset - 1])

    def pair_back(self):
        place = self.out.at[self.links.core, self.half_rows(0)]
        return self.copy(place, place, 11, self.links.along)

    def further_copy(self, number):
        place = self.mine.at[0, self.piece_rows(0)]
        return self.copy(place, self.further_in.at[number], 12 + number, self.links.further[number])

    def send(self, part):
        self.part_copy(part).start()

    def middle(self):
        self.part_copy(1).wait_recv()
        self.mine[1, 0 : self.size] = add(self.mine[1, 0 : self.size], self.core_in[1])
        self.narrow_copy().start()

    def settle(self):
        self.part_copy(0).wait_recv()
        self.narrow_copy().wait_recv()
        self.mine[0, 0 : self.size] = add(self.mine[0, 0 : self.size], self.core_in[0], self.narrow_in[...])
        self.pair_copy().start()

    def cross(self):
        rows = self.half_rows(0)
        self.pair_copy().wait_recv()
        self.mine[0, rows] = add(self.mine[0, rows], self.pair_in[...])
        for offset in range(1, 4):
            self.line_copy(offset).start()

    def spread(self):
        rows = self.piece_rows(0)
        for offset in range(1, 4):
            self.line_copy(offset).wait_recv()
        total = add(self.mine[0, rows], self.line_in[0], self.line_in[1], self.line_in[2])
        for number in range(len(self.links.further)):
            self.mine[0, rows] = total
            copy = self.further_copy(number)
            copy.start()
            copy.wait()
            total = add(total, self.further_in[number])
        self.out[self.links.core, rows] = total
        for offset in range(1, 4):
            self.line_back(offset).start()

    def widen(self):
        for offset in range(1, 4):
            self.line_back(offset).wait_recv()
        self.pair_back().start()

    def result_copy(self, part):
        return pltpu.make_async_copy(self.out.at[part], self.result.at[part], self.result_sem.at[self.number, part])

    def share(self):
        self.pair_back().wait_recv()
        self.share_copy().start()
        self.result_copy(self.links.core).start()

    def collect(self):
        self.share_copy().wait_recv()
        self.result_copy(1 - self.links.core).start()
        self.collected = True

    def free_theirs(self):
        for part in range(2):
            self.part_copy(part).wait_send()

    def wait_all(self, theirs_waited):
        if not self.collected:
            self.collect()
        if not theirs_waited:
            self.free_theirs()
        copies = [self.share_copy(), self.narrow_copy(), self.pair_back()]
        for offset in range(1, 4):
            copies.append(self.line_back(offset))
            copies.append(self.line_copy(offset))
        copies.append(self.pair_copy())
        for copy in copies:
            copy.wait_send()

    def wait_results(self):
        for part in range(2):
            self.result_copy(part).wait()


def add(*terms):
    total = terms[0].astype(F32)
    for term in terms[1:]:
        total = total + term.astype(F32)
    return total.astype(BF16)


def all_backward(layers, chips, *refs):
    passed, cotangent_near, refs = refs[:3], refs[3], refs[4:]
    gains, refs = refs[:6], refs[6:]
    kept = [refs[STATES * layer : STATES * (layer + 1)] for layer in range(layers)]
    refs = refs[STATES * layers :]
    (out_rows, rows_ref, small_out), refs = refs[:3], refs[3:]
    results, refs = refs[:KINDS], refs[KINDS:]
    outs, refs = refs[:KINDS], refs[KINDS:]
    state, refs = refs[:STATES], refs[STATES:]
    (acc, turned, summed_ref, mixed_grad_ref, inner_ref, query_grad_ref, here_ref, away_ref, rows_low, rows_back), refs = refs[:10], refs[10:]
    away_in, refs = refs[:layers], refs[layers:]
    theirs, refs = refs[:KINDS], refs[KINDS:]
    buffers = []
    for layer in range(layers):
        buffers.append([refs[6 * kind : 6 * kind + 6] for kind in range(KINDS)])
        refs = refs[6 * KINDS :]
    (small, core_small, mid_small, row_small, sum_small, step_small), refs = refs[:6], refs[6:]
    (result_sem, out_low, cotangent, flag, pass_sem, load_sem, away_send, away_recv, grad_send, grad_recv, misc_send, misc_recv, step_send, step_recv) = refs
    (wi, wo, we, ws, query, pair, remote_pair, mixed, total_ref, normed, first, first_scale, active, slope, second, second_scale, hidden_low) = state
    links = Links()
    links.plane(chips)
    core = links.core
    steps = chips.bit_length() - 1
    bits = links.bits

    def load_copy(layer, number):
        return pltpu.make_async_copy(kept[layer][number], state[number], load_sem.at[number])

    def load(layer, numbers):
        for number in numbers:
            load_copy(layer, number).start()

    def loaded(layer, *numbers):
        for number in numbers:
            load_copy(layer, number).wait()

    block_group = (14, 15, 3, 13, 12, 2, 9, 10, 11, 1, 7)
    pair_group = (4, 5, 6, 8)
    input_group = (16, 0)
    passes = [pltpu.make_async_copy(passed[number], (out_low, cotangent, flag)[number], pass_sem.at[number]) for number in range(3)]
    near = pltpu.make_async_copy(cotangent_near, cotangent, pass_sem.at[1])

    @pl.when(links.moved)
    def _():
        passes[1].start()

    @pl.when(jnp.logical_not(links.moved))
    def _():
        near.start()

    passes[2].start()
    load(layers - 1, block_group[:7])
    links.greet([links.across, links.beside, links.opposite] + links.line_peers + bits)
    misc = (misc_send, misc_recv)
    gradients = []
    for layer in range(layers):
        group = []
        for kind in range(KINDS):
            mine, core_in, narrow_in, pair_in, line_in, further_in = buffers[layer][kind]
            group.append(Gradient(
                links, KINDS * layer + kind, mine, theirs[kind], core_in, narrow_in, pair_in, line_in, further_in,
                outs[kind].at[layer], results[kind].at[layer], result_sem, (grad_send, grad_recv),
            ))
        gradients.append(group)
    rows, width = mixed.shape[1], mixed.shape[2]
    units, depth = ws.shape[1], ws.shape[2]
    halves = lane_halves((rows, width))
    passes[2].wait()
    shift = jnp.where(flag[0:1, 0:1] < 0.5, 0.0, MASKED)
    small[...] = jnp.zeros(small.shape, F32)
    half = lax.broadcasted_iota(jnp.int32, (16, width), 1) // DH
    which = lax.broadcasted_iota(jnp.int32, (16, width), 0) // 8
    selector = (half == which).astype(F32)
    passes[1].wait()
    acc[...] = cotangent[...].astype(F32)
    passes[0].start()
    load(layers - 1, block_group[7:] + pair_group + input_group)
    swap_rows = remote(rows_back, rows_ref, misc, 0, links.opposite)
    swap_out = remote(out_low, out_rows, misc, 4, links.opposite)

    def start_out():
        passes[0].wait()

        @pl.when(links.moved)
        def _():
            swap_out.start()

        @pl.when(jnp.logical_not(links.moved))
        def _():
            out_rows[...] = out_low[...]

    for layer in reversed(range(layers)):
        shrink, expand, output, input_one, input_two = gradients[layer]
        before = gradients[layer + 1] if layer + 1 < layers else None
        vector = lambda at: gains[at][layer : layer + 1]

        def put(gradient, index, at, value):
            @pl.when(index < 2)
            def _():
                gradient.mine[index, at : at + value.shape[0]] = value

            @pl.when(index >= 2)
            def _():
                gradient.theirs[index - 2, at : at + value.shape[0]] = value

        def act(name, *which):
            return [getattr(gradient, name) for gradient in which]

        loaded(layer, 14, 15)
        incoming = acc[...]
        widened = norm_backward(incoming, second[...], second_scale[...], vector(4))
        sums = [column_sum(incoming), column_sum(incoming * second[...]), column_sum(widened)]
        acc[...] = widened
        rows_low[...] = widened.astype(BF16)
        loaded(layer, 9)
        turned[...] = normed[...].T
        loaded(layer, 3, 13, 12, 2)
        if before:
            for gradient in before:
                gradient.free_theirs()
        partly = lambda part, *which: [functools.partial(gradient.send, part) for gradient in which]
        block_hooks = [[], partly(1, shrink, expand), [], partly(0, shrink, expand) + act("middle", shrink, expand)]
        if before:
            block_hooks[0] += act("cross", before[0])
            block_hooks[2] += act("settle", before[1])

        def one_quarter(step, carry):
            at_step(step, block_hooks)
            index = backwards(step)
            branch = rows_low[...]
            inner = (dot_rt(branch, ws[index]) * slope[index].astype(F32)).astype(BF16)
            put(shrink, index, 0, dot_lt(active[index], branch).astype(BF16))
            put(expand, index, 0, dot(turned[...], inner).astype(BF16))
            small[index, 8 * layer + 6 : 8 * layer + 7, 0:units] = column_sum(inner.astype(F32))
            acc[...] += dot_rt(inner, we[index])
            return carry

        if not before:
            links.wait_greetings()
        lax.fori_loop(0, 4, one_quarter, 0)
        loaded(layer, 10, 11, 1, 7)
        outgoing = acc[...]
        summed = norm_backward(outgoing, first[...], first_scale[...], vector(1))
        sums += [column_sum(outgoing), column_sum(outgoing * first[...]), column_sum(summed)]
        for number, value in enumerate(sums):
            for quarter in range(4):
                small[quarter, 8 * layer + number : 8 * layer + number + 1] = value
        summed_ref[...] = summed
        rows_low[...] = summed.astype(BF16)
        if before:
            before[0].spread()
            before[2].settle()

        def one_output(step, carry):
            index = backwards(step)
            mixed_grad = dot_rt(rows_low[...], wo[index]).astype(BF16)
            mixed_grad_ref[index] = mixed_grad
            put(output, index, 0, dot_lt(mixed[index], rows_low[...]).astype(BF16))
            product = mixed_grad.astype(F32) * mixed[index].astype(F32)
            inner_ref[index] = lax.dot_general(
                selector, product, (((1,), (1,)), ((), ())), precision=lax.Precision.HIGHEST, preferred_element_type=F32
            )
            return carry

        lax.fori_loop(0, 4, one_output, 0)
        output.send(0)
        output.send(1)
        if layer > 0:
            load(layer - 1, block_group)
        loaded(layer, *pair_group)
        pair_hooks = [[], [output.middle], [], []]
        if before:
            pair_hooks[0] += act("settle", before[3], before[4]) + act("cross", before[1])
            pair_hooks[1] += act("cross", before[2])
            pair_hooks[2] += act("widen", before[0]) + act("cross", before[3], before[4])
            pair_hooks[3] += act("spread", before[1], before[2])
        else:
            pair_hooks[3] += act("settle", shrink)

        def away_copy(there):
            return remote(away_ref.at[there], away_in[layer].at[there], (away_send, away_recv), (layer, there), links.beside)

        if before:
            for there in range(4):
                remote(away_ref.at[there], away_in[layer + 1].at[there], (away_send, away_recv), (layer + 1, there), links.beside).wait_send()

        def one_pair(step, carry):
            at_step(step, pair_hooks)
            there = backwards(step)
            index = lax.rem(there + 2, 4)
            queries, grads = query[index], mixed_grad_ref[index]
            query_turned = None
            for side in range(2):
                source, place = (pair, index) if side == 0 else (remote_pair, there)
                keys, values = source[place, :, :width], source[place, :, width:]
                key_grad = value_grad = None
                for part in range(2):
                    mask = halves if part == 0 else jnp.logical_not(halves)
                    masked_query = jnp.where(mask, queries, BF16(0))
                    masked_grad = jnp.where(mask, grads, BF16(0))
                    masked_key = jnp.where(mask, keys, BF16(0))
                    level = total_ref[index, 8 * part : 8 * part + 1]
                    if side == 1:
                        level = level - shift
                    weights = jnp.exp(dot_rt(keys, masked_query) - level)
                    update = dot(weights.astype(BF16), masked_grad)
                    value_grad = update if value_grad is None else value_grad + update
                    slopes = dot_rt(values, masked_grad) - inner_ref[index, 8 * part : 8 * part + 1]
                    slopes = (weights * slopes).astype(BF16)
                    update = dot(slopes, masked_query)
                    key_grad = update if key_grad is None else key_grad + update
                    update = dot_lt(slopes, masked_key)
                    query_turned = update if query_turned is None else query_turned + update
                if side == 0:
                    here_ref[index, :, :width] = key_grad
                    here_ref[index, :, width:] = value_grad
                else:
                    away_ref[there, :, :width] = key_grad.astype(BF16)
                    away_ref[there, :, width:] = value_grad.astype(BF16)
            away_copy(there).start()
            query_grad_ref[index] = (query_turned * DH ** (-0.5)).astype(BF16)
            return carry

        lax.fori_loop(0, 4, one_pair, 0)
        if layer > 0:
            load(layer - 1, pair_group)
        loaded(layer, *input_group)
        turned[...] = hidden_low[...].T
        acc[...] = summed_ref[...]
        input_hooks = [[], partly(1, input_one, input_two), [], act("middle", input_one, input_two) + partly(0, input_one, input_two)]
        if before:
            input_hooks[0] += act("settle", shrink)
            input_hooks[3] += act("share", before[0])

        def one_input(step, carry):
            at_step(step, input_hooks)
            index = backwards(step)
            away_copy(index).wait_recv()
            pair_grad = (here_ref[index] + away_in[layer][index].astype(F32)).astype(BF16)
            triple = jnp.concatenate([query_grad_ref[index], pair_grad], 1)
            update = dot(turned[...], triple).astype(BF16)
            put(input_one, index, 0, update[: depth // 2])
            put(input_two, index, 0, update[depth // 2 :])
            acc[...] += dot_rt(triple, wi[index])
            small[index, 8 * layer + 7 : 8 * layer + 8, 0 : 3 * width] = column_sum(triple.astype(F32))
            return carry

        lax.fori_loop(0, 4, one_input, 0)
        if layer > 0:
            load(layer - 1, input_group)

    shrink, expand, output, input_one, input_two = gradients[0]
    rows_back[...] = acc[...].astype(BF16)
    copy_core = remote(small.at[pl.ds(2, 2)], core_small, misc, 1, links.beside)
    copy_row = remote(mid_small, row_small, misc, 2, links.across)
    share_small = remote(small_out.at[core], small_out.at[core], misc, 3, links.beside)

    def step_copy(step):
        return remote(sum_small.at[step], step_small.at[step], (step_send, step_recv), step, bits[step])

    copy_core.start()
    copy_core.wait_recv()
    mid_small[...] = small[1] + core_small[1]
    copy_row.start()

    assert layers == 2
    shrink_two, expand_two, output_two, input_three, input_four = gradients[1]
    plan = [
        (expand_two, "widen"), (output_two, "widen"), (input_three, "spread"), (input_four, "spread"), (shrink, "cross"),
        (expand, "settle"), (expand_two, "share"), (output_two, "share"), (input_three, "widen"), (input_four, "widen"),
        (shrink, "spread"), (output, "settle"), (expand, "cross"), (input_one, "settle"), (input_two, "settle"), (output, "cross"),
        (input_three, "share"), (input_four, "share"), None, (input_one, "cross"), (shrink, "widen"), (expand, "spread"),
        (input_two, "cross"), (output, "spread"), None, (input_one, "spread"), (shrink, "share"), (input_two, "spread"),
        (expand, "widen"), (input_one, "widen"), None, (output, "widen"), (input_two, "widen"), (expand, "share"), (output, "share"),
    ]
    plan += [(gradient, "collect") for gradient in gradients[1]] + [None] * (steps - 2) + [(input_one, "share"), (input_two, "share")]
    def start_rows():
        @pl.when(links.moved)
        def _():
            swap_rows.start()

    step, value = 0, None
    for entry in plan:
        if entry:
            getattr(entry[0], entry[1])()
            if entry == (input_one, "settle"):
                start_out()
                start_rows()
            continue
        if step == 0:
            copy_row.wait_recv()
            value = small[0] + core_small[0] + row_small[...]
        else:
            step_copy(step - 1).wait_recv()
            value = value + step_small[step - 1]
        if step < steps:
            sum_small[step] = value
            step_copy(step).start()
        else:
            small_out[core] = value
            share_small.start()
        step += 1
    assert step == steps + 1

    @pl.when(links.moved)
    def _():
        for copy in (swap_rows, swap_out):
            copy.wait_recv()
            copy.wait_send()

    @pl.when(jnp.logical_not(links.moved))
    def _():
        rows_ref[...] = rows_back[...]

    share_small.wait_recv()
    share_small.wait_send()
    copy_core.wait_send()
    copy_row.wait_send()
    for step in range(steps):
        step_copy(step).wait_send()
    for there in range(4):
        remote(away_ref.at[there], away_in[0].at[there], (away_send, away_recv), (0, there), links.beside).wait_send()
    for layer in range(layers):
        for gradient in gradients[layer]:
            gradient.wait_all(layer > 0)
    for layer in range(layers):
        for gradient in gradients[layer]:
            gradient.wait_results()


def assemble_kernel(layers, *refs):
    (shrink, expand, output, input_one, input_two, small, out_rows, in_rows), refs = refs[:8], refs[8:]
    (shrink_ref, expand_ref, output_ref, input_ref, out_rows_ref, in_rows_ref), refs = refs[:6], refs[6:]
    vector_refs, (expand_bias_ref, query_bias_ref, value_bias_ref) = refs[:6], refs[6:]
    units, depth, width = shrink_ref.shape[1], shrink_ref.shape[2], output_ref.shape[1]
    shrink_ref[0] = shrink[0, 0, 0:units].astype(F32)
    expand_ref[0] = expand[0, 0, 0:depth].astype(F32)
    output_ref[0] = output[0, 0, 0:width].astype(F32)
    for kind in range(3):
        columns = slice(kind * width, (kind + 1) * width)
        input_ref[0, kind, 0 : depth // 2] = input_one[0, 0, 0 : depth // 2, columns].astype(F32)
        input_ref[0, kind, depth // 2 :] = input_two[0, 0, 0 : depth // 2, columns].astype(F32)
    out_rows_ref[...] = out_rows[...].astype(F32)
    in_rows_ref[...] = in_rows[...].astype(F32)

    @pl.when(pl.program_id(0) + pl.program_id(1) == 0)
    def _():
        for layer in range(layers):
            for number in range(6):
                vector_refs[number][layer : layer + 1] = small[0, 8 * layer + number : 8 * layer + number + 1]
            for part in range(2):
                row = slice(8 * layer + 6, 8 * layer + 7)
                expand_bias_ref[layer : layer + 1, part * units : (part + 1) * units] = small[part, row, 0:units]
                row = slice(8 * layer + 7, 8 * layer + 8)
                query_bias_ref[layer : layer + 1, part * width : (part + 1) * width] = small[part, row, 0:width]
                value_bias_ref[layer : layer + 1, part * width : (part + 1) * width] = small[part, row, 2 * width : 3 * width]


VM = pl.BlockSpec(memory_space=pltpu.VMEM)
AN = pl.BlockSpec(memory_space=pl.ANY)
SM = pl.BlockSpec(memory_space=pltpu.SMEM)


def shaped(dtype, *dims):
    return jax.ShapeDtypeStruct(dims, dtype)


def cost(flops, size):
    return pl.CostEstimate(flops=flops, bytes_accessed=size, transcendentals=0)


def local(
    tokens, input_weight, query_bias, value_bias, output_weight, output_bias, first_gain, first_shift,
    expand_weight, expand_bias, shrink_weight, shrink_bias, second_gain, second_shift, lengths, bucket, cotangent,
):
    wide, narrow = lax.axis_size("wide"), lax.axis_size("narrow")
    assert narrow == 2 and wide % 2 == 0
    layers, depth = input_weight.shape[0], input_weight.shape[1]
    rows = tokens.shape[0]
    width = input_weight.shape[3] // 2
    units = expand_weight.shape[2] // 2

    input_own = input_weight.transpose(0, 2, 1, 3)
    output_own = output_weight.reshape(layers, 2, width, depth)
    shrink_own = shrink_weight.reshape(layers, 2, units, depth)
    gains = (output_bias, first_gain, first_shift, shrink_bias, second_gain, second_shift)
    biases = (query_bias, value_bias, expand_bias)
    query_shape = shaped(BF16, 4, rows, width)
    pair_shape = shaped(BF16, 4, rows, 2 * width)
    row_shape = shaped(F32, rows, depth)
    low_shape = shaped(BF16, rows, depth)
    scale_shape = shaped(F32, rows, 1)
    stat_shape = shaped(F32, 4, 16, rows)
    wide_shape = shaped(BF16, 4, rows, units)
    state_shapes = [
        shaped(BF16, 4, depth, 3 * width), shaped(BF16, 4, width, depth), shaped(BF16, 4, depth, units), shaped(BF16, 4, units, depth),
        query_shape, pair_shape, pair_shape, query_shape, stat_shape, low_shape, row_shape, scale_shape, wide_shape, wide_shape, row_shape, scale_shape, low_shape,
    ]
    state_scratch = [pltpu.VMEM(shape.shape, shape.dtype) for shape in state_shapes]
    kept_shapes = state_shapes * layers
    results = pl.pallas_call(
        functools.partial(all_forward, layers),
        out_shape=[low_shape, low_shape, shaped(F32, 8, 128)] + kept_shapes,
        in_specs=[SM] + [AN] * 2 + [VM] * 9 + [AN] * 4,
        out_specs=[AN] * (3 + len(kept_shapes)),
        scratch_shapes=state_scratch * layers + [pltpu.VMEM(bias.shape, F32) for bias in biases] + [
            pltpu.SemaphoreType.DMA((layers, STATES)), pltpu.SemaphoreType.DMA((3,)),
            pltpu.VMEM((rows, depth), BF16), pltpu.VMEM((rows, depth), BF16), pltpu.VMEM((8, 128), F32), pltpu.VMEM((8, 128), F32),
            pltpu.VMEM((rows, depth), F32),
            pltpu.SemaphoreType.DMA((12 * layers,)),
            pltpu.SemaphoreType.DMA((34 * layers,)), pltpu.SemaphoreType.DMA((34 * layers,)),
            pltpu.SemaphoreType.DMA((layers, 4)), pltpu.SemaphoreType.DMA((layers, 4)),
            pltpu.SemaphoreType.DMA((6,)), pltpu.SemaphoreType.DMA((6,)),
        ],
        compiler_params=pltpu.CompilerParams(collective_id=1, has_side_effects=True, vmem_limit_bytes=62 * 2**20),
        cost_estimate=cost(10**10, 10**8),
        name="forward",
    )(bucket, tokens, cotangent, *biases, *gains, input_own, output_own, expand_weight, shrink_own)
    chips = wide // 2
    further = (chips // 8).bit_length() - 1
    tall = lambda size: -(-size // 128) * 128
    sizes = ((units, depth), (depth, units), (width, depth), (depth // 2, 3 * width), (depth // 2, 3 * width))
    out_shapes = [shaped(BF16, layers, 2, tall(size), columns) for size, columns in sizes]
    theirs_scratch = [pltpu.VMEM((2, size, columns), BF16) for size, columns in sizes]
    buffer_scratch = []
    for layer, (kind, (size, columns)) in itertools.product(range(layers), enumerate(sizes)):
        piece = tall(size) // 8
        buffer_scratch += [
            pltpu.VMEM((2, tall(size), columns), BF16), pltpu.VMEM((2, size, columns), BF16), pltpu.VMEM((size, columns), BF16),
            pltpu.VMEM((4 * piece, columns), BF16), pltpu.VMEM((3, piece, columns), BF16),
            pltpu.VMEM((further, piece, columns) if further else (1, 16, 128), BF16),
        ]
    small_rows = 8 * layers
    steps = chips.bit_length() - 1
    small_scratch = pltpu.VMEM((small_rows, depth), F32)
    grad_sem = pltpu.SemaphoreType.DMA((KINDS * layers, 12 + further))
    results = pl.pallas_call(
        functools.partial(all_backward, layers, chips),
        out_shape=[low_shape, low_shape, shaped(F32, 2, small_rows, depth)] + out_shapes,
        in_specs=[AN] * 4 + [VM] * 6 + [AN] * len(kept_shapes),
        out_specs=[VM] * 3 + [AN] * KINDS,
        scratch_shapes=[pltpu.VMEM(shape.shape, BF16) for shape in out_shapes] + state_scratch + [
            pltpu.VMEM((rows, depth), F32), pltpu.VMEM((depth, rows), BF16), pltpu.VMEM((rows, depth), F32),
            pltpu.VMEM(query_shape.shape, BF16), pltpu.VMEM(stat_shape.shape, F32), pltpu.VMEM(query_shape.shape, BF16),
            pltpu.VMEM(pair_shape.shape, F32), pltpu.VMEM(pair_shape.shape, BF16), pltpu.VMEM((rows, depth), BF16), pltpu.VMEM((rows, depth), BF16),
        ] + [pltpu.VMEM(pair_shape.shape, BF16)] * layers + theirs_scratch + buffer_scratch + [
            pltpu.VMEM((4, small_rows, depth), F32), pltpu.VMEM((2, small_rows, depth), F32), small_scratch, small_scratch,
            pltpu.VMEM((steps, small_rows, depth), F32), pltpu.VMEM((steps, small_rows, depth), F32),
            pltpu.SemaphoreType.DMA((KINDS * layers, 2)),
            pltpu.VMEM((rows, depth), BF16), pltpu.VMEM((rows, depth), BF16), pltpu.VMEM((8, 128), F32), pltpu.SemaphoreType.DMA((3,)),
            pltpu.SemaphoreType.DMA((STATES,)),
            pltpu.SemaphoreType.DMA((layers, 4)), pltpu.SemaphoreType.DMA((layers, 4)),
            grad_sem, grad_sem,
            pltpu.SemaphoreType.DMA((5,)), pltpu.SemaphoreType.DMA((5,)),
            pltpu.SemaphoreType.DMA((steps,)), pltpu.SemaphoreType.DMA((steps,)),
        ],
        compiler_params=pltpu.CompilerParams(collective_id=0, has_side_effects=True, vmem_limit_bytes=67043328),
        cost_estimate=cost(10**10, 10**8),
        name="backward",
    )(*results[:3], cotangent, *gains, *results[3:])
    out_rows, in_rows, small = results[:3]
    whole = lambda *dims: pl.BlockSpec(dims, lambda layer, part: (0,) * len(dims))
    piece = lambda shape: pl.BlockSpec((1, 1) + shape.shape[2:], lambda layer, part: (layer, part, 0, 0))
    strip = pl.BlockSpec((rows // (2 * layers), depth), lambda layer, part: (2 * layer + part, 0))
    upright = lambda size: pl.BlockSpec((1, size, depth), lambda layer, part: (layer, part, 0))
    vector_shape = shaped(F32, layers, depth)
    outs = pl.pallas_call(
        functools.partial(assemble_kernel, layers),
        grid=(layers, 2),
        out_shape=[
            shaped(F32, layers, 2 * units, depth), shaped(F32, layers, depth, 2 * units), shaped(F32, layers, 2 * width, depth),
            shaped(F32, layers, 3, depth, 2 * width), row_shape, row_shape,
        ] + [vector_shape] * 6 + [shaped(F32, layers, 2 * units), shaped(F32, layers, 2 * width), shaped(F32, layers, 2 * width)],
        in_specs=[piece(shape) for shape in out_shapes] + [whole(2, small_rows, depth), strip, strip],
        out_specs=[
            upright(units), pl.BlockSpec((1, depth, units), lambda layer, part: (layer, 0, part)), upright(width),
            pl.BlockSpec((1, 3, depth, width), lambda layer, part: (layer, 0, 0, part)), strip, strip,
        ] + [whole(layers, depth)] * 6 + [whole(layers, 2 * units), whole(layers, 2 * width), whole(layers, 2 * width)],
        compiler_params=pltpu.CompilerParams(vmem_limit_bytes=67043328),
        cost_estimate=cost(10**6, 2 * 10**7),
        name="assemble",
    )(*results[3:], small, out_rows, in_rows)
    shrink_grad, expand_grad, output_grad, input_grad, layer_output, input_rows = outs[:6]
    second_shift_grad, second_gain_grad, shrink_bias_grad, first_shift_grad, first_gain_grad, output_bias_grad = outs[6:12]
    expand_bias_grad, query_bias_grad, value_bias_grad = outs[12:]
    return (
        layer_output,
        input_rows,
        input_grad.transpose(0, 2, 1, 3),
        query_bias_grad,
        value_bias_grad,
        output_grad,
        output_bias_grad,
        first_gain_grad,
        first_shift_grad,
        expand_grad,
        expand_bias_grad,
        shrink_grad,
        shrink_bias_grad,
        second_gain_grad,
        second_shift_grad,
    )


def solution(mesh):
    split = P(AXES, None)
    in_specs = (
        split, P(None, None, None, "narrow"), P(None, "narrow"), P(None, "narrow"), P(None, "narrow", None), P(), P(), P(),
        P(None, None, "narrow"), P(None, "narrow"), P(None, "narrow", None), P(), P(), P(), P("wide"), P("wide"), split,
    )
    out_specs = (
        split, split, P(None, None, None, "narrow"), P(None, "narrow"), P(None, "narrow"), P(None, "narrow", None), P(), P(), P(),
        P(None, None, "narrow"), P(None, "narrow"), P(None, "narrow", None), P(), P(), P(),
    )
    return jax.shard_map(local, mesh=mesh, in_specs=in_specs, out_specs=out_specs, check_vma=False)
```
